32 devices in a mesh: dp: 8 (over y, x, core), tensor: 4 (over z).
Axes of the slice: x: 2, y: 2, z: 4, core: 2. Of those that a mesh axis runs over, the one named last changes fastest.
Arguments:
- inputs: bfloat16 [384, 200704], P('tensor', 'dp'), may hold values from -6 to 6
- crop_size: int32 [256, 4, 2], P('dp'), may hold values from 6 to 14, as said below
- crop_offset: int32 [256, 4, 2], P('dp'), may hold values from 0 to 8, as said below
- a_log: float32 [384, 64], P('tensor'), may hold values from -1.5 to 0.5
- a_imag: float32 [384, 64], P('tensor'), may hold values from 0 to 6
- c_height: float32 [2, 384, 64], P(None, 'tensor'), may hold values from -0.36 to 0.36
- c_width: float32 [2, 384, 64], P(None, 'tensor'), may hold values from -0.36 to 0.36
- log_dt: float32 [2, 384], P(None, 'tensor'), may hold values from -3 to -0.7
- skip_gain: float32 [384], P('tensor'), may hold values from 0.5 to 1.5
- ln_gain: float32 [384], replicated, may hold values from 0.1 to 1.9
- ln_bias: float32 [384], replicated, may hold values from -1.8 to 1.8
- w_in: bfloat16 [384, 1536], P(None, 'tensor'), may hold values from -0.3125 to 0.3125
- b_in: float32 [1536], P('tensor'), may hold values from -1.8 to 1.8
- w_out: bfloat16 [1536, 384], P('tensor'), may hold values from -0.15625 to 0.15625
- b_out: float32 [384], replicated, may hold values from -1.8 to 1.8
- layer_scale: float32 [384], replicated, may hold values from 0.5 to 2
- grad_out: bfloat16 [384, 200704], P('tensor', 'dp'), may hold values from -6 to 6
Outputs:
- result: bfloat16 [384, 200704], P('tensor', 'dp')
- grad_inputs: float32 [384, 200704], P('tensor', 'dp')
- grad_a_log: float32 [384, 64], P('tensor')
- grad_a_imag: float32 [384, 64], P('tensor')
- grad_c_height: float32 [2, 384, 64], P(None, 'tensor')
- grad_c_width: float32 [2, 384, 64], P(None, 'tensor')
- grad_log_dt: float32 [2, 384], P(None, 'tensor')
- grad_skip_gain: float32 [384], P('tensor')
- grad_ln_gain: float32 [384], P('tensor')
- grad_ln_bias: float32 [384], P('tensor')
- grad_w_in: float32 [384, 1536], P(None, 'tensor')
- grad_b_in: float32 [1536], P('tensor')
- grad_w_out: float32 [1536, 384], P('tensor')
- grad_b_out: float32 [384], P('tensor')
- grad_layer_scale: float32 [384], P('tensor')
The draws below stay inside these ranges and needn't reach their ends.
Inputs may be any that keep to these rules, and one draw needn't show every extreme that they name: `crop_size`: each crop fits its slot (offset plus size at most 14); in every canvas one slot, drawn from the seed, holds a full 14 x 14 crop, and another holds a crop of the least size. `crop_offset`: offsets with crop_size give crops inside their slots.
All inputs are finite; a program needn't handle non-finite values.
Results may differ from the reference program's by a relative error of at most 0.0071.
Values may be sent and summed in bfloat16 or wider, within the bound.
A program may use at most 448 MiB of HBM per device.

```python
import math
import jax
import jax.numpy as jnp
from jax import lax

D = 384
FF = 1536
NSTATE = 64
CROP = 14
NCAN = 256
SIDE = 28


def crop_plan(key):
    base_key = jax.random.fold_in(key, 11)
    key_size, key_full, key_offset = jax.random.split(base_key, 3)
    extent = jax.random.randint(key_size, (NCAN, 4, 2), 6, CROP + 1)
    full_slot = jax.random.randint(key_full, (NCAN, 1, 1), 0, 4)
    least_slot = (full_slot + 1) % 4
    slot_ids = jnp.arange(4, dtype=jnp.int32)[None, :, None]
    extent = jnp.where(slot_ids == full_slot, CROP, extent)
    extent = jnp.where(slot_ids == least_slot, 6, extent).astype(jnp.int32)
    raw_bits = jax.random.randint(key_offset, (NCAN, 4, 2), 0, 1 << 20)
    anchor = raw_bits % (CROP + 1 - extent)
    anchor = jnp.where(slot_ids == least_slot, CROP - 6, anchor).astype(jnp.int32)
    return (extent, anchor)


def draw_crop_size(key, part):
    return crop_plan(key)[0]


def draw_crop_offset(key, part):
    return crop_plan(key)[1]


def block_levels(rng, dims, shards, least, largest):
    level, own = 1.0, jax.random.fold_in(rng, 6)
    for position, shards_of in shards:
        draws = jnp.exp(jax.random.uniform(jax.random.fold_in(own, position), (shards_of,), jnp.float32, least / len(shards), largest / len(shards)))
        level = level * jnp.repeat(draws, dims[position] // shards_of).reshape([-1 if axis == position else 1 for axis in range(len(dims))])
    return level


def bell_draw(key, shape, scale, limit, shards=(), kind=jnp.bfloat16):
    array = scale * jax.random.normal(key, shape, jnp.float32)
    if shards:
        array = array * block_levels(key, shape, shards, -0.22, 0.18)
    return jnp.clip(array, -limit, limit).astype(kind)


def setup_inputs(seed: int = 0) -> dict:
    splits = jax.random.split(jax.random.key(seed), 18)
    inputs = bell_draw(splits[0], (D, NCAN * SIDE * SIDE), 1.0, 6.0, ((0, 4), (1, 8)))
    crop_size = draw_crop_size(jax.random.fold_in(splits[17], 71), 0)
    crop_offset = draw_crop_offset(jax.random.fold_in(splits[17], 71), 0)
    a_log = jnp.clip(-1.5 + 2.0 * jax.random.uniform(splits[3], (D, NSTATE), jnp.float32) ** block_levels(splits[3], (D, NSTATE), ((0, 4),), -0.2, 0.2), -1.5, 0.5)
    a_imag = jnp.clip(6.0 * jax.random.uniform(splits[4], (D, NSTATE), jnp.float32) ** block_levels(splits[4], (D, NSTATE), ((0, 4),), -0.2, 0.2), 0.0, 6.0)
    c_height = bell_draw(splits[5], (2, D, NSTATE), 0.06, 0.36, ((1, 4),), jnp.float32)
    c_width = bell_draw(splits[6], (2, D, NSTATE), 0.06, 0.36, ((1, 4),), jnp.float32)
    log_dt = jnp.clip(-3.0 + 2.3 * jax.random.uniform(splits[7], (2, D), jnp.float32) ** block_levels(splits[7], (2, D), ((1, 4),), -0.2, 0.2), -3.0, -0.7)
    skip_gain = jnp.clip(0.5 + 1.0 * jax.random.uniform(splits[8], (D,), jnp.float32) ** block_levels(splits[8], (D,), ((0, 4),), -0.2, 0.2), 0.5, 1.5)
    ln_gain = jnp.clip(1.0 + 0.18 * jax.random.normal(splits[9], (D,), jnp.float32), 0.1, 1.9)
    ln_bias = bell_draw(splits[10], (D,), 0.3, 1.8, (), jnp.float32)
    w_in = bell_draw(splits[11], (D, FF), D ** -0.5, 0.3125, ((1, 4),))
    b_in = bell_draw(splits[12], (FF,), 0.3, 1.8, ((0, 4),), jnp.float32)
    w_out = bell_draw(splits[13], (FF, D), FF ** -0.5, 0.15625, ((0, 4),))
    b_out = bell_draw(splits[14], (D,), 0.3, 1.8, (), jnp.float32)
    layer_scale = jnp.clip(jnp.exp(jax.random.uniform(splits[15], (D,), jnp.float32, math.log(0.5), math.log(2.0))), 0.5, 2.0)
    grad_out = bell_draw(splits[16], (D, NCAN * SIDE * SIDE), 1.0, 6.0, ((0, 4), (1, 8)))
    return {"inputs": inputs, "crop_size": crop_size, "crop_offset": crop_offset, "a_log": a_log, "a_imag": a_imag, "c_height": c_height, "c_width": c_width, "log_dt": log_dt, "skip_gain": skip_gain, "ln_gain": ln_gain, "ln_bias": ln_bias, "w_in": w_in, "b_in": b_in, "w_out": w_out, "b_out": b_out, "layer_scale": layer_scale, "grad_out": grad_out}


@jax.custom_vjp
def low(v):
    return lax.optimization_barrier(v.astype(jnp.bfloat16)).astype(jnp.float32)

@jax.custom_vjp
def low_back(v):
    return v

def low_keep(v):
    return (low(v), None)

def low_pass(kept, grad):
    return (grad,)

def back_keep(v):
    return (v, None)

def back_low(kept, grad):
    return (low(grad),)
low.defvjp(low_keep, low_pass)
low_back.defvjp(back_keep, back_low)
EPS = 1e-06

def crop_mask(crop_size, crop_offset, crop_len):
    canvases = crop_size.shape[0]
    spot_idx = jnp.arange(crop_len, dtype=jnp.int32)
    extent = crop_size.reshape(canvases, 2, 2, 2).astype(jnp.int32)
    anchor = crop_offset.reshape(canvases, 2, 2, 2).astype(jnp.int32)
    row_in = (spot_idx >= anchor[..., 0:1]) & (spot_idx < anchor[..., 0:1] + extent[..., 0:1])
    col_in = (spot_idx >= anchor[..., 1:2]) & (spot_idx < anchor[..., 1:2] + extent[..., 1:2])
    row_turned = jnp.transpose(row_in, (0, 1, 3, 2))
    return (row_turned[:, :, :, :, None] & col_in[:, :, None, :, :]).astype(jnp.float32)

def mixer_kernel(a_log, a_imag, c_pair, step_size, crop_len):
    lag_steps = jnp.arange(crop_len).astype(jnp.float32)
    decays = jnp.exp(-(step_size[:, None] * jnp.exp(a_log))[:, :, None] * lag_steps)
    phases = (step_size[:, None] * a_imag)[:, :, None] * lag_steps
    waves = c_pair[0][:, :, None] * jnp.cos(phases) - c_pair[1][:, :, None] * jnp.sin(phases)
    return lax.optimization_barrier(jnp.sum(decays * waves, axis=1))

def toeplitz(kernel, crop_len):
    spot_idx = jnp.arange(crop_len, dtype=jnp.int32)
    lag_table = (spot_idx[:, None, None] == spot_idx[None, :, None] - spot_idx[None, None, :]).astype(jnp.float32)
    return jnp.einsum('cl,lhk->chk', kernel, lag_table, precision=lax.Precision.HIGHEST)

def mixer_apply(mixer_params, source, inside):
    a_log, a_imag, c_height, c_width, log_dt, skip_gain = mixer_params
    crop_len = source.shape[2]
    step_size = jnp.exp(log_dt)
    kern_height = toeplitz(mixer_kernel(a_log, a_imag, c_height, step_size[0], crop_len), crop_len)
    kern_width = toeplitz(mixer_kernel(a_log, a_imag, c_width, step_size[1], crop_len), crop_len)
    masked = inside[..., None] * source
    along_rows = jnp.einsum('chk,nakbwc->nahbwc', kern_height, masked, precision=lax.Precision.HIGHEST)
    conv_out = jnp.einsum('cwk,nahbkc->nahbwc', kern_width, along_rows, precision=lax.Precision.HIGHEST)
    return inside[..., None] * conv_out + skip_gain * source

def reference(inputs, crop_size, crop_offset, a_log, a_imag, c_height, c_width, log_dt, skip_gain, ln_gain, ln_bias, w_in, b_in, w_out, b_out, layer_scale, grad_out):
    canvases = crop_size.shape[0]
    inside = crop_mask(crop_size, crop_offset, CROP)

    def forward(source, p_alog, p_aimag, p_ch, p_cw, p_dt, p_skip, p_gain, p_bias, p_win, p_bin, p_wout, p_bout, p_scale):
        shaped = source.reshape(canvases, 2, CROP, 2, CROP, D)
        mixed = low(mixer_apply((p_alog, p_aimag, p_ch, p_cw, p_dt, p_skip), shaped, inside).reshape(-1, D))
        row_mean = lax.optimization_barrier(jnp.mean(mixed, axis=1, keepdims=True))
        centered = mixed - row_mean
        row_scale = lax.rsqrt(lax.optimization_barrier(jnp.mean(centered * centered, axis=1, keepdims=True)) + EPS)
        normed_low = low(centered * row_scale * p_gain + p_bias)
        pre_act = low_back(jnp.dot(normed_low, p_win, precision=lax.Precision.HIGHEST) + p_bin)
        hidden = low(jax.nn.gelu(pre_act))
        branch = low_back(jnp.dot(hidden, p_wout, precision=lax.Precision.HIGHEST) + p_bout)
        return source.reshape(-1, D) + p_scale * branch
    source_rows = jnp.transpose(inputs.astype(jnp.float32))
    outcome, pullback = jax.vjp(forward, source_rows, a_log, a_imag, c_height, c_width, log_dt, skip_gain, ln_gain, ln_bias, w_in.astype(jnp.float32), b_in, w_out.astype(jnp.float32), b_out, layer_scale)
    grads = pullback(jnp.transpose(grad_out.astype(jnp.float32)))
    return (jnp.transpose(outcome).astype(jnp.bfloat16), jnp.transpose(grads[0]), grads[1], grads[2], grads[3], grads[4], grads[5], grads[6], grads[7], grads[8], grads[9], grads[10], grads[11], grads[12], grads[13])
```

```python
import functools

import jax
import jax.numpy as jnp
from jax import lax
from jax.experimental import pallas as pl
from jax.experimental.pallas import tpu as pltpu
from jax.sharding import PartitionSpec as P

F32, BF16 = jnp.float32, jnp.bfloat16
CROP = 14
SIDE = 2 * CROP
NPIX = SIDE * SIDE
LANES = 128
GROUP = 32
STEP = 896
FTILE = 256
EPS = 1e-06
GELU_C = 0.7978845608028654
GELU_A = 0.044715
VMEM = 60 << 20


def nn(a, b):
    return lax.dot_general(a, b, (((1,), (0,)), ((), ())), preferred_element_type=F32)


def nt(a, b):
    return lax.dot_general(a, b, (((1,), (1,)), ((), ())), preferred_element_type=F32)


def lanes_to_rows(load, rows):
    @pl.loop(0, rows.shape[0] // STEP)
    def _(j):
        off = pl.multiple_of(j * STEP, LANES)
        rows[pl.ds(off, STEP), :] = jnp.transpose(load(off).astype(F32))


def rows_to_lanes(rows, store):
    @pl.loop(0, rows.shape[0] // STEP)
    def _(j):
        off = pl.multiple_of(j * STEP, LANES)
        store(off, jnp.transpose(rows[pl.ds(off, STEP), :]).astype(BF16))


def conv(y, taps):
    return [sum((taps[l] * y[i - l] for l in range(1, i + 1)), taps[0] * y[i]) for i in range(CROP)]


def conv_back(y, taps):
    return [
        sum((taps[l] * y[i + l] for l in range(1, CROP - i)), taps[0] * y[i]) for i in range(CROP)
    ]


def tap_rows(kern_ref, base):
    return [jnp.broadcast_to(kern_ref[pl.ds(base + l, 1), :], (8, LANES)) for l in range(CROP)]


def spot(slot, h, w):
    first = (slot // 2) * (CROP * SIDE) + (slot % 2) * CROP
    return pl.ds(first + h * SIDE + w, 8, stride=NPIX)


def mix_fwd_kernel(x_ref, kern_ref, mask_ref, out_ref, rows, inner):
    lanes_to_rows(lambda o: x_ref[:, 0, :, pl.ds(o, STEP)].reshape(LANES, STEP), rows)
    skip = jnp.broadcast_to(kern_ref[pl.ds(2 * CROP, 1), :], (8, LANES))

    @pl.loop(0, 4)
    def _(slot):
        @pl.loop(0, CROP)
        def _(h):
            taps = tap_rows(kern_ref, CROP)
            row_in = mask_ref[slot, h]
            y = [rows[spot(slot, h, w), :] * mask_ref[slot, CROP + w] for w in range(CROP)]
            for w, v in enumerate(conv(y, taps)):
                inner[h, w] = v * row_in

        @pl.loop(0, CROP)
        def _(w):
            taps = tap_rows(kern_ref, 0)
            col_in = mask_ref[slot, CROP + w]
            y = [inner[h, w] for h in range(CROP)]
            for h, v in enumerate(conv(y, taps)):
                at = spot(slot, h, w)
                rows[at, :] = v * (mask_ref[slot, h] * col_in) + skip * rows[at, :]

    def store(off, v):
        out_ref[:, 0, :, pl.ds(off, STEP)] = v.reshape(4, GROUP, STEP)

    rows_to_lanes(rows, store)


def mix_fwd(x4, kern, mask):
    pix = x4.shape[3]
    tile = pl.BlockSpec((4, 1, GROUP, pix), lambda q: (0, q, 0, 0))
    return pl.pallas_call(
        mix_fwd_kernel,
        grid=(x4.shape[1],),
        out_shape=jax.ShapeDtypeStruct(x4.shape, BF16),
        in_specs=[
            tile,
            pl.BlockSpec((32, LANES), lambda q: (0, q)),
            pl.BlockSpec(mask.shape, lambda q: (0, 0, 0, 0)),
        ],
        out_specs=tile,
        scratch_shapes=[pltpu.VMEM((pix, LANES), F32), pltpu.VMEM((CROP, CROP, 8, LANES), F32)],
        compiler_params=pltpu.CompilerParams(vmem_limit_bytes=VMEM),
        cost_estimate=pl.CostEstimate(flops=25 * 10**9, bytes_accessed=10**7, transcendentals=0),
        name="mix_fwd",
    )(x4, kern, mask)


def mix_bwd_kernel(x_ref, g_ref, kern_ref, mask_ref, out_ref, gk_ref, rows, grow, inner, mid):
    lanes_to_rows(lambda o: x_ref[:, 0, :, pl.ds(o, STEP)].reshape(LANES, STEP), rows)
    lanes_to_rows(lambda o: g_ref[:, 0, :, pl.ds(o, STEP)].reshape(LANES, STEP), grow)
    skip = jnp.broadcast_to(kern_ref[pl.ds(2 * CROP, 1), :], (8, LANES))
    zero = jnp.zeros((8, LANES), F32)

    def per_slot(slot, sums):
        gk_height, gk_width, gskip = sums

        @pl.loop(0, CROP)
        def _(h):
            taps = tap_rows(kern_ref, CROP)
            row_in = mask_ref[slot, h]
            y = [rows[spot(slot, h, w), :] * mask_ref[slot, CROP + w] for w in range(CROP)]
            for w, v in enumerate(conv(y, taps)):
                inner[h, w] = v * row_in

        def down(w, acc):
            taps = tap_rows(kern_ref, 0)
            col_in = mask_ref[slot, CROP + w]
            u = [grow[spot(slot, h, w), :] * (mask_ref[slot, h] * col_in) for h in range(CROP)]
            for h, v in enumerate(conv_back(u, taps)):
                mid[h, w] = v * mask_ref[slot, h]
            a = [inner[h, w] for h in range(CROP)]
            return tuple(
                sum((u[h] * a[h - l] for h in range(l, CROP)), acc[l]) for l in range(CROP)
            )

        gk_height = lax.fori_loop(0, CROP, down, gk_height)

        def across(h, acc):
            gk_width, gskip = acc
            taps = tap_rows(kern_ref, CROP)
            u = [mid[h, w] for w in range(CROP)]
            x = [rows[spot(slot, h, w), :] for w in range(CROP)]
            y = [x[w] * mask_ref[slot, CROP + w] for w in range(CROP)]
            gk_width = tuple(
                sum((u[w] * y[w - l] for w in range(l, CROP)), gk_width[l]) for l in range(CROP)
            )
            for w, v in enumerate(conv_back(u, taps)):
                at = spot(slot, h, w)
                g = grow[at, :]
                gskip = gskip + g * x[w]
                grow[at, :] = v * mask_ref[slot, CROP + w] + skip * g
            return gk_width, gskip

        gk_width, gskip = lax.fori_loop(0, CROP, across, (gk_width, gskip))
        return gk_height, gk_width, gskip

    gk_height, gk_width, gskip = lax.fori_loop(
        0, 4, per_slot, ((zero,) * CROP, (zero,) * CROP, zero)
    )
    gk_ref[...] = jnp.zeros_like(gk_ref)
    for row, v in enumerate((*gk_height, *gk_width, gskip)):
        gk_ref[pl.ds(row, 1), :] = jnp.sum(v, axis=0, keepdims=True)

    def store(off, v):
        out_ref[:, :, pl.ds(off, STEP)] = v.reshape(4, GROUP, STEP)

    rows_to_lanes(grow, store)


def mix_bwd(x4, g4, kern, mask, q):
    pix = x4.shape[3]
    tile = pl.BlockSpec((4, 1, GROUP, pix), lambda i: (0, q, 0, 0))
    return pl.pallas_call(
        mix_bwd_kernel,
        grid=(1,),
        out_shape=(
            jax.ShapeDtypeStruct((4, GROUP, pix), BF16),
            jax.ShapeDtypeStruct((32, LANES), F32),
        ),
        in_specs=[
            tile,
            tile,
            pl.BlockSpec((32, LANES), lambda i: (0, q)),
            pl.BlockSpec(mask.shape, lambda i: (0, 0, 0, 0)),
        ],
        out_specs=(
            pl.BlockSpec((4, GROUP, pix), lambda i: (0, 0, 0)),
            pl.BlockSpec((32, LANES), lambda i: (0, 0)),
        ),
        scratch_shapes=[pltpu.VMEM((pix, LANES), F32)] * 2
        + [pltpu.VMEM((CROP, CROP, 8, LANES), F32)] * 2,
        compiler_params=pltpu.CompilerParams(vmem_limit_bytes=VMEM),
        cost_estimate=pl.CostEstimate(flops=20 * 10**9, bytes_accessed=10**7, transcendentals=0),
        name="mix_bwd",
    )(x4, g4, kern, mask)


def norm(m):
    centered = m - jnp.mean(m, axis=0, keepdims=True)
    scale = lax.rsqrt(jnp.mean(centered * centered, axis=0, keepdims=True) + EPS)
    return centered * scale, scale


def ff_fwd_kernel(mix_ref, x_ref, win_t, wout_t, chan_ref, bin_ref, res_ref, hid_ref, slope_ref):
    normed, _ = norm(mix_ref[...].astype(F32))
    low = (normed * chan_ref[:, 0:1] + chan_ref[:, 1:2]).astype(BF16)
    for t in range(win_t.shape[0] // FTILE):
        sl = pl.ds(t * FTILE, FTILE)
        pre = nn(win_t[sl, :], low) + bin_ref[sl, 0:1]
        square = pre * pre
        th = jnp.tanh(pre * (GELU_C + (GELU_C * GELU_A) * square))
        half = 0.5 * th + 0.5
        hid_ref[sl, :] = (pre * half).astype(BF16)
        inner_slope = GELU_C + (3 * GELU_C * GELU_A) * square
        slope_ref[sl, :] = (half + pre * (0.5 - 0.5 * th * th) * inner_slope).astype(BF16)
    branch = nn(wout_t[...], hid_ref[...]) + chan_ref[:, 2:3]
    res_ref[...] = (x_ref[...].astype(F32) + chan_ref[:, 3:4] * branch).astype(BF16)


def lane_block(rows):
    return pl.BlockSpec((rows, STEP), lambda i: (0, i))


def whole(a):
    return pl.BlockSpec(a.shape, lambda i: (0,) * len(a.shape))


def ff_fwd(mix, x, win_t, wout_t, chan, bin_):
    width, pix = mix.shape
    ff = win_t.shape[0]
    return pl.pallas_call(
        ff_fwd_kernel,
        grid=(pix // STEP,),
        out_shape=(
            jax.ShapeDtypeStruct((width, pix), BF16),
            jax.ShapeDtypeStruct((ff, pix), BF16),
            jax.ShapeDtypeStruct((ff, pix), BF16),
        ),
        in_specs=[lane_block(width), lane_block(width)]
        + [whole(a) for a in (win_t, wout_t, chan, bin_)],
        out_specs=(lane_block(width), lane_block(ff), lane_block(ff)),
        compiler_params=pltpu.CompilerParams(vmem_limit_bytes=VMEM),
        cost_estimate=pl.CostEstimate(
            flops=4 * width * ff * pix, bytes_accessed=6 * 10**7, transcendentals=ff * pix
        ),
        name="ff_fwd",
    )(mix, x, win_t, wout_t, chan, bin_)


def fold(v):
    return sum(
        (v[:, i * LANES : (i + 1) * LANES] for i in range(1, v.shape[1] // LANES)), v[:, :LANES]
    )


def ff_bwd_kernel(
    go_ref, mix_ref, hid_ref, slope_ref, win, wout, chan_ref, gm_ref, dwo, dwi, bin_ref, vec_ref, gp
):
    @pl.when(pl.program_id(0) == 0)
    def _():
        for ref in (dwo, dwi, bin_ref, vec_ref):
            ref[...] = jnp.zeros_like(ref)

    go = go_ref[...].astype(F32)
    gb = (go * chan_ref[:, 3:4]).astype(BF16)
    vec_ref[0] += fold(gb.astype(F32))
    vec_ref[3] += fold(go)
    normed, scale = norm(mix_ref[...].astype(F32))
    low = (normed * chan_ref[:, 0:1] + chan_ref[:, 1:2]).astype(BF16)
    for t in range(wout.shape[0] // FTILE):
        sl = pl.ds(t * FTILE, FTILE)
        tile = (nn(wout[sl, :], gb) * slope_ref[sl, :].astype(F32)).astype(BF16)
        gp[sl, :] = tile
        bin_ref[sl, :] += fold(tile.astype(F32))
        dwo[sl, :] += nt(hid_ref[sl, :], gb)
        dwi[sl, :] += nt(tile, low)
    gn = nn(win[...], gp[...])
    vec_ref[1] += fold(gn * normed)
    vec_ref[2] += fold(gn)
    g1 = gn * chan_ref[:, 0:1]
    m1 = jnp.mean(g1, axis=0, keepdims=True)
    m2 = jnp.mean(g1 * normed, axis=0, keepdims=True)
    gm_ref[...] = scale * (g1 - m1 - normed * m2)


def ff_bwd(go, mix, hid, slope, win, wout, chan):
    width, pix = mix.shape
    ff = wout.shape[0]
    shapes = (
        jax.ShapeDtypeStruct((width, pix), F32),
        jax.ShapeDtypeStruct((ff, width), F32),
        jax.ShapeDtypeStruct((ff, width), F32),
        jax.ShapeDtypeStruct((ff, LANES), F32),
        jax.ShapeDtypeStruct((4, width, LANES), F32),
    )
    return pl.pallas_call(
        ff_bwd_kernel,
        grid=(pix // STEP,),
        out_shape=shapes,
        in_specs=[lane_block(width), lane_block(width), lane_block(ff), lane_block(ff)]
        + [whole(a) for a in (win, wout, chan)],
        out_specs=(lane_block(width),) + tuple(whole(s) for s in shapes[1:]),
        scratch_shapes=[pltpu.VMEM((ff, STEP), BF16)],
        compiler_params=pltpu.CompilerParams(vmem_limit_bytes=VMEM),
        cost_estimate=pl.CostEstimate(
            flops=8 * width * ff * pix, bytes_accessed=7 * 10**7, transcendentals=0
        ),
        name="ff_bwd",
    )(go, mix, hid, slope, win, wout, chan)


def finish_kernel(g_ref, go_ref, *rest):
    rest[-1][...] = go_ref[...].astype(F32) + g_ref[0].astype(F32)


def finish(g, grad_out, q, earlier):
    parts, rows, pix = g.shape
    tile = pl.BlockSpec((rows, pix), lambda s: (q, s))
    operands = (g, grad_out) if earlier is None else (g, grad_out, earlier)
    return pl.pallas_call(
        finish_kernel,
        grid=(parts,),
        out_shape=jax.ShapeDtypeStruct(grad_out.shape, F32),
        in_specs=[pl.BlockSpec((1, rows, pix), lambda s: (s, 0, 0)), tile]
        + [pl.BlockSpec(memory_space=pl.ANY)] * (earlier is not None),
        out_specs=tile,
        input_output_aliases={} if earlier is None else {2: 0},
        compiler_params=pltpu.CompilerParams(vmem_limit_bytes=32 << 20),
        name="finish",
    )(*operands)


def lag_kernels(a_log, a_imag, c_height, c_width, log_dt):
    step = jnp.exp(log_dt)[:, None, :, None]
    lags = jnp.arange(CROP, dtype=F32)[None, :, None, None]
    decays = jnp.exp(-(step * jnp.exp(a_log)[None, None]) * lags)
    phases = step * a_imag[None, None] * lags
    coef = jnp.stack([c_height, c_width])
    waves = coef[:, 0][:, None] * jnp.cos(phases) - coef[:, 1][:, None] * jnp.sin(phases)
    return jnp.sum(decays * waves, axis=3)


def slot_mask(crop_size, crop_offset):
    spots = jnp.arange(CROP, dtype=jnp.int32)
    low = crop_offset[..., None]
    inside = (spots >= low) & (spots < low + crop_size[..., None])
    inside = jnp.transpose(inside, (1, 2, 3, 0)).reshape(4, 2 * CROP, crop_size.shape[0])
    return jnp.broadcast_to(inside.astype(F32)[..., None], (*inside.shape, LANES))


def per_device(
    parts,
    groups,
    inputs,
    crop_size,
    crop_offset,
    a_log,
    a_imag,
    c_height,
    c_width,
    log_dt,
    skip_gain,
    ln_gain,
    ln_bias,
    w_in,
    b_in,
    w_out,
    b_out,
    layer_scale,
    grad_out,
):
    local, pixels = inputs.shape
    pix = pixels // parts
    width = local * parts
    tiles = local // GROUP
    me = lax.axis_index("tensor")

    def exchange(a):
        return lax.all_to_all(a, "tensor", 0, 0, tiled=True)

    def by_owner(a):
        return jnp.transpose(a.reshape(local, parts, pix), (1, 0, 2))

    x_all = exchange(by_owner(inputs))
    x_all, late = lax.optimization_barrier((x_all, grad_out))
    go_all = exchange(by_owner(late))

    lag, lag_back = jax.vjp(lag_kernels, a_log, a_imag, c_height, c_width, log_dt)
    kern = jnp.concatenate(
        [lag.reshape(2 * CROP, local), skip_gain[None], jnp.zeros((3, local), F32)]
    )
    kern = lax.all_gather(kern, "tensor")
    kern = jnp.transpose(kern.reshape(parts, 32, tiles, GROUP), (1, 2, 0, 3)).reshape(32, width)
    mine = crop_size.shape[0] // parts
    mask = slot_mask(
        lax.dynamic_slice_in_dim(crop_size, me * mine, mine),
        lax.dynamic_slice_in_dim(crop_offset, me * mine, mine),
    )
    win_t = lax.all_gather(jnp.transpose(w_in), "tensor", axis=0, tiled=True)
    wout = lax.all_gather(w_out, "tensor", axis=0, tiled=True)
    bin_ = lax.all_gather(b_in, "tensor", axis=0, tiled=True)
    ff = bin_.shape[0]
    chan = jnp.pad(jnp.stack([ln_gain, ln_bias, b_out, layer_scale], 1), ((0, 0), (0, LANES - 4)))

    x4 = x_all.reshape(parts, tiles, GROUP, pix)
    mixed = mix_fwd(x4, kern, mask).reshape(width, pix)
    res, hid, slope = ff_fwd(
        mixed,
        x_all.reshape(width, pix),
        win_t,
        jnp.transpose(wout),
        chan,
        jnp.broadcast_to(bin_[:, None], (ff, LANES)),
    )
    go_all, res = lax.optimization_barrier((go_all, res))
    res_own = exchange(res.reshape(parts, local, pix))
    gm, dwo, dwi, g_bin, vec = ff_bwd(
        go_all.reshape(width, pix), mixed, hid, slope, jnp.transpose(win_t), wout, chan
    )
    g4 = gm.reshape(parts, tiles, GROUP, pix)
    grad_inputs, gk = None, []
    for q in range(tiles):
        gx, gk_q = mix_bwd(x4, g4, kern, mask, q)
        gk.append(gk_q)
        grad_inputs = finish(exchange(gx), grad_out, q, grad_inputs)
    result = jnp.transpose(res_own, (1, 0, 2)).reshape(local, pixels)

    rows = ff // parts // groups
    dw = jnp.stack([dwo, dwi]).reshape(2, parts, groups, rows, width)
    dw = lax.psum_scatter(dw, "dp", scatter_dimension=2)
    dw = lax.psum_scatter(dw, "tensor", scatter_dimension=1)
    dw = lax.all_gather(dw, "dp", axis=1, tiled=True)

    vec = jnp.sum(vec, axis=2)
    g_scale = jnp.sum(dwo * wout.astype(F32), axis=0) / layer_scale + b_out * vec[3]
    vec = vec.at[3].set(g_scale)
    gk = jnp.stack(gk)
    vec, g_bin, gk = lax.psum((vec, jnp.sum(g_bin, axis=1), gk), ("dp", "tensor"))
    vec = lax.dynamic_slice_in_dim(vec, me * local, local, 1)
    g_bin = lax.dynamic_slice_in_dim(g_bin, me * b_in.shape[0], b_in.shape[0])
    gk = lax.dynamic_slice_in_dim(gk, me * GROUP, GROUP, 2)
    gk = jnp.transpose(gk, (1, 0, 2)).reshape(32, local)
    lag_grads = lag_back(gk[: 2 * CROP].reshape(2, CROP, local))
    return (
        result,
        grad_inputs,
        lag_grads[0],
        lag_grads[1],
        lag_grads[2],
        lag_grads[3],
        lag_grads[4],
        gk[2 * CROP],
        vec[1],
        vec[2],
        jnp.transpose(dw[1]),
        g_bin,
        dw[0],
        vec[0],
        vec[3],
    )


def solution(mesh):
    in_specs = (
        P("tensor", "dp"),
        P("dp", None, None),
        P("dp", None, None),
        P("tensor", None),
        P("tensor", None),
        P(None, "tensor", None),
        P(None, "tensor", None),
        P(None, "tensor"),
        P("tensor"),
        P(),
        P(),
        P(None, "tensor"),
        P("tensor"),
        P("tensor", None),
        P(),
        P(),
        P("tensor", "dp"),
    )
    out_specs = (
        P("tensor", "dp"),
        P("tensor", "dp"),
        P("tensor", None),
        P("tensor", None),
        P(None, "tensor", None),
        P(None, "tensor", None),
        P(None, "tensor"),
        P("tensor"),
        P("tensor"),
        P("tensor"),
        P(None, "tensor"),
        P("tensor"),
        P("tensor", None),
        P("tensor"),
        P("tensor"),
    )
    return jax.shard_map(
        functools.partial(per_device, mesh.shape["tensor"], mesh.shape["dp"]),
        mesh=mesh,
        in_specs=in_specs,
        out_specs=out_specs,
        check_vma=False,
    )
```

```python
import functools

import jax
import jax.numpy as jnp
from jax import lax
from jax.experimental import pallas as pl
from jax.experimental.pallas import tpu as pltpu
from jax.sharding import PartitionSpec as P

F32, BF16 = jnp.float32, jnp.bfloat16
CROP = 14
SIDE = 2 * CROP
NPIX = SIDE * SIDE
LANES = 128
GROUP = 32
STEP = 896
EPS = 1e-06
GELU_C = 0.7978845608028654
GELU_A = 0.044715
VMEM = 63 << 20
MESH = pl.DeviceIdType.MESH


def nn(a, b):
    return lax.dot_general(a, b, (((1,), (0,)), ((), ())), preferred_element_type=F32)


def nt(a, b):
    return lax.dot_general(a, b, (((1,), (1,)), ((), ())), preferred_element_type=F32)


def conv(y, taps):
    return [sum((taps[l] * y[i - l] for l in range(1, i + 1)), taps[0] * y[i]) for i in range(CROP)]


def conv_back(y, taps):
    return [
        sum((taps[l] * y[i + l] for l in range(1, CROP - i)), taps[0] * y[i]) for i in range(CROP)
    ]


def spot(slot, h, w):
    first = (slot // 2) * (CROP * SIDE) + (slot % 2) * CROP
    return pl.ds(first + h * SIDE + w, 8, stride=NPIX)


def lanes_to_rows(load, rows):
    @pl.loop(0, rows.shape[0] // STEP)
    def _(j):
        off = pl.multiple_of(j * STEP, LANES)
        rows[pl.ds(off, STEP), :] = jnp.transpose(load(off).astype(F32))


def rows_to_lanes(rows, store):
    @pl.loop(0, rows.shape[0] // STEP)
    def _(j):
        off = pl.multiple_of(j * STEP, LANES)
        store(off, jnp.transpose(rows[pl.ds(off, STEP), :]).astype(BF16))


def tap_rows(kern, q, base):
    return [jnp.broadcast_to(kern[q, pl.ds(base + l, 1), :], (8, LANES)) for l in range(CROP)]


def tile_of(ref, q, off):
    return ref[:, pl.ds(pl.multiple_of(q * GROUP, GROUP), GROUP), pl.ds(off, STEP)].reshape(
        LANES, STEP
    )


def put_tile(ref, q, off, v):
    ref[:, pl.ds(pl.multiple_of(q * GROUP, GROUP), GROUP), pl.ds(off, STEP)] = v.reshape(
        ref.shape[0], GROUP, STEP
    )


def along_width(q, slot, rows, kern, mask, inner):
    @pl.loop(0, CROP)
    def _(h):
        taps = tap_rows(kern, q, CROP)
        row_in = mask[slot, h]
        y = [rows[spot(slot, h, w), :] * mask[slot, CROP + w] for w in range(CROP)]
        for w, v in enumerate(conv(y, taps)):
            inner[h, w] = v * row_in


def mix_fwd(q, x_all, rows, kern, mask, inner, mixed):
    lanes_to_rows(lambda off: tile_of(x_all, q, off), rows)
    skip = jnp.broadcast_to(kern[q, pl.ds(2 * CROP, 1), :], (8, LANES))

    @pl.loop(0, 4)
    def _(slot):
        along_width(q, slot, rows, kern, mask, inner)

        @pl.loop(0, CROP)
        def _(w):
            taps = tap_rows(kern, q, 0)
            col_in = mask[slot, CROP + w]
            y = [inner[h, w] for h in range(CROP)]
            for h, v in enumerate(conv(y, taps)):
                at = spot(slot, h, w)
                rows[at, :] = v * (mask[slot, h] * col_in) + skip * rows[at, :]

    rows_to_lanes(rows, lambda off, v: put_tile(mixed, q, off, v))


def mix_bwd(q, x_all, rows, grow, kern, mask, inner, mid, out, gkern):
    lanes_to_rows(lambda off: tile_of(x_all, q, off), rows)
    skip = jnp.broadcast_to(kern[q, pl.ds(2 * CROP, 1), :], (8, LANES))
    zero = jnp.zeros((8, LANES), F32)

    def per_slot(slot, sums):
        gk_height, gk_width, gskip = sums
        along_width(q, slot, rows, kern, mask, inner)

        def down(w, acc):
            taps = tap_rows(kern, q, 0)
            col_in = mask[slot, CROP + w]
            u = [grow[q, spot(slot, h, w), :] * (mask[slot, h] * col_in) for h in range(CROP)]
            for h, v in enumerate(conv_back(u, taps)):
                mid[h, w] = v * mask[slot, h]
            a = [inner[h, w] for h in range(CROP)]
            return tuple(
                sum((u[h] * a[h - l] for h in range(l, CROP)), acc[l]) for l in range(CROP)
            )

        gk_height = lax.fori_loop(0, CROP, down, gk_height)

        def across(h, acc):
            gk_width, gskip = acc
            taps = tap_rows(kern, q, CROP)
            u = [mid[h, w] for w in range(CROP)]
            x = [rows[spot(slot, h, w), :] for w in range(CROP)]
            y = [x[w] * mask[slot, CROP + w] for w in range(CROP)]
            gk_width = tuple(
                sum((u[w] * y[w - l] for w in range(l, CROP)), gk_width[l]) for l in range(CROP)
            )
            for w, v in enumerate(conv_back(u, taps)):
                at = spot(slot, h, w)
                g = grow[q, at, :]
                gskip = gskip + g * x[w]
                grow[q, at, :] = v * mask[slot, CROP + w] + skip * g
            return gk_width, gskip

        gk_width, gskip = lax.fori_loop(0, CROP, across, (gk_width, gskip))
        return gk_height, gk_width, gskip

    gk_height, gk_width, gskip = lax.fori_loop(
        0, 4, per_slot, ((zero,) * CROP, (zero,) * CROP, zero)
    )
    gkern[q] = jnp.zeros((LANES, LANES), F32)
    for row, v in enumerate((*gk_height, *gk_width, gskip)):
        gkern[q, pl.ds(row, 1), :] = jnp.sum(v, axis=0, keepdims=True)
    rows_to_lanes(grow.at[q], lambda off, v: put_tile(out, q, off, v))


def lag_waves(step, a_log, a_imag):
    rate = -step * jnp.exp(a_log)
    phase = step * a_imag
    size = jnp.exp(rate)
    re1, im1 = size * jnp.cos(phase), size * jnp.sin(phase)
    re, im = jnp.ones_like(re1), jnp.zeros_like(im1)
    out = []
    for _ in range(CROP):
        out.append((re, im))
        re, im = re * re1 - im * im1, re * im1 + im * re1
    return rate, phase, out


def column_set(acc, k, col):
    lane = lax.broadcasted_iota(jnp.int32, acc.shape, 1)
    return jnp.where(lane == k, col, acc)


def lag_kernels(steps, skip, a_log, a_imag, coefs):
    acc = jnp.zeros((a_log.shape[0], LANES), F32)
    for j in range(2):
        _, _, waves = lag_waves(steps[j], a_log[...], a_imag[...])
        for l, (re, im) in enumerate(waves):
            col = jnp.sum(coefs[j][0] * re - coefs[j][1] * im, axis=1, keepdims=True)
            acc = column_set(acc, CROP * j + l, col)
    return column_set(acc, 2 * CROP, skip)


def lag_grads(cols, steps, a_log, a_imag, coefs, g_alog, g_aimag, g_coefs):
    ga, gi, gdt = 0.0, 0.0, []
    for j in range(2):
        rate, phase, waves = lag_waves(steps[j], a_log[...], a_imag[...])
        cre, cim = coefs[j][0], coefs[j][1]
        g_re = g_im = p = r = 0.0
        for l, (re, im) in enumerate(waves):
            g = cols[:, CROP * j + l : CROP * j + l + 1]
            g_re = g_re + g * re
            g_im = g_im - g * im
            if l:
                p = p + (l * g) * (cre * re - cim * im)
                r = r - (l * g) * (cre * im + cim * re)
        g_coefs[j][0] = g_re
        g_coefs[j][1] = g_im
        ga = ga + p * rate
        gi = gi + r * steps[j]
        gdt.append(jnp.sum(p * rate + r * phase, axis=1, keepdims=True))
    g_alog[...] = ga
    g_aimag[...] = gi
    return gdt


def norm(m):
    centered = m - jnp.mean(m, axis=0, keepdims=True)
    scale = lax.rsqrt(jnp.mean(centered * centered, axis=0, keepdims=True) + EPS)
    return centered * scale, scale


def fold(v):
    return sum(
        (v[:, i * LANES : (i + 1) * LANES] for i in range(1, v.shape[1] // LANES)), v[:, :LANES]
    )


def block_kernel(
    parts,
    groups,
    x,
    go,
    size_ref,
    offset_ref,
    a_log,
    a_imag,
    c_height,
    c_width,
    log_dt,
    skip_gain,
    ln_gain,
    ln_bias,
    w_in,
    b_in,
    w_out,
    b_out,
    layer_scale,
    res_own,
    g_own,
    dw_own,
    g_alog,
    g_aimag,
    g_height,
    g_width,
    row_own,
    go_all,
    hid_far,
    slope_far,
    res,
    dw_peer,
    x_all,
    mixed,
    res_near,
    rows,
    grow,
    inner,
    mid,
    mask,
    kern_mine,
    kern_all,
    kern,
    gkern,
    bin_mine,
    bin_all,
    bin_col,
    chan,
    square,
    win,
    win_t,
    wout,
    wout_t,
    hid,
    slope,
    gp,
    go_near,
    dw,
    dw_sum,
    dw_tensor,
    dw_done,
    bin_acc,
    vec,
    col_mine,
    col_peer,
    col_sum,
    col_tensor,
    send,
    recv,
    own,
    hid_sem,
    slope_sem,
    go_sem,
    res_sem,
    gx_send,
    gx_recv,
    gx_own,
):
    local, pix = x_all.shape[1], x_all.shape[2]
    width = local * parts
    ff = win_t.shape[0]
    shard = ff // parts
    slab = shard // groups
    chunks = pix // STEP
    me = lax.axis_index("tensor")
    dp = lax.axis_index("dp")
    mine = lax.rem(dp, groups)
    first = dp - mine
    across = [{"tensor": lax.rem(me + s, parts)} for s in range(1, parts)]
    beside = [{"dp": first + lax.rem(mine + s, groups)} for s in range(1, groups)]

    barrier = pltpu.get_barrier_semaphore()
    for peer in across + beside:
        pl.semaphore_signal(barrier, inc=1, device_id=peer, device_id_type=MESH)
    pl.semaphore_wait(barrier, len(across) + len(beside))

    count = [0, 0]

    def remote(src, dst, peer, sems=None):
        if sems is None:
            sems = (send.at[count[0]], recv.at[count[0]])
            count[0] += 1
        copy = pltpu.make_async_remote_copy(
            src_ref=src,
            dst_ref=dst,
            send_sem=sems[0],
            recv_sem=sems[1],
            device_id=peer,
            device_id_type=MESH,
        )
        copy.start()
        return copy

    def near(src, dst, sem=None):
        if sem is None:
            sem = own.at[count[1]]
            count[1] += 1
        copy = pltpu.make_async_copy(src, dst, sem)
        copy.start()
        return copy

    sent = []

    def arrived(copies):
        for copy in copies:
            copy.wait_recv()
        sent.extend(copies)

    def pixels(ref, peer):
        return ref.at[:, pl.ds(pl.multiple_of(peer * pix, LANES), pix)]

    def to_owner(ref, out):
        copies = [remote(pixels(ref, p["tensor"]), out.at[me], p) for p in across]
        return copies, near(pixels(ref, me), out.at[me])

    x_copies, x_near = to_owner(x, x_all)
    my_slab = pl.ds(pl.multiple_of(mine * slab, slab), slab)
    my_cols = pl.ds(pl.multiple_of(me * shard, LANES), shard)
    w_near = [
        near(w_in.at[my_slab, :], win.at[my_slab, my_cols]),
        near(w_out.at[my_slab, :], wout.at[me, my_slab, :]),
    ]
    w_copies = [remote(w_in.at[my_slab, :], win.at[my_slab, my_cols], p) for p in across]
    w_copies += [remote(w_out.at[my_slab, :], wout.at[me, my_slab, :], p) for p in across]

    square[...] = jnp.zeros_like(square)
    square[0:2, 0:local] = log_dt[...]
    square[2:3, 0:local] = skip_gain[...]
    turned = jnp.transpose(square[:, 0:LANES])
    steps = [jnp.exp(turned[0:local, j : j + 1]) for j in range(2)]
    coefs = [c_height, c_width]
    kern_mine[...] = lag_kernels(steps, turned[0:local, 2:3], a_log, a_imag, coefs)
    bin_mine[...] = jnp.broadcast_to(b_in[...], bin_mine.shape)
    kern_all[me] = kern_mine[...]
    bin_all[me] = bin_mine[...]
    k_copies = [remote(kern_mine, kern_all.at[me], p) for p in across]
    k_copies += [remote(bin_mine, bin_all.at[me], p) for p in across]

    for copy in w_near:
        copy.wait()
    arrived(w_copies)
    w_copies = [remote(win.at[my_slab, :], win.at[my_slab, :], p) for p in beside]
    w_copies += [remote(wout.at[:, my_slab, :], wout.at[:, my_slab, :], p) for p in beside]

    row = 0
    for ref in (ln_gain, ln_bias, b_out, layer_scale):
        square[row : row + 1, :] = ref[...]
        row += 1
    for i in range(width // LANES):
        chan[i * LANES : (i + 1) * LANES, :] = jnp.transpose(square[:, i * LANES : (i + 1) * LANES])
    at = pl.ds(pl.multiple_of(me * 8, 8), 8)
    lo, extent = offset_ref[at, :], size_ref[at, :]
    for slot in range(4):
        for j in range(2):
            k = 2 * slot + j
            low = jnp.broadcast_to(lo[:, k : k + 1], (8, LANES))
            high = low + jnp.broadcast_to(extent[:, k : k + 1], (8, LANES))
            for s in range(CROP):
                mask[slot, CROP * j + s] = jnp.where((low <= s) & (s < high), 1.0, 0.0)
    arrived(k_copies)
    for q in range(local // GROUP):
        part = kern_all[:, q * GROUP : (q + 1) * GROUP, :].reshape(LANES, LANES)
        kern[q] = jnp.transpose(part)
    for t in range(parts):
        for i in range(shard // LANES):
            block = jnp.broadcast_to(bin_all[t, 0:1, i * LANES : (i + 1) * LANES], (LANES, LANES))
            bin_col[t * shard + i * LANES : t * shard + (i + 1) * LANES, :] = jnp.transpose(block)
    arrived(w_copies)
    for t in range(parts):
        cols = slice(t * shard, (t + 1) * shard)
        win_t[cols, :] = jnp.transpose(win[:, cols].astype(F32)).astype(BF16)
        wout_t[:, cols] = jnp.transpose(wout[t].astype(F32)).astype(BF16)

    arrived(x_copies)
    x_near.wait()
    go_copies, go_own = to_owner(go, go_all)

    @pl.loop(0, local // GROUP)
    def _(q):
        mix_fwd(q, x_all, rows, kern, mask, inner, mixed)

    def hid_copy(t, j, back):
        sl = pl.ds(t * shard, shard)
        lanes = pl.ds(pl.multiple_of(j * STEP, LANES), STEP)
        pair = [(hid.at[sl, :], hid_far.at[sl, lanes]), (slope.at[sl, :], slope_far.at[sl, lanes])]
        pair = [p[::-1] if back else p for p in pair]
        return [
            pltpu.make_async_copy(*p, sem.at[t]) for p, sem in zip(pair, (hid_sem, slope_sem))
        ]

    def res_copy(j):
        lanes = pl.ds(pl.multiple_of(j * STEP, LANES), STEP)
        return pltpu.make_async_copy(res_near, res.at[:, :, lanes], res_sem)

    def low_of(off):
        normed, scale = norm(mixed[:, :, pl.ds(off, STEP)].reshape(width, STEP).astype(F32))
        return normed, scale, (normed * chan[:, 0:1] + chan[:, 1:2]).astype(BF16)

    @pl.loop(0, chunks)
    def _(j):
        off = pl.multiple_of(j * STEP, LANES)
        _, _, low = low_of(off)
        for t in range(parts):
            sl = pl.ds(t * shard, shard)
            pre = nn(win_t[sl, :], low) + bin_col[sl, 0:1]
            square_pre = pre * pre
            th = jnp.tanh(pre * (GELU_C + (GELU_C * GELU_A) * square_pre))
            half = 0.5 * th + 0.5
            inner_slope = GELU_C + (3 * GELU_C * GELU_A) * square_pre

            @pl.when(j > 0)
            def _():
                for copy in hid_copy(t, j, False):
                    copy.wait()

            hid[sl, :] = (pre * half).astype(BF16)
            slope[sl, :] = (half + pre * (0.5 - 0.5 * th * th) * inner_slope).astype(BF16)
            for copy in hid_copy(t, j, False):
                copy.start()
        branch = nn(wout_t[...], hid[...]) + chan[:, 2:3]
        source = x_all[:, :, pl.ds(off, STEP)].reshape(width, STEP).astype(F32)
        out = (source + chan[:, 3:4] * branch).astype(BF16)

        @pl.when(j > 0)
        def _():
            res_copy(j).wait()

        res_near[...] = out.reshape(parts, local, STEP)
        res_copy(j).start()

    for t in range(parts):
        for copy in hid_copy(t, 0, False):
            copy.wait()
        for copy in hid_copy(t, 0, True):
            copy.start()

    res_copy(0).wait()

    arrived(go_copies)
    go_own.wait()
    res_copies = [remote(res.at[p["tensor"]], res_own.at[me], p) for p in across]
    res_mine = near(res.at[me], res_own.at[me])

    for ref in (dw, bin_acc, vec):
        ref[...] = jnp.zeros_like(ref)

    def go_copy(j):
        lanes = pl.ds(pl.multiple_of(j * STEP, LANES), STEP)
        return pltpu.make_async_copy(go_all.at[:, :, lanes], go_near, go_sem)

    go_copy(0).start()

    @pl.loop(0, chunks)
    def _(j):
        off = pl.multiple_of(j * STEP, LANES)
        go_copy(j).wait()
        grad = go_near[...].reshape(width, STEP).astype(F32)
        gb = (grad * chan[:, 3:4]).astype(BF16)
        vec[0] += fold(gb.astype(F32))
        vec[3] += fold(grad)

        @pl.when(j + 1 < chunks)
        def _():
            go_copy(j + 1).start()

        normed, scale, low = low_of(off)
        for t in range(parts):
            sl = pl.ds(t * shard, shard)
            for copy in hid_copy(t, j, True):
                copy.wait()
            tile = (nn(wout[t], gb) * slope[sl, :].astype(F32)).astype(BF16)
            gp[sl, :] = tile
            bin_acc[sl, :] += fold(tile.astype(F32))
            dw[0, t] += nt(hid[sl, :], gb)
            dw[1, t] += nt(tile, low)

            @pl.when(j + 1 < chunks)
            def _():
                for copy in hid_copy(t, j + 1, True):
                    copy.start()

        gn = nn(win[...], gp[...])
        vec[1] += fold(gn * normed)
        vec[2] += fold(gn)
        g1 = gn * chan[:, 0:1]
        m1 = jnp.mean(g1, axis=0, keepdims=True)
        m2 = jnp.mean(g1 * normed, axis=0, keepdims=True)
        gm = (scale * (g1 - m1 - normed * m2)).reshape(parts, local, STEP)
        for q in range(local // GROUP):
            block = gm[:, q * GROUP : (q + 1) * GROUP, :].reshape(LANES, STEP)
            grow[q, pl.ds(off, STEP), :] = jnp.transpose(block)

    def slab_of(peer):
        return pl.ds(pl.multiple_of((peer["dp"] - first) * slab, slab), slab)

    dw_near = near(dw.at[:, :, my_slab, :], dw_peer.at[:, :, my_slab, :])
    dw_copies = [
        remote(dw.at[:, :, slab_of(p), :], dw_peer.at[:, :, my_slab, :], p) for p in beside
    ]

    def gx_tile(q):
        return pl.ds(pl.multiple_of(q * GROUP, GROUP), GROUP)

    def gx_copies(q):
        at = gx_tile(q)
        return [
            pltpu.make_async_remote_copy(
                src_ref=mixed.at[p["tensor"], at, :],
                dst_ref=g_own.at[me, at, :],
                send_sem=gx_send.at[q, s],
                recv_sem=gx_recv.at[q, s],
                device_id=p,
                device_id_type=MESH,
            )
            for s, p in enumerate(across)
        ] + [pltpu.make_async_copy(mixed.at[me, at, :], g_own.at[me, at, :], gx_own.at[q])]

    @pl.loop(0, local // GROUP)
    def _(q):
        mix_bwd(q, x_all, rows, grow, kern, mask, inner, mid, mixed, gkern)
        for copy in gx_copies(q):
            copy.start()

    for q in range(local // GROUP):
        col_mine[:, q * GROUP : (q + 1) * GROUP, :] = jnp.transpose(gkern[q]).reshape(
            parts, GROUP, LANES
        )
    acc = col_mine[...].reshape(width, LANES)
    sums = [jnp.sum(vec[k], axis=1, keepdims=True) for k in range(4)]
    for k in range(3):
        acc = column_set(acc, 32 + k, sums[k])
    square[0:1, :] = sum(
        jnp.sum(wout[t].astype(F32) * dw[0, t], axis=0, keepdims=True) for t in range(parts)
    )
    products = jnp.concatenate(
        [
            jnp.transpose(square[:, i * LANES : (i + 1) * LANES])[:, 0:1]
            for i in range(width // LANES)
        ]
    )
    acc = column_set(acc, 35, products / chan[:, 3:4] + chan[:, 2:3] * sums[3])
    hidden_sums = jnp.sum(bin_acc[...], axis=1, keepdims=True)
    for k in range(shard // local):
        starts = [t * shard + k * local for t in range(parts)]
        acc = column_set(acc, 36 + k, jnp.concatenate([hidden_sums[i : i + local] for i in starts]))
    col_mine[...] = acc.reshape(parts, local, LANES)
    col_peer[mine] = col_mine[...]
    col_copies = [remote(col_mine, col_peer.at[mine], p) for p in beside]

    dw_near.wait()
    for copy in dw_copies:
        copy.wait()
    near(dw_peer, dw).wait()
    slabs = [dw[:, :, i * slab : (i + 1) * slab, :] for i in range(groups)]
    dw_sum[...] = sum(slabs[1:], slabs[0])
    dw_tensor[me] = dw_sum[:, me]
    dw_copies = [remote(dw_sum.at[:, p["tensor"]], dw_tensor.at[me], p) for p in across]
    arrived(col_copies)
    col_sum[...] = sum((col_peer[i] for i in range(1, groups)), col_peer[0])
    col_tensor[me] = col_sum[me]
    col_copies = [remote(col_sum.at[p["tensor"]], col_tensor.at[me], p) for p in across]
    arrived(dw_copies)
    dw_done[...] = sum((dw_tensor[i] for i in range(1, parts)), dw_tensor[0])
    dw_near = near(dw_done, dw_own.at[:, my_slab, :])
    dw_copies = [remote(dw_done, dw_own.at[:, my_slab, :], p) for p in beside]
    arrived(col_copies)
    cols = sum((col_tensor[i] for i in range(1, parts)), col_tensor[0])
    gdt = lag_grads(cols, steps, a_log, a_imag, coefs, g_alog, g_aimag, [g_height, g_width])
    for j in range(2):
        cols = column_set(cols, j, gdt[j])
    square[0:local, 0:LANES] = cols
    row_own[...] = jnp.transpose(square[:, 0:LANES])

    arrived(dw_copies)
    dw_near.wait()
    arrived(res_copies)
    res_mine.wait()

    @pl.loop(0, local // GROUP)
    def _(q):
        for copy in gx_copies(q):
            copy.wait()

    for copy in sent:
        copy.wait_send()


def block(parts, groups, args):
    x, size = args[0], args[2]
    local, pixels = x.shape
    pix = pixels // parts
    width = local * parts
    w_in = args[12]
    shard = w_in.shape[1]
    ff = shard * parts
    slab = shard // groups
    tiles = local // GROUP
    states = args[4].shape[1]
    shape = jax.ShapeDtypeStruct
    vmem = pl.BlockSpec(memory_space=pltpu.VMEM)
    hbm = pl.BlockSpec(memory_space=pl.ANY)
    in_specs = [hbm, hbm] + [vmem] * 10 + [hbm, vmem, hbm, vmem, vmem]
    outs = [
        (shape((parts, local, pix), BF16), hbm),
        (shape((parts, local, pix), BF16), hbm),
        (shape((2, shard, width), F32), hbm),
        (shape((local, states), F32), vmem),
        (shape((local, states), F32), vmem),
        (shape((2, local, states), F32), vmem),
        (shape((2, local, states), F32), vmem),
        (shape((LANES, LANES), F32), vmem),
        (shape((parts, local, pix), BF16), hbm),
        (shape((ff, pix), BF16), hbm),
        (shape((ff, pix), BF16), hbm),
        (shape((parts, local, pix), BF16), hbm),
        (shape((2, parts, shard, width), F32), hbm),
    ]
    remotes = 9 * (parts - 1) + 5 * (groups - 1)
    dma = pltpu.SemaphoreType.DMA
    scratch = [
        pltpu.VMEM((parts, local, pix), BF16),
        pltpu.VMEM((parts, local, pix), BF16),
        pltpu.VMEM((parts, local, STEP), BF16),
        pltpu.VMEM((pix, LANES), F32),
        pltpu.VMEM((tiles, pix, LANES), F32),
        pltpu.VMEM((CROP, CROP, 8, LANES), F32),
        pltpu.VMEM((CROP, CROP, 8, LANES), F32),
        pltpu.VMEM((4, 2 * CROP, 8, LANES), F32),
        pltpu.VMEM((local, LANES), F32),
        pltpu.VMEM((parts, local, LANES), F32),
        pltpu.VMEM((tiles, LANES, LANES), F32),
        pltpu.VMEM((tiles, LANES, LANES), F32),
        pltpu.VMEM((8, shard), F32),
        pltpu.VMEM((parts, 8, shard), F32),
        pltpu.VMEM((ff, LANES), F32),
        pltpu.VMEM((width, LANES), F32),
        pltpu.VMEM((LANES, width), F32),
        pltpu.VMEM((width, ff), BF16),
        pltpu.VMEM((ff, width), BF16),
        pltpu.VMEM((parts, shard, width), BF16),
        pltpu.VMEM((width, ff), BF16),
        pltpu.VMEM((ff, STEP), BF16),
        pltpu.VMEM((ff, STEP), BF16),
        pltpu.VMEM((ff, STEP), BF16),
        pltpu.VMEM((parts, local, STEP), BF16),
        pltpu.VMEM((2, parts, shard, width), F32),
        pltpu.VMEM((2, parts, slab, width), F32),
        pltpu.VMEM((parts, 2, slab, width), F32),
        pltpu.VMEM((2, slab, width), F32),
        pltpu.VMEM((ff, LANES), F32),
        pltpu.VMEM((4, width, LANES), F32),
        pltpu.VMEM((parts, local, LANES), F32),
        pltpu.VMEM((groups, parts, local, LANES), F32),
        pltpu.VMEM((parts, local, LANES), F32),
        pltpu.VMEM((parts, local, LANES), F32),
        dma((remotes,)),
        dma((remotes,)),
        dma((8,)),
        dma((parts,)),
        dma((parts,)),
        dma,
        dma,
        dma((tiles, parts - 1)),
        dma((tiles, parts - 1)),
        dma((tiles,)),
    ]
    return pl.pallas_call(
        functools.partial(block_kernel, parts, groups),
        out_shape=[o[0] for o in outs],
        in_specs=in_specs,
        out_specs=[o[1] for o in outs],
        scratch_shapes=scratch,
        compiler_params=pltpu.CompilerParams(
            collective_id=0, has_side_effects=True, vmem_limit_bytes=VMEM
        ),
        name="block",
    )(*args)


def finish_kernel(res_ref, g_ref, go_ref, result_ref, grad_ref):
    result_ref[...] = res_ref[0]
    grad_ref[...] = go_ref[...].astype(F32) + g_ref[0].astype(F32)


def finish(res_own, g_own, grad_out):
    parts, local, pix = g_own.shape
    part = pl.BlockSpec((1, GROUP, pix), lambda s, q: (s, q, 0))
    tile = pl.BlockSpec((GROUP, pix), lambda s, q: (q, s))
    return pl.pallas_call(
        finish_kernel,
        grid=(parts, local // GROUP),
        out_shape=(
            jax.ShapeDtypeStruct(grad_out.shape, BF16),
            jax.ShapeDtypeStruct(grad_out.shape, F32),
        ),
        in_specs=[part, part, tile],
        out_specs=(tile, tile),
        compiler_params=pltpu.CompilerParams(vmem_limit_bytes=32 << 20),
        name="finish",
    )(res_own, g_own, grad_out)


def per_device(
    parts,
    dp_size,
    inputs,
    crop_size,
    crop_offset,
    a_log,
    a_imag,
    c_height,
    c_width,
    log_dt,
    skip_gain,
    ln_gain,
    ln_bias,
    w_in,
    b_in,
    w_out,
    b_out,
    layer_scale,
    grad_out,
):
    local = inputs.shape[0]
    canvases = crop_size.shape[0]
    groups = min(dp_size, 8)
    args = (
        inputs,
        grad_out,
        crop_size.reshape(canvases, 8),
        crop_offset.reshape(canvases, 8),
        a_log,
        a_imag,
        c_height,
        c_width,
        log_dt,
        skip_gain[None],
        ln_gain[None],
        ln_bias[None],
        w_in,
        b_in[None],
        w_out,
        b_out[None],
        layer_scale[None],
    )
    out = block(parts, groups, args)
    result, grad_inputs = finish(out[0], out[1], grad_out)
    sums = tuple(out[2:8])
    if dp_size > groups:
        teams = [[r + groups * g for g in range(dp_size // groups)] for r in range(groups)]
        sums = lax.psum(sums, "dp", axis_index_groups=teams)
    dw, g_alog, g_aimag, g_height, g_width, rows = sums
    rows = rows[:, :local]
    return (
        result,
        grad_inputs,
        g_alog,
        g_aimag,
        g_height,
        g_width,
        rows[0:2],
        rows[2 * CROP],
        rows[33],
        rows[34],
        jnp.transpose(dw[1]),
        rows[36 : 36 + b_in.shape[0] // local].reshape(b_in.shape),
        dw[0],
        rows[32],
        rows[35],
    )


def solution(mesh):
    in_specs = (
        P("tensor", "dp"),
        P("dp", None, None),
        P("dp", None, None),
        P("tensor", None),
        P("tensor", None),
        P(None, "tensor", None),
        P(None, "tensor", None),
        P(None, "tensor"),
        P("tensor"),
        P(),
        P(),
        P(None, "tensor"),
        P("tensor"),
        P("tensor", None),
        P(),
        P(),
        P("tensor", "dp"),
    )
    out_specs = (
        P("tensor", "dp"),
        P("tensor", "dp"),
        P("tensor", None),
        P("tensor", None),
        P(None, "tensor", None),
        P(None, "tensor", None),
        P(None, "tensor"),
        P("tensor"),
        P("tensor"),
        P("tensor"),
        P(None, "tensor"),
        P("tensor"),
        P("tensor", None),
        P("tensor"),
        P("tensor"),
    )
    return jax.shard_map(
        functools.partial(per_device, mesh.shape["tensor"], mesh.shape["dp"]),
        mesh=mesh,
        in_specs=in_specs,
        out_specs=out_specs,
        check_vma=False,
    )
```

```python
import functools

import jax
import jax.numpy as jnp
from jax import lax
from jax.experimental import pallas as pl
from jax.experimental.pallas import tpu as pltpu
from jax.sharding import PartitionSpec as P

F32, BF16 = jnp.float32, jnp.bfloat16
CROP = 14
SIDE = 2 * CROP
NPIX = SIDE * SIDE
LANES = 128
GROUP = 32
STEP = 896
EPS = 1e-06
GELU_C = 0.7978845608028654
GELU_A = 0.044715
VMEM = 63 << 20
MESH = pl.DeviceIdType.MESH


def nn(a, b):
    return lax.dot_general(a, b, (((1,), (0,)), ((), ())), preferred_element_type=F32)


def nt(a, b):
    return lax.dot_general(a, b, (((1,), (1,)), ((), ())), preferred_element_type=F32)


def conv(y, taps):
    return [sum((taps[l] * y[i - l] for l in range(1, i + 1)), taps[0] * y[i]) for i in range(CROP)]


def conv_back(y, taps):
    return [
        sum((taps[l] * y[i + l] for l in range(1, CROP - i)), taps[0] * y[i]) for i in range(CROP)
    ]


def spot(slot, h, w):
    first = (slot // 2) * (CROP * SIDE) + (slot % 2) * CROP
    return pl.ds(first + h * SIDE + w, 8, stride=NPIX)


def lanes_to_rows(load, rows):
    @pl.loop(0, rows.shape[0] // STEP)
    def _(j):
        off = pl.multiple_of(j * STEP, LANES)
        rows[pl.ds(off, STEP), :] = jnp.transpose(load(off).astype(F32))


def rows_to_lanes(rows, store):
    @pl.loop(0, rows.shape[0] // STEP)
    def _(j):
        off = pl.multiple_of(j * STEP, LANES)
        store(off, jnp.transpose(rows[pl.ds(off, STEP), :]).astype(BF16))


def tap_rows(kern, q, base):
    return [jnp.broadcast_to(kern[q, pl.ds(base + l, 1), :], (8, LANES)) for l in range(CROP)]


def tile_of(ref, q, off):
    return ref[:, pl.ds(pl.multiple_of(q * GROUP, GROUP), GROUP), pl.ds(off, STEP)].reshape(
        LANES, STEP
    )


def put_tile(ref, q, off, v):
    ref[:, pl.ds(pl.multiple_of(q * GROUP, GROUP), GROUP), pl.ds(off, STEP)] = v.reshape(
        ref.shape[0], GROUP, STEP
    )


def along_width(q, slot, rows, kern, mask, inner):
    @pl.loop(0, CROP)
    def _(h):
        taps = tap_rows(kern, q, CROP)
        row_in = mask[slot, h]
        y = [rows[spot(slot, h, w), :] * mask[slot, CROP + w] for w in range(CROP)]
        for w, v in enumerate(conv(y, taps)):
            inner[h, w] = v * row_in


def mix_fwd(q, x_all, rows, kern, mask, inner, mixed):
    lanes_to_rows(lambda off: tile_of(x_all, q, off), rows)
    skip = jnp.broadcast_to(kern[q, pl.ds(2 * CROP, 1), :], (8, LANES))

    @pl.loop(0, 4)
    def _(slot):
        along_width(q, slot, rows, kern, mask, inner)

        @pl.loop(0, CROP)
        def _(w):
            taps = tap_rows(kern, q, 0)
            col_in = mask[slot, CROP + w]
            y = [inner[h, w] for h in range(CROP)]
            for h, v in enumerate(conv(y, taps)):
                at = spot(slot, h, w)
                rows[at, :] = v * (mask[slot, h] * col_in) + skip * rows[at, :]

    rows_to_lanes(rows, lambda off, v: put_tile(mixed, q, off, v))


def mix_bwd(q, x_all, rows, grow, kern, mask, inner, mid, out, gkern):
    lanes_to_rows(lambda off: tile_of(x_all, q, off), rows)
    skip = jnp.broadcast_to(kern[q, pl.ds(2 * CROP, 1), :], (8, LANES))
    zero = jnp.zeros((8, LANES), F32)

    def per_slot(slot, sums):
        gk_height, gk_width, gskip = sums
        along_width(q, slot, rows, kern, mask, inner)

        def down(w, acc):
            taps = tap_rows(kern, q, 0)
            col_in = mask[slot, CROP + w]
            u = [grow[q, spot(slot, h, w), :] * (mask[slot, h] * col_in) for h in range(CROP)]
            for h, v in enumerate(conv_back(u, taps)):
                mid[h, w] = v * mask[slot, h]
            a = [inner[h, w] for h in range(CROP)]
            return tuple(
                sum((u[h] * a[h - l] for h in range(l, CROP)), acc[l]) for l in range(CROP)
            )

        gk_height = lax.fori_loop(0, CROP, down, gk_height)

        def across(h, acc):
            gk_width, gskip = acc
            taps = tap_rows(kern, q, CROP)
            u = [mid[h, w] for w in range(CROP)]
            x = [rows[spot(slot, h, w), :] for w in range(CROP)]
            y = [x[w] * mask[slot, CROP + w] for w in range(CROP)]
            gk_width = tuple(
                sum((u[w] * y[w - l] for w in range(l, CROP)), gk_width[l]) for l in range(CROP)
            )
            for w, v in enumerate(conv_back(u, taps)):
                at = spot(slot, h, w)
                g = grow[q, at, :]
                gskip = gskip + g * x[w]
                grow[q, at, :] = v * mask[slot, CROP + w] + skip * g
            return gk_width, gskip

        gk_width, gskip = lax.fori_loop(0, CROP, across, (gk_width, gskip))
        return gk_height, gk_width, gskip

    gk_height, gk_width, gskip = lax.fori_loop(
        0, 4, per_slot, ((zero,) * CROP, (zero,) * CROP, zero)
    )
    gkern[q] = jnp.zeros((32, LANES), F32)
    for row, v in enumerate((*gk_height, *gk_width, gskip)):
        gkern[q, pl.ds(row, 1), :] = jnp.sum(v, axis=0, keepdims=True)
    rows_to_lanes(grow.at[q], lambda off, v: put_tile(out, q, off, v))


def lag_waves(step, a_log, a_imag):
    rate = -step * jnp.exp(a_log)
    phase = step * a_imag
    size = jnp.exp(rate)
    re1, im1 = size * jnp.cos(phase), size * jnp.sin(phase)
    re, im = jnp.ones_like(re1), jnp.zeros_like(im1)
    out = []
    for _ in range(CROP):
        out.append((re, im))
        re, im = re * re1 - im * im1, re * im1 + im * re1
    return rate, phase, out


def column_set(acc, k, col):
    lane = lax.broadcasted_iota(jnp.int32, acc.shape, 1)
    return jnp.where(lane == k, col, acc)


def lag_kernels(steps, a_log, a_imag, coefs, out):
    local = a_log.shape[1]
    for j in range(2):
        _, _, waves = lag_waves(steps[j], a_log[...], a_imag[...])
        for l, (re, im) in enumerate(waves):
            row = jnp.sum(coefs[j][0] * re - coefs[j][1] * im, axis=0, keepdims=True)
            out[CROP * j + l : CROP * j + l + 1, 0:local] = row


def lag_grads(rows, steps, a_log, a_imag, coefs, g_alog, g_aimag, g_coefs):
    ga, gi, gdt = 0.0, 0.0, []
    for j in range(2):
        rate, phase, waves = lag_waves(steps[j], a_log[...], a_imag[...])
        cre, cim = coefs[j][0], coefs[j][1]
        g_re = g_im = p = r = 0.0
        for l, (re, im) in enumerate(waves):
            g = rows[CROP * j + l : CROP * j + l + 1, 0 : a_log.shape[1]]
            g_re = g_re + g * re
            g_im = g_im - g * im
            if l:
                p = p + (l * g) * (cre * re - cim * im)
                r = r - (l * g) * (cre * im + cim * re)
        g_coefs[j][0] = g_re
        g_coefs[j][1] = g_im
        ga = ga + p * rate
        gi = gi + r * steps[j]
        gdt.append(jnp.sum(p * rate + r * phase, axis=0, keepdims=True))
    g_alog[...] = ga
    g_aimag[...] = gi
    return gdt


def norm(m):
    centered = m - jnp.mean(m, axis=0, keepdims=True)
    scale = lax.rsqrt(jnp.mean(centered * centered, axis=0, keepdims=True) + EPS)
    return centered * scale, scale


def fold(v):
    return sum(
        (v[:, i * LANES : (i + 1) * LANES] for i in range(1, v.shape[1] // LANES)), v[:, :LANES]
    )


def block_kernel(
    parts,
    groups,
    x,
    go,
    size_ref,
    offset_ref,
    a_log,
    a_imag,
    c_height,
    c_width,
    log_dt,
    skip_gain,
    ln_gain,
    ln_bias,
    w_in,
    b_in,
    w_out,
    b_out,
    layer_scale,
    res_own,
    g_own,
    dw_own,
    g_alog,
    g_aimag,
    g_height,
    g_width,
    row_own,
    go_all,
    hid_far,
    slope_far,
    res,
    dw_peer,
    x_all,
    mixed,
    res_near,
    rows,
    grow,
    inner,
    mid,
    mask,
    small_mine,
    small_all,
    kern,
    gkern,
    bin_col,
    chan,
    square,
    turned,
    win,
    win_t,
    wout,
    wout_t,
    hid,
    slope,
    gp,
    go_near,
    dw,
    dw_sum,
    dw_low,
    dw_tensor,
    dw_done,
    bin_acc,
    vec,
    pack_mine,
    pack_peer,
    pack_sum,
    pack_tensor,
    send,
    recv,
    own,
    hid_sem,
    slope_sem,
    go_sem,
    res_sem,
    gx_send,
    gx_recv,
    gx_own,
):
    local, pix = x_all.shape[1], x_all.shape[2]
    width = local * parts
    ff = win_t.shape[0]
    shard = ff // parts
    slab = shard // groups
    chunks = pix // STEP
    me = lax.axis_index("tensor")
    dp = lax.axis_index("dp")
    mine = lax.rem(dp, groups)
    first = dp - mine
    across = [{"tensor": lax.rem(me + s, parts)} for s in range(1, parts)]
    beside = [{"dp": first + lax.rem(mine + s, groups)} for s in range(1, groups)]

    barrier = pltpu.get_barrier_semaphore()
    for peer in across + beside:
        pl.semaphore_signal(barrier, inc=1, device_id=peer, device_id_type=MESH)
    pl.semaphore_wait(barrier, len(across) + len(beside))

    count = [0, 0]

    def remote(src, dst, peer, sems=None):
        if sems is None:
            sems = (send.at[count[0]], recv.at[count[0]])
            count[0] += 1
        copy = pltpu.make_async_remote_copy(
            src_ref=src,
            dst_ref=dst,
            send_sem=sems[0],
            recv_sem=sems[1],
            device_id=peer,
            device_id_type=MESH,
        )
        copy.start()
        return copy

    def near(src, dst, sem=None):
        if sem is None:
            sem = own.at[count[1]]
            count[1] += 1
        copy = pltpu.make_async_copy(src, dst, sem)
        copy.start()
        return copy

    sent = []

    def arrived(copies):
        for copy in copies:
            copy.wait_recv()
        sent.extend(copies)

    def pixels(ref, peer):
        return ref.at[:, pl.ds(pl.multiple_of(peer * pix, LANES), pix)]

    def to_owner(ref, out):
        return [remote(pixels(ref, p["tensor"]), out.at[me], p) for p in across]

    my_slab = pl.ds(pl.multiple_of(mine * slab, slab), slab)
    my_cols = pl.ds(pl.multiple_of(me * shard, LANES), shard)
    w_copies = [remote(w_in.at[my_slab, :], win.at[my_slab, my_cols], p) for p in across]
    w_copies += [remote(w_out.at[my_slab, :], wout.at[me, my_slab, :], p) for p in across]
    w_near = [
        near(w_in.at[my_slab, :], win.at[my_slab, my_cols]),
        near(w_out.at[my_slab, :], wout.at[me, my_slab, :]),
    ]
    steps = [jnp.exp(log_dt[j : j + 1, :]) for j in range(2)]
    coefs = [c_height, c_width]
    small_mine[...] = jnp.zeros_like(small_mine)
    lag_kernels(steps, a_log, a_imag, coefs, small_mine)
    small_mine[2 * CROP : 2 * CROP + 1, 0:local] = skip_gain[...].reshape(1, local)
    biases = b_in[...].reshape(1, shard)
    for i in range(shard // LANES):
        small_mine[32 + i : 33 + i, :] = biases[:, i * LANES : (i + 1) * LANES]
    small_all[me] = small_mine[...]
    small_copies = [remote(small_mine, small_all.at[me], p) for p in across]
    x_copies = to_owner(x, x_all)
    x_near = near(pixels(x, me), x_all.at[me])

    for copy in w_near:
        copy.wait()
    arrived(w_copies)
    w_copies = [remote(win.at[my_slab, :], win.at[my_slab, :], p) for p in beside]
    w_copies += [remote(wout.at[:, my_slab, :], wout.at[:, my_slab, :], p) for p in beside]

    square[...] = jnp.zeros_like(square)
    for row, ref in enumerate((ln_gain, ln_bias, b_out, layer_scale)):
        square[row : row + 1, :] = ref[...].reshape(1, width)
    for i in range(width // LANES):
        chan[i * LANES : (i + 1) * LANES, :] = jnp.transpose(square[:, i * LANES : (i + 1) * LANES])
    canvases = size_ref.shape[1]
    square[0:8, 0:canvases] = offset_ref[...].astype(F32)
    square[8:16, 0:canvases] = size_ref[...].astype(F32)
    turned[...] = jnp.transpose(square[:, 0:LANES])
    at = pl.ds(pl.multiple_of(me * 8, 8), 8)
    for slot in range(4):
        for j in range(2):
            k = 2 * slot + j
            low = jnp.broadcast_to(turned[at, k : k + 1], (8, LANES))
            high = low + jnp.broadcast_to(turned[at, 8 + k : 9 + k], (8, LANES))
            for s in range(CROP):
                mask[slot, CROP * j + s] = jnp.where((low <= s) & (s < high), 1.0, 0.0)
    arrived(small_copies)
    for q in range(local // GROUP):
        kern[q] = jnp.concatenate(
            [small_all[t, 0:32, q * GROUP : (q + 1) * GROUP] for t in range(parts)], axis=1
        )
    for t in range(parts):
        for i in range(shard // LANES):
            block = jnp.broadcast_to(small_all[t, 32 + i : 33 + i, :], (LANES, LANES))
            bin_col[t * shard + i * LANES : t * shard + (i + 1) * LANES, :] = jnp.transpose(block)
    arrived(w_copies)
    for t in range(parts):
        cols = slice(t * shard, (t + 1) * shard)
        win_t[cols, :] = jnp.transpose(win[:, cols].astype(F32)).astype(BF16)
        wout_t[:, cols] = jnp.transpose(wout[t].astype(F32)).astype(BF16)

    arrived(x_copies)
    x_near.wait()
    go_copies = to_owner(go, go_all)

    @pl.loop(0, local // GROUP)
    def _(q):
        mix_fwd(q, x_all, rows, kern, mask, inner, mixed)

    def hid_copy(t, j, back):
        sl = pl.ds(t * shard, shard)
        lanes = pl.ds(pl.multiple_of(j * STEP, LANES), STEP)
        pair = [(hid.at[sl, :], hid_far.at[sl, lanes]), (slope.at[sl, :], slope_far.at[sl, lanes])]
        pair = [p[::-1] if back else p for p in pair]
        return [
            pltpu.make_async_copy(*p, sem.at[t]) for p, sem in zip(pair, (hid_sem, slope_sem))
        ]

    others = [p["tensor"] for p in across]

    def res_chunk(j):
        lanes = pl.ds(pl.multiple_of(j * STEP, LANES), STEP)
        pairs = [(t, res) for t in others] + [(me, res_own)]
        return [
            pltpu.make_async_copy(res_near.at[t], ref.at[t, :, lanes], res_sem.at[i])
            for i, (t, ref) in enumerate(pairs)
        ]

    def low_of(off):
        normed, scale = norm(mixed[:, :, pl.ds(off, STEP)].reshape(width, STEP).astype(F32))
        return normed, scale, (normed * chan[:, 0:1] + chan[:, 1:2]).astype(BF16)

    @pl.loop(0, chunks)
    def _(j):
        off = pl.multiple_of(j * STEP, LANES)
        _, _, low = low_of(off)
        for t in range(parts):
            sl = pl.ds(t * shard, shard)
            pre = nn(win_t[sl, :], low) + bin_col[sl, 0:1]
            square_pre = pre * pre
            th = jnp.tanh(pre * (GELU_C + (GELU_C * GELU_A) * square_pre))
            half = 0.5 * th + 0.5
            inner_slope = GELU_C + (3 * GELU_C * GELU_A) * square_pre

            @pl.when(j > 0)
            def _():
                for copy in hid_copy(t, j, False):
                    copy.wait()

            hid[sl, :] = (pre * half).astype(BF16)
            slope[sl, :] = (half + pre * (0.5 - 0.5 * th * th) * inner_slope).astype(BF16)
            for copy in hid_copy(t, j, False):
                copy.start()
        branch = nn(wout_t[...], hid[...]) + chan[:, 2:3]
        source = x_all[:, :, pl.ds(off, STEP)].reshape(width, STEP).astype(F32)
        out = (source + chan[:, 3:4] * branch).astype(BF16)

        @pl.when(j > 0)
        def _():
            for copy in res_chunk(j):
                copy.wait()

        res_near[...] = out.reshape(parts, local, STEP)
        for copy in res_chunk(j):
            copy.start()

    for t in range(parts):
        for copy in hid_copy(t, 0, False):
            copy.wait()
        for copy in hid_copy(t, 0, True):
            copy.start()

    for copy in res_chunk(0):
        copy.wait()

    arrived(go_copies)
    res_copies = [remote(res.at[p["tensor"]], res_own.at[me], p) for p in across]

    for ref in (dw, bin_acc, vec):
        ref[...] = jnp.zeros_like(ref)

    def go_chunk(j):
        off = pl.multiple_of(j * STEP, LANES)
        mine_at = pl.ds(pl.multiple_of(me * pix + off, LANES), STEP)
        sources = [(t, go_all.at[t, :, pl.ds(off, STEP)]) for t in others] + [(me, go.at[:, mine_at])]
        return [
            pltpu.make_async_copy(src, go_near.at[t], go_sem.at[i])
            for i, (t, src) in enumerate(sources)
        ]

    for copy in go_chunk(0):
        copy.start()

    @pl.loop(0, chunks)
    def _(j):
        off = pl.multiple_of(j * STEP, LANES)
        for copy in go_chunk(j):
            copy.wait()
        grad = go_near[...].reshape(width, STEP).astype(F32)
        gb = (grad * chan[:, 3:4]).astype(BF16)
        vec[0] += fold(gb.astype(F32))
        vec[3] += fold(grad)

        @pl.when(j + 1 < chunks)
        def _():
            for copy in go_chunk(j + 1):
                copy.start()

        normed, scale, low = low_of(off)
        for t in range(parts):
            sl = pl.ds(t * shard, shard)
            for copy in hid_copy(t, j, True):
                copy.wait()
            tile = (nn(wout[t], gb) * slope[sl, :].astype(F32)).astype(BF16)
            gp[sl, :] = tile
            bin_acc[sl, :] += fold(tile.astype(F32))
            dw[0, t] += nt(hid[sl, :], gb)
            dw[1, t] += nt(tile, low)

            @pl.when(j + 1 < chunks)
            def _():
                for copy in hid_copy(t, j + 1, True):
                    copy.start()

        gn = nn(win[...], gp[...])
        vec[1] += fold(gn * normed)
        vec[2] += fold(gn)
        g1 = gn * chan[:, 0:1]
        m1 = jnp.mean(g1, axis=0, keepdims=True)
        m2 = jnp.mean(g1 * normed, axis=0, keepdims=True)
        gm = (scale * (g1 - m1 - normed * m2)).reshape(parts, local, STEP)
        for q in range(local // GROUP):
            block = gm[:, q * GROUP : (q + 1) * GROUP, :].reshape(LANES, STEP)
            grow[q, pl.ds(off, STEP), :] = jnp.transpose(block)

    def slab_of(peer):
        return pl.ds(pl.multiple_of((peer["dp"] - first) * slab, slab), slab)

    dw_near = near(dw.at[:, :, my_slab, :], dw_peer.at[:, :, my_slab, :])
    dw_copies = [
        remote(dw.at[:, :, slab_of(p), :], dw_peer.at[:, :, my_slab, :], p) for p in beside
    ]

    def gx_tile(q):
        return pl.ds(pl.multiple_of(q * GROUP, GROUP), GROUP)

    def gx_copies(q):
        at = gx_tile(q)
        return [
            pltpu.make_async_remote_copy(
                src_ref=mixed.at[p["tensor"], at, :],
                dst_ref=g_own.at[me, at, :],
                send_sem=gx_send.at[q, s],
                recv_sem=gx_recv.at[q, s],
                device_id=p,
                device_id_type=MESH,
            )
            for s, p in enumerate(across)
        ] + [pltpu.make_async_copy(mixed.at[me, at, :], g_own.at[me, at, :], gx_own.at[q])]

    @pl.loop(0, local // GROUP)
    def _(q):
        mix_bwd(q, x_all, rows, grow, kern, mask, inner, mid, mixed, gkern)

        @pl.when(q + 1 < local // GROUP)
        def _():
            for copy in gx_copies(q):
                copy.start()

    for t in range(parts):
        lanes = slice(t * GROUP, (t + 1) * GROUP)
        pack_mine[t] = jnp.zeros(pack_mine.shape[1:], F32)
        pack_mine[t, 0:32, 0:local] = jnp.concatenate(
            [gkern[q, 0:32, lanes] for q in range(local // GROUP)], axis=1
        )
    acc = jnp.zeros((width, LANES), F32)
    sums = [jnp.sum(vec[k], axis=1, keepdims=True) for k in range(4)]
    for k in range(3):
        acc = column_set(acc, k, sums[k])
    square[0:1, :] = sum(
        jnp.sum(wout[t].astype(F32) * dw[0, t], axis=0, keepdims=True) for t in range(parts)
    )
    products = jnp.concatenate(
        [
            jnp.transpose(square[:, i * LANES : (i + 1) * LANES])[:, 0:1]
            for i in range(width // LANES)
        ]
    )
    acc = column_set(acc, 3, products / chan[:, 3:4] + chan[:, 2:3] * sums[3])
    hidden_sums = jnp.sum(bin_acc[...], axis=1, keepdims=True)
    for k in range(shard // local):
        starts = [t * shard + k * local for t in range(parts)]
        acc = column_set(acc, 4 + k, jnp.concatenate([hidden_sums[i : i + local] for i in starts]))
    for t in range(parts):
        square[0:local, 0:LANES] = acc[t * local : (t + 1) * local]
        pack_mine[t, 32:40, :] = jnp.transpose(square[:, 0:LANES])[0:8]
    pack_peer[mine] = pack_mine[...]
    pack_copies = [remote(pack_mine, pack_peer.at[mine], p) for p in beside]

    dw_near.wait()
    for copy in dw_copies:
        copy.wait()
    near(dw_peer, dw).wait()
    slabs = [dw[:, :, i * slab : (i + 1) * slab, :] for i in range(groups)]
    dw_sum[...] = sum(slabs[1:], slabs[0])
    dw_low[...] = dw_sum[...].astype(BF16)
    dw_copies = [remote(dw_low.at[:, t], dw_tensor.at[me], p) for t, p in zip(others, across)]
    arrived(pack_copies)
    pack_sum[...] = sum((pack_peer[i] for i in range(1, groups)), pack_peer[0])
    pack_tensor[me] = pack_sum[me]
    pack_copies = [remote(pack_sum.at[t], pack_tensor.at[me], p) for t, p in zip(others, across)]
    for copy in gx_copies(local // GROUP - 1):
        copy.start()

    arrived(dw_copies)
    dw_done[...] = sum((dw_tensor[t].astype(F32) for t in others), dw_sum[:, me])
    dw_near = near(dw_done, dw_own.at[:, my_slab, :])
    dw_copies = [remote(dw_done, dw_own.at[:, my_slab, :], p) for p in beside]
    arrived(pack_copies)
    total = sum((pack_tensor[i] for i in range(1, parts)), pack_tensor[0])
    gdt = lag_grads(total, steps, a_log, a_imag, coefs, g_alog, g_aimag, [g_height, g_width])
    row_own[...] = total
    for j in range(2):
        row_own[29 + j : 30 + j, 0:local] = gdt[j]

    arrived(dw_copies)
    dw_near.wait()
    arrived(res_copies)

    @pl.loop(0, local // GROUP)
    def _(q):
        for copy in gx_copies(q):
            copy.wait()

    for copy in sent:
        copy.wait_send()


def block(parts, groups, args):
    x, size = args[0], args[2]
    local, pixels = x.shape
    pix = pixels // parts
    width = local * parts
    w_in = args[12]
    shard = w_in.shape[1]
    ff = shard * parts
    slab = shard // groups
    tiles = local // GROUP
    states = args[4].shape[0]
    shape = jax.ShapeDtypeStruct
    vmem = pl.BlockSpec(memory_space=pltpu.VMEM)
    hbm = pl.BlockSpec(memory_space=pl.ANY)
    in_specs = [hbm, hbm] + [vmem] * 10 + [hbm, vmem, hbm, vmem, vmem]
    outs = [
        (shape((parts, local, pix), BF16), hbm),
        (shape((parts, local, pix), BF16), hbm),
        (shape((2, shard, width), F32), hbm),
        (shape((states, local), F32), vmem),
        (shape((states, local), F32), vmem),
        (shape((2, states, local), F32), vmem),
        (shape((2, states, local), F32), vmem),
        (shape((40, LANES), F32), vmem),
        (shape((parts, local, pix), BF16), hbm),
        (shape((ff, pix), BF16), hbm),
        (shape((ff, pix), BF16), hbm),
        (shape((parts, local, pix), BF16), hbm),
        (shape((2, parts, shard, width), F32), hbm),
    ]
    remotes = 8 * (parts - 1) + 5 * (groups - 1)
    dma = pltpu.SemaphoreType.DMA
    scratch = [
        pltpu.VMEM((parts, local, pix), BF16),
        pltpu.VMEM((parts, local, pix), BF16),
        pltpu.VMEM((parts, local, STEP), BF16),
        pltpu.VMEM((pix, LANES), F32),
        pltpu.VMEM((tiles, pix, LANES), F32),
        pltpu.VMEM((CROP, CROP, 8, LANES), F32),
        pltpu.VMEM((CROP, CROP, 8, LANES), F32),
        pltpu.VMEM((4, 2 * CROP, 8, LANES), F32),
        pltpu.VMEM((40, LANES), F32),
        pltpu.VMEM((parts, 40, LANES), F32),
        pltpu.VMEM((tiles, 32, LANES), F32),
        pltpu.VMEM((tiles, 32, LANES), F32),
        pltpu.VMEM((ff, LANES), F32),
        pltpu.VMEM((width, LANES), F32),
        pltpu.VMEM((LANES, width), F32),
        pltpu.VMEM((LANES, LANES), F32),
        pltpu.VMEM((width, ff), BF16),
        pltpu.VMEM((ff, width), BF16),
        pltpu.VMEM((parts, shard, width), BF16),
        pltpu.VMEM((width, ff), BF16),
        pltpu.VMEM((ff, STEP), BF16),
        pltpu.VMEM((ff, STEP), BF16),
        pltpu.VMEM((ff, STEP), BF16),
        pltpu.VMEM((parts, local, STEP), BF16),
        pltpu.VMEM((2, parts, shard, width), F32),
        pltpu.VMEM((2, parts, slab, width), F32),
        pltpu.VMEM((2, parts, slab, width), BF16),
        pltpu.VMEM((parts, 2, slab, width), BF16),
        pltpu.VMEM((2, slab, width), F32),
        pltpu.VMEM((ff, LANES), F32),
        pltpu.VMEM((4, width, LANES), F32),
        pltpu.VMEM((parts, 40, LANES), F32),
        pltpu.VMEM((groups, parts, 40, LANES), F32),
        pltpu.VMEM((parts, 40, LANES), F32),
        pltpu.VMEM((parts, 40, LANES), F32),
        dma((remotes,)),
        dma((remotes,)),
        dma((8,)),
        dma((parts,)),
        dma((parts,)),
        dma((parts,)),
        dma((parts,)),
        dma((tiles, parts - 1)),
        dma((tiles, parts - 1)),
        dma((tiles,)),
    ]
    return pl.pallas_call(
        functools.partial(block_kernel, parts, groups),
        out_shape=[o[0] for o in outs],
        in_specs=in_specs,
        out_specs=[o[1] for o in outs],
        scratch_shapes=scratch,
        compiler_params=pltpu.CompilerParams(
            collective_id=0, has_side_effects=True, vmem_limit_bytes=VMEM
        ),
        name="block",
    )(*args)


def finish_kernel(
    res_ref,
    g_ref,
    go_ref,
    dw,
    g_alog,
    g_aimag,
    g_height,
    g_width,
    rows,
    result_ref,
    grad_ref,
    alog_out,
    aimag_out,
    height_out,
    width_out,
    dt_out,
    skip_out,
    gain_out,
    bias_out,
    win_out,
    bin_out,
    wout_out,
    bout_out,
    scale_out,
):
    result_ref[...] = res_ref[0]
    grad_ref[...] = go_ref[...].astype(F32) + g_ref[0].astype(F32)

    @pl.when((pl.program_id(0) == 0) & (pl.program_id(1) == 0))
    def _():
        alog_out[...] = g_alog[...]
        aimag_out[...] = g_aimag[...]
        height_out[...] = g_height[...]
        width_out[...] = g_width[...]
        local = skip_out.shape[0]
        dt_out[...] = rows[29:31, 0:local]
        singles = ((skip_out, 28), (gain_out, 33), (bias_out, 34), (bout_out, 32), (scale_out, 35))
        for out, k in singles:
            out[...] = rows[k : k + 1, 0:local].reshape(local)
        count = bin_out.shape[0] // local
        bin_out[...] = jnp.concatenate(
            [rows[36 + k : 37 + k, 0:local] for k in range(count)], axis=1
        ).reshape(bin_out.shape)
        win_out[...] = jnp.transpose(dw[1])
        wout_out[...] = dw[0]


def finish(res_own, g_own, grad_out, sums):
    parts, local, pix = g_own.shape
    dw, g_alog, _, g_height, _, _ = sums
    part = pl.BlockSpec((1, GROUP, pix), lambda s, q: (s, q, 0))
    tile = pl.BlockSpec((GROUP, pix), lambda s, q: (q, s))

    def whole(a):
        return pl.BlockSpec(a.shape, lambda s, q: (0,) * len(a.shape))

    shape = jax.ShapeDtypeStruct
    line = shape((local,), F32)
    small = (
        g_alog,
        g_alog,
        g_height,
        g_height,
        shape((2, local), F32),
        line,
        line,
        line,
        shape((dw.shape[2], dw.shape[1]), F32),
        shape((dw.shape[1],), F32),
        shape(dw.shape[1:], F32),
        line,
        line,
    )
    small = tuple(shape(a.shape, F32) for a in small)
    return pl.pallas_call(
        finish_kernel,
        grid=(parts, local // GROUP),
        out_shape=(shape(grad_out.shape, BF16), shape(grad_out.shape, F32)) + small,
        in_specs=[part, part, tile] + [whole(a) for a in sums],
        out_specs=(tile, tile) + tuple(whole(a) for a in small),
        compiler_params=pltpu.CompilerParams(vmem_limit_bytes=VMEM),
        name="finish",
    )(res_own, g_own, grad_out, *sums)


def per_device(
    parts,
    dp_size,
    inputs,
    crop_size,
    crop_offset,
    a_log,
    a_imag,
    c_height,
    c_width,
    log_dt,
    skip_gain,
    ln_gain,
    ln_bias,
    w_in,
    b_in,
    w_out,
    b_out,
    layer_scale,
    grad_out,
):
    canvases = crop_size.shape[0]
    groups = min(dp_size, 8)
    args = (
        inputs,
        grad_out,
        jnp.transpose(crop_size.reshape(canvases, 8)),
        jnp.transpose(crop_offset.reshape(canvases, 8)),
        jnp.transpose(a_log),
        jnp.transpose(a_imag),
        jnp.transpose(c_height, (0, 2, 1)),
        jnp.transpose(c_width, (0, 2, 1)),
        log_dt,
        skip_gain,
        ln_gain,
        ln_bias,
        w_in,
        b_in,
        w_out,
        b_out,
        layer_scale,
    )
    out = block(parts, groups, args)
    sums = tuple(out[2:8])
    if dp_size > groups:
        teams = [[r + groups * g for g in range(dp_size // groups)] for r in range(groups)]
        sums = lax.psum(sums, "dp", axis_index_groups=teams)
    done = finish(out[0], out[1], grad_out, sums)
    return (
        done[0],
        done[1],
        jnp.transpose(done[2]),
        jnp.transpose(done[3]),
        jnp.transpose(done[4], (0, 2, 1)),
        jnp.transpose(done[5], (0, 2, 1)),
        *done[6:],
    )


def solution(mesh):
    in_specs = (
        P("tensor", "dp"),
        P("dp", None, None),
        P("dp", None, None),
        P("tensor", None),
        P("tensor", None),
        P(None, "tensor", None),
        P(None, "tensor", None),
        P(None, "tensor"),
        P("tensor"),
        P(),
        P(),
        P(None, "tensor"),
        P("tensor"),
        P("tensor", None),
        P(),
        P(),
        P("tensor", "dp"),
    )
    out_specs = (
        P("tensor", "dp"),
        P("tensor", "dp"),
        P("tensor", None),
        P("tensor", None),
        P(None, "tensor", None),
        P(None, "tensor", None),
        P(None, "tensor"),
        P("tensor"),
        P("tensor"),
        P("tensor"),
        P(None, "tensor"),
        P("tensor"),
        P("tensor", None),
        P("tensor"),
        P("tensor"),
    )
    return jax.shard_map(
        functools.partial(per_device, mesh.shape["tensor"], mesh.shape["dp"]),
        mesh=mesh,
        in_specs=in_specs,
        out_specs=out_specs,
        check_vma=False,
    )
```

```python
import functools

import jax
import jax.numpy as jnp
from jax import lax
from jax.experimental import pallas as pl
from jax.experimental.pallas import tpu as pltpu
from jax.sharding import PartitionSpec as P

F32, BF16 = jnp.float32, jnp.bfloat16
CROP = 14
SIDE = 2 * CROP
NPIX = SIDE * SIDE
LANES = 128
GROUP = 32
STEP = 896
EPS = 1e-06
GELU_C = 0.7978845608028654
GELU_A = 0.044715
VMEM = 63 << 20
MESH = pl.DeviceIdType.MESH


def nn(a, b):
    return lax.dot_general(a, b, (((1,), (0,)), ((), ())), preferred_element_type=F32)


def nt(a, b):
    return lax.dot_general(a, b, (((1,), (1,)), ((), ())), preferred_element_type=F32)


def conv(y, taps):
    return [sum((taps[l] * y[i - l] for l in range(1, i + 1)), taps[0] * y[i]) for i in range(CROP)]


def conv_back(y, taps):
    return [
        sum((taps[l] * y[i + l] for l in range(1, CROP - i)), taps[0] * y[i]) for i in range(CROP)
    ]


def spot(slot, h, w):
    first = (slot // 2) * (CROP * SIDE) + (slot % 2) * CROP
    return pl.ds(first + h * SIDE + w, 8, stride=NPIX)


def lanes_to_rows(load, rows):
    @pl.loop(0, rows.shape[0] // STEP)
    def _(j):
        off = pl.multiple_of(j * STEP, LANES)
        rows[pl.ds(off, STEP), :] = jnp.transpose(load(off).astype(F32))


def rows_to_lanes(rows, store):
    @pl.loop(0, rows.shape[0] // STEP)
    def _(j):
        off = pl.multiple_of(j * STEP, LANES)
        store(off, jnp.transpose(rows[pl.ds(off, STEP), :]).astype(BF16))


def tap_rows(kern, q, base):
    return [jnp.broadcast_to(kern[q, pl.ds(base + l, 1), :], (8, LANES)) for l in range(CROP)]


def tile_of(ref, q, off):
    return ref[:, pl.ds(pl.multiple_of(q * GROUP, GROUP), GROUP), pl.ds(off, STEP)].reshape(
        LANES, STEP
    )


def put_tile(ref, q, off, v):
    ref[:, pl.ds(pl.multiple_of(q * GROUP, GROUP), GROUP), pl.ds(off, STEP)] = v.reshape(
        ref.shape[0], GROUP, STEP
    )


def along_width(q, slot, rows, kern, mask, inner):
    @pl.loop(0, CROP)
    def _(h):
        taps = tap_rows(kern, q, CROP)
        row_in = mask[slot, h]
        y = [rows[spot(slot, h, w), :] * mask[slot, CROP + w] for w in range(CROP)]
        for w, v in enumerate(conv(y, taps)):
            inner[h, w] = v * row_in


def mix_fwd(q, x_all, rows, kern, mask, inner, mixed):
    lanes_to_rows(lambda off: tile_of(x_all, q, off), rows)
    skip = jnp.broadcast_to(kern[q, pl.ds(2 * CROP, 1), :], (8, LANES))

    @pl.loop(0, 4)
    def _(slot):
        along_width(q, slot, rows, kern, mask, inner)

        @pl.loop(0, CROP)
        def _(w):
            taps = tap_rows(kern, q, 0)
            col_in = mask[slot, CROP + w]
            y = [inner[h, w] for h in range(CROP)]
            for h, v in enumerate(conv(y, taps)):
                at = spot(slot, h, w)
                rows[at, :] = v * (mask[slot, h] * col_in) + skip * rows[at, :]

    rows_to_lanes(rows, lambda off, v: put_tile(mixed, q, off, v))


def mix_bwd(q, x_all, rows, grow, kern, mask, inner, mid, out, gkern):
    lanes_to_rows(lambda off: tile_of(x_all, q, off), rows)
    skip = jnp.broadcast_to(kern[q, pl.ds(2 * CROP, 1), :], (8, LANES))
    zero = jnp.zeros((8, LANES), F32)

    def per_slot(slot, sums):
        gk_height, gk_width, gskip = sums
        along_width(q, slot, rows, kern, mask, inner)

        def down(w, acc):
            taps = tap_rows(kern, q, 0)
            col_in = mask[slot, CROP + w]
            u = [grow[q, spot(slot, h, w), :] * (mask[slot, h] * col_in) for h in range(CROP)]
            for h, v in enumerate(conv_back(u, taps)):
                mid[h, w] = v * mask[slot, h]
            a = [inner[h, w] for h in range(CROP)]
            return tuple(
                sum((u[h] * a[h - l] for h in range(l, CROP)), acc[l]) for l in range(CROP)
            )

        gk_height = lax.fori_loop(0, CROP, down, gk_height)

        def across(h, acc):
            gk_width, gskip = acc
            taps = tap_rows(kern, q, CROP)
            u = [mid[h, w] for w in range(CROP)]
            x = [rows[spot(slot, h, w), :] for w in range(CROP)]
            y = [x[w] * mask[slot, CROP + w] for w in range(CROP)]
            gk_width = tuple(
                sum((u[w] * y[w - l] for w in range(l, CROP)), gk_width[l]) for l in range(CROP)
            )
            for w, v in enumerate(conv_back(u, taps)):
                at = spot(slot, h, w)
                g = grow[q, at, :]
                gskip = gskip + g * x[w]
                grow[q, at, :] = v * mask[slot, CROP + w] + skip * g
            return gk_width, gskip

        gk_width, gskip = lax.fori_loop(0, CROP, across, (gk_width, gskip))
        return gk_height, gk_width, gskip

    gk_height, gk_width, gskip = lax.fori_loop(
        0, 4, per_slot, ((zero,) * CROP, (zero,) * CROP, zero)
    )
    gkern[q] = jnp.zeros((32, LANES), F32)
    for row, v in enumerate((*gk_height, *gk_width, gskip)):
        gkern[q, pl.ds(row, 1), :] = jnp.sum(v, axis=0, keepdims=True)

    @pl.loop(0, rows.shape[0] // STEP)
    def _(j):
        off = pl.multiple_of(j * STEP, LANES)
        turned = jnp.transpose(grow[q, pl.ds(off, STEP), :])
        put_tile(out, q, off, (tile_of(out, q, off).astype(F32) + turned).astype(BF16))


def lag_waves(step, a_log, a_imag):
    rate = -step * jnp.exp(a_log)
    phase = step * a_imag
    size = jnp.exp(rate)
    re1, im1 = size * jnp.cos(phase), size * jnp.sin(phase)
    re, im = jnp.ones_like(re1), jnp.zeros_like(im1)
    out = []
    for _ in range(CROP):
        out.append((re, im))
        re, im = re * re1 - im * im1, re * im1 + im * re1
    return rate, phase, out


def column_set(acc, k, col):
    lane = lax.broadcasted_iota(jnp.int32, acc.shape, 1)
    return jnp.where(lane == k, col, acc)


def lag_kernels(steps, a_log, a_imag, coefs, out):
    local = a_log.shape[1]
    for j in range(2):
        _, _, waves = lag_waves(steps[j], a_log[...], a_imag[...])
        for l, (re, im) in enumerate(waves):
            row = jnp.sum(coefs[j][0] * re - coefs[j][1] * im, axis=0, keepdims=True)
            out[CROP * j + l : CROP * j + l + 1, 0:local] = row


def lag_grads(rows, steps, a_log, a_imag, coefs, g_alog, g_aimag, g_coefs):
    ga, gi, gdt = 0.0, 0.0, []
    for j in range(2):
        rate, phase, waves = lag_waves(steps[j], a_log[...], a_imag[...])
        cre, cim = coefs[j][0], coefs[j][1]
        g_re = g_im = p = r = 0.0
        for l, (re, im) in enumerate(waves):
            g = rows[CROP * j + l : CROP * j + l + 1, 0 : a_log.shape[1]]
            g_re = g_re + g * re
            g_im = g_im - g * im
            if l:
                p = p + (l * g) * (cre * re - cim * im)
                r = r - (l * g) * (cre * im + cim * re)
        g_coefs[j][0] = g_re
        g_coefs[j][1] = g_im
        ga = ga + p * rate
        gi = gi + r * steps[j]
        gdt.append(jnp.sum(p * rate + r * phase, axis=0, keepdims=True))
    g_alog[...] = ga
    g_aimag[...] = gi
    return gdt


def norm(m):
    centered = m - jnp.mean(m, axis=0, keepdims=True)
    scale = lax.rsqrt(jnp.mean(centered * centered, axis=0, keepdims=True) + EPS)
    return centered * scale, scale


def fold(v):
    return sum(
        (v[:, i * LANES : (i + 1) * LANES] for i in range(1, v.shape[1] // LANES)), v[:, :LANES]
    )


def block_kernel(
    parts,
    groups,
    x,
    go,
    size_ref,
    offset_ref,
    a_log,
    a_imag,
    c_height,
    c_width,
    log_dt,
    skip_gain,
    ln_gain,
    ln_bias,
    w_in,
    b_in,
    w_out,
    b_out,
    layer_scale,
    res_own,
    g_own,
    dw_own,
    g_alog,
    g_aimag,
    g_height,
    g_width,
    row_own,
    go_all,
    hid_far,
    slope_far,
    res,
    dw_peer,
    x_all,
    mixed,
    res_near,
    rows,
    grow,
    inner,
    mid,
    mask,
    small_mine,
    small_all,
    kern,
    gkern,
    bin_col,
    chan,
    square,
    turned,
    win,
    win_t,
    wout,
    wout_t,
    hid,
    slope,
    gp,
    go_near,
    dw,
    dw_sum,
    dw_low,
    dw_tensor,
    dw_done,
    bin_acc,
    vec,
    pack_mine,
    pack_peer,
    pack_sum,
    pack_tensor,
    send,
    recv,
    own,
    hop_send,
    hop_recv,
    hid_sem,
    slope_sem,
    go_sem,
    res_sem,
    gx_send,
    gx_recv,
    gx_own,
):
    local, pix = x_all.shape[1], x_all.shape[2]
    width = local * parts
    ff = win_t.shape[0]
    shard = ff // parts
    slab = shard // groups
    chunks = pix // STEP
    me = lax.axis_index("tensor")
    dp = lax.axis_index("dp")
    mine = lax.rem(dp, groups)
    first = dp - mine
    across = [{"tensor": lax.rem(me + s, parts)} for s in range(1, parts)]
    beside = [{"dp": first + lax.rem(mine + s, groups)} for s in range(1, groups)]

    barrier = pltpu.get_barrier_semaphore()
    for peer in across + beside:
        pl.semaphore_signal(barrier, inc=1, device_id=peer, device_id_type=MESH)
    pl.semaphore_wait(barrier, len(across) + len(beside))

    count = [0, 0]

    def remote(src, dst, peer, sems=None):
        if sems is None:
            sems = (send.at[count[0]], recv.at[count[0]])
            count[0] += 1
        copy = pltpu.make_async_remote_copy(
            src_ref=src,
            dst_ref=dst,
            send_sem=sems[0],
            recv_sem=sems[1],
            device_id=peer,
            device_id_type=MESH,
        )
        copy.start()
        return copy

    def near(src, dst, sem=None):
        if sem is None:
            sem = own.at[count[1]]
            count[1] += 1
        copy = pltpu.make_async_copy(src, dst, sem)
        copy.start()
        return copy

    sent = []

    def arrived(copies):
        for copy in copies:
            copy.wait_recv()
        sent.extend(copies)

    def pixels(ref, peer):
        return ref.at[:, pl.ds(pl.multiple_of(peer * pix, LANES), pix)]

    def to_owner(ref, out):
        return [remote(pixels(ref, p["tensor"]), out.at[me], p) for p in across]

    my_slab = pl.ds(pl.multiple_of(mine * slab, slab), slab)
    steps = [jnp.exp(log_dt[j : j + 1, :]) for j in range(2)]
    coefs = [c_height, c_width]

    partner = {"tensor": me + 1 - 2 * lax.rem(me, 2)}
    inner_device = {"tensor": jnp.where(me < 2, 2, 1)}
    is_inner = (me == 1) | (me == 2)
    other_half = 2 - 2 * (me // 2)

    def cols_of(t):
        return pl.ds(pl.multiple_of(t * shard, LANES), shard)

    def pieces(t):
        return [
            (win.at[my_slab, cols_of(t)], win.at[my_slab, cols_of(t)]),
            (wout.at[t, my_slab, :], wout.at[t, my_slab, :]),
            (small_all.at[t], small_all.at[t]),
        ]

    def hop(i, k, pair, peer, way):
        return pltpu.make_async_remote_copy(
            src_ref=pair[0],
            dst_ref=pair[1],
            send_sem=hop_send.at[way, i],
            recv_sem=hop_recv.at[k, i],
            device_id=peer,
            device_id_type=MESH,
        )

    first_hops = []
    slabs = [w_in.at[my_slab, :], w_out.at[my_slab, :], small_mine]
    for i in range(3):
        if i == 2:
            small_mine[...] = jnp.zeros_like(small_mine)
            lag_kernels(steps, a_log, a_imag, coefs, small_mine)
            small_mine[2 * CROP : 2 * CROP + 1, 0:local] = skip_gain[...].reshape(1, local)
            biases = b_in[...].reshape(1, shard)
            for j in range(shard // LANES):
                small_mine[32 + j : 33 + j, :] = biases[:, j * LANES : (j + 1) * LANES]
        pair = (slabs[i], pieces(me)[i][1])
        first_hops.append(hop(i, 0, pair, partner, 0))
        first_hops.append(hop(i, 1 + lax.rem(me, 2), pair, inner_device, 1))
        for copy in first_hops[-2:]:
            copy.start()
    w_near = [near(slabs[i], pieces(me)[i][1]) for i in range(2)]
    small_all[me] = small_mine[...]

    def handed_on(k):
        found = pieces(other_half + k)
        return [hop(i, 1 + k, found[i], partner, 2 + k) for i in range(3)]

    @pl.when(is_inner)
    def _():
        for k in range(2):
            for copy in handed_on(k):
                copy.wait_recv()
            for copy in handed_on(k):
                copy.start()

    x_copies = to_owner(x, x_all)
    x_near = near(pixels(x, me), x_all.at[me])

    @pl.when(jnp.logical_not(is_inner))
    def _():
        for k in range(2):
            for copy in handed_on(k):
                copy.wait_recv()

    for copy in w_near:
        copy.wait()
    for copy in first_hops[::2]:
        copy.wait_recv()
    w_copies = [remote(win.at[my_slab, :], win.at[my_slab, :], p) for p in beside]
    w_copies += [remote(wout.at[:, my_slab, :], wout.at[:, my_slab, :], p) for p in beside]

    square[...] = jnp.zeros_like(square)
    for row, ref in enumerate((ln_gain, ln_bias, b_out, layer_scale)):
        square[row : row + 1, :] = ref[...].reshape(1, width)
    for i in range(width // LANES):
        chan[i * LANES : (i + 1) * LANES, :] = jnp.transpose(square[:, i * LANES : (i + 1) * LANES])
    canvases = size_ref.shape[1]
    square[0:8, 0:canvases] = offset_ref[...].astype(F32)
    square[8:16, 0:canvases] = size_ref[...].astype(F32)
    turned[...] = jnp.transpose(square[:, 0:LANES])
    at = pl.ds(pl.multiple_of(me * 8, 8), 8)
    for slot in range(4):
        for j in range(2):
            k = 2 * slot + j
            low = jnp.broadcast_to(turned[at, k : k + 1], (8, LANES))
            high = low + jnp.broadcast_to(turned[at, 8 + k : 9 + k], (8, LANES))
            for s in range(CROP):
                mask[slot, CROP * j + s] = jnp.where((low <= s) & (s < high), 1.0, 0.0)
    for q in range(local // GROUP):
        kern[q] = jnp.concatenate(
            [small_all[t, 0:32, q * GROUP : (q + 1) * GROUP] for t in range(parts)], axis=1
        )
    for t in range(parts):
        for i in range(shard // LANES):
            block = jnp.broadcast_to(small_all[t, 32 + i : 33 + i, :], (LANES, LANES))
            bin_col[t * shard + i * LANES : t * shard + (i + 1) * LANES, :] = jnp.transpose(block)
    arrived(w_copies)
    for t in range(parts):
        cols = slice(t * shard, (t + 1) * shard)
        win_t[cols, :] = jnp.transpose(win[:, cols].astype(F32)).astype(BF16)
        wout_t[:, cols] = jnp.transpose(wout[t].astype(F32)).astype(BF16)

    arrived(x_copies)
    x_near.wait()
    go_copies = to_owner(go, go_all)

    @pl.loop(0, local // GROUP)
    def _(q):
        mix_fwd(q, x_all, rows, kern, mask, inner, mixed)

    def hid_copy(t, j, back):
        sl = pl.ds(t * shard, shard)
        lanes = pl.ds(pl.multiple_of(j * STEP, LANES), STEP)
        pair = [(hid.at[sl, :], hid_far.at[sl, lanes]), (slope.at[sl, :], slope_far.at[sl, lanes])]
        pair = [p[::-1] if back else p for p in pair]
        return [
            pltpu.make_async_copy(*p, sem.at[t]) for p, sem in zip(pair, (hid_sem, slope_sem))
        ]

    others = [p["tensor"] for p in across]

    def res_chunk(j):
        lanes = pl.ds(pl.multiple_of(j * STEP, LANES), STEP)
        pairs = [(t, res) for t in others] + [(me, res_own)]
        return [
            pltpu.make_async_copy(res_near.at[t], ref.at[t, :, lanes], res_sem.at[i])
            for i, (t, ref) in enumerate(pairs)
        ]

    def low_of(off):
        normed, scale = norm(mixed[:, :, pl.ds(off, STEP)].reshape(width, STEP).astype(F32))
        return normed, scale, (normed * chan[:, 0:1] + chan[:, 1:2]).astype(BF16)

    @pl.loop(0, chunks)
    def _(j):
        off = pl.multiple_of(j * STEP, LANES)
        _, _, low = low_of(off)
        for t in range(parts):
            sl = pl.ds(t * shard, shard)
            pre = nn(win_t[sl, :], low) + bin_col[sl, 0:1]
            square_pre = pre * pre
            th = jnp.tanh(pre * (GELU_C + (GELU_C * GELU_A) * square_pre))
            half = 0.5 * th + 0.5
            inner_slope = GELU_C + (3 * GELU_C * GELU_A) * square_pre

            @pl.when(j > 0)
            def _():
                for copy in hid_copy(t, j, False):
                    copy.wait()

            hid[sl, :] = (pre * half).astype(BF16)
            slope[sl, :] = (half + pre * (0.5 - 0.5 * th * th) * inner_slope).astype(BF16)
            for copy in hid_copy(t, j, False):
                copy.start()
        branch = nn(wout_t[...], hid[...]) + chan[:, 2:3]
        source = x_all[:, :, pl.ds(off, STEP)].reshape(width, STEP).astype(F32)
        out = (source + chan[:, 3:4] * branch).astype(BF16)

        @pl.when(j > 0)
        def _():
            for copy in res_chunk(j):
                copy.wait()

        res_near[...] = out.reshape(parts, local, STEP)
        for copy in res_chunk(j):
            copy.start()

    for t in range(parts):
        for copy in hid_copy(t, 0, False):
            copy.wait()
        for copy in hid_copy(t, 0, True):
            copy.start()

    for copy in res_chunk(0):
        copy.wait()

    arrived(go_copies)
    res_copies = [remote(res.at[p["tensor"]], res_own.at[me], p) for p in across]

    for ref in (dw, bin_acc, vec):
        ref[...] = jnp.zeros_like(ref)

    def go_chunk(j):
        off = pl.multiple_of(j * STEP, LANES)
        mine_at = pl.ds(pl.multiple_of(me * pix + off, LANES), STEP)
        sources = [(t, go_all.at[t, :, pl.ds(off, STEP)]) for t in others] + [(me, go.at[:, mine_at])]
        return [
            pltpu.make_async_copy(src, go_near.at[t], go_sem.at[i])
            for i, (t, src) in enumerate(sources)
        ]

    for copy in go_chunk(0):
        copy.start()

    @pl.loop(0, chunks)
    def _(j):
        off = pl.multiple_of(j * STEP, LANES)
        for copy in go_chunk(j):
            copy.wait()
        grad = go_near[...].reshape(width, STEP).astype(F32)
        gb = (grad * chan[:, 3:4]).astype(BF16)
        vec[0] += fold(gb.astype(F32))
        vec[3] += fold(grad)

        @pl.when(j + 1 < chunks)
        def _():
            for copy in go_chunk(j + 1):
                copy.start()

        normed, scale, low = low_of(off)
        for t in range(parts):
            sl = pl.ds(t * shard, shard)
            for copy in hid_copy(t, j, True):
                copy.wait()
            tile = (nn(wout[t], gb) * slope[sl, :].astype(F32)).astype(BF16)
            gp[sl, :] = tile
            bin_acc[sl, :] += fold(tile.astype(F32))
            dw[0, t] += nt(hid[sl, :], gb)
            dw[1, t] += nt(tile, low)

            @pl.when(j + 1 < chunks)
            def _():
                for copy in hid_copy(t, j + 1, True):
                    copy.start()

        gn = nn(win[...], gp[...])
        vec[1] += fold(gn * normed)
        vec[2] += fold(gn)
        g1 = gn * chan[:, 0:1]
        m1 = jnp.mean(g1, axis=0, keepdims=True)
        m2 = jnp.mean(g1 * normed, axis=0, keepdims=True)
        gm = (scale * (g1 - m1 - normed * m2)).reshape(parts, local, STEP)
        for q in range(local // GROUP):
            block = gm[:, q * GROUP : (q + 1) * GROUP, :].reshape(LANES, STEP)
            grow[q, pl.ds(off, STEP), :] = jnp.transpose(block)

    def slab_of(peer):
        return pl.ds(pl.multiple_of((peer["dp"] - first) * slab, slab), slab)

    dw_near = near(dw.at[:, :, my_slab, :], dw_peer.at[:, :, my_slab, :])
    dw_copies = [
        remote(dw.at[:, :, slab_of(p), :], dw_peer.at[:, :, my_slab, :], p) for p in beside
    ]

    back = [near(go_all.at[t], mixed.at[t]) for t in others]
    back.append(near(pixels(go, me), mixed.at[me]))
    for copy in back:
        copy.wait()

    def gx_tile(q):
        return pl.ds(pl.multiple_of(q * GROUP, GROUP), GROUP)

    def gx_copies(q):
        at = gx_tile(q)
        return [
            pltpu.make_async_remote_copy(
                src_ref=mixed.at[p["tensor"], at, :],
                dst_ref=g_own.at[me, at, :],
                send_sem=gx_send.at[q, s],
                recv_sem=gx_recv.at[q, s],
                device_id=p,
                device_id_type=MESH,
            )
            for s, p in enumerate(across)
        ] + [pltpu.make_async_copy(mixed.at[me, at, :], g_own.at[me, at, :], gx_own.at[q])]

    @pl.loop(0, local // GROUP)
    def _(q):
        mix_bwd(q, x_all, rows, grow, kern, mask, inner, mid, mixed, gkern)

        @pl.when(q + 1 < local // GROUP)
        def _():
            for copy in gx_copies(q):
                copy.start()

    for t in range(parts):
        lanes = slice(t * GROUP, (t + 1) * GROUP)
        pack_mine[t] = jnp.zeros(pack_mine.shape[1:], F32)
        pack_mine[t, 0:32, 0:local] = jnp.concatenate(
            [gkern[q, 0:32, lanes] for q in range(local // GROUP)], axis=1
        )
    acc = jnp.zeros((width, LANES), F32)
    sums = [jnp.sum(vec[k], axis=1, keepdims=True) for k in range(4)]
    for k in range(3):
        acc = column_set(acc, k, sums[k])
    square[0:1, :] = sum(
        jnp.sum(wout[t].astype(F32) * dw[0, t], axis=0, keepdims=True) for t in range(parts)
    )
    products = jnp.concatenate(
        [
            jnp.transpose(square[:, i * LANES : (i + 1) * LANES])[:, 0:1]
            for i in range(width // LANES)
        ]
    )
    acc = column_set(acc, 3, products / chan[:, 3:4] + chan[:, 2:3] * sums[3])
    hidden_sums = jnp.sum(bin_acc[...], axis=1, keepdims=True)
    for k in range(shard // local):
        starts = [t * shard + k * local for t in range(parts)]
        acc = column_set(acc, 4 + k, jnp.concatenate([hidden_sums[i : i + local] for i in starts]))
    for t in range(parts):
        square[0:local, 0:LANES] = acc[t * local : (t + 1) * local]
        pack_mine[t, 32:40, :] = jnp.transpose(square[:, 0:LANES])[0:8]
    pack_peer[mine] = pack_mine[...]
    pack_copies = [remote(pack_mine, pack_peer.at[mine], p) for p in beside]

    dw_near.wait()
    for copy in dw_copies:
        copy.wait()
    near(dw_peer, dw).wait()
    terms = [dw[:, :, i * slab : (i + 1) * slab, :] for i in range(groups)]
    dw_sum[...] = sum(terms[1:], terms[0])
    dw_low[...] = dw_sum[...].astype(BF16)
    dw_copies = [remote(dw_low.at[:, t], dw_tensor.at[me], p) for t, p in zip(others, across)]
    arrived(pack_copies)
    pack_sum[...] = sum((pack_peer[i] for i in range(1, groups)), pack_peer[0])
    pack_tensor[me] = pack_sum[me]
    pack_copies = [remote(pack_sum.at[t], pack_tensor.at[me], p) for t, p in zip(others, across)]
    for copy in gx_copies(local // GROUP - 1):
        copy.start()

    arrived(dw_copies)
    dw_done[...] = sum((dw_tensor[t].astype(F32) for t in others), dw_sum[:, me])
    dw_near = near(dw_done, dw_own.at[:, my_slab, :])
    dw_copies = [remote(dw_done, dw_own.at[:, my_slab, :], p) for p in beside]
    arrived(pack_copies)
    total = sum((pack_tensor[i] for i in range(1, parts)), pack_tensor[0])
    gdt = lag_grads(total, steps, a_log, a_imag, coefs, g_alog, g_aimag, [g_height, g_width])
    row_own[...] = total
    for j in range(2):
        row_own[29 + j : 30 + j, 0:local] = gdt[j]

    arrived(dw_copies)
    dw_near.wait()
    arrived(res_copies)

    @pl.loop(0, local // GROUP)
    def _(q):
        for copy in gx_copies(q):
            copy.wait()

    for copy in sent + first_hops:
        copy.wait_send()

    @pl.when(is_inner)
    def _():
        for k in range(2):
            for copy in handed_on(k):
                copy.wait_send()


def block(parts, groups, args):
    x, size = args[0], args[2]
    local, pixels = x.shape
    pix = pixels // parts
    width = local * parts
    w_in = args[12]
    shard = w_in.shape[1]
    ff = shard * parts
    slab = shard // groups
    tiles = local // GROUP
    states = args[4].shape[0]
    shape = jax.ShapeDtypeStruct
    vmem = pl.BlockSpec(memory_space=pltpu.VMEM)
    hbm = pl.BlockSpec(memory_space=pl.ANY)
    in_specs = [hbm, hbm] + [vmem] * 10 + [hbm, vmem, hbm, vmem, vmem]
    outs = [
        (shape((parts, local, pix), BF16), hbm),
        (shape((parts, local, pix), BF16), hbm),
        (shape((2, shard, width), F32), hbm),
        (shape((states, local), F32), vmem),
        (shape((states, local), F32), vmem),
        (shape((2, states, local), F32), vmem),
        (shape((2, states, local), F32), vmem),
        (shape((40, LANES), F32), vmem),
        (shape((parts, local, pix), BF16), hbm),
        (shape((ff, pix), BF16), hbm),
        (shape((ff, pix), BF16), hbm),
        (shape((parts, local, pix), BF16), hbm),
        (shape((2, parts, shard, width), F32), hbm),
    ]
    remotes = 5 * (parts - 1) + 5 * (groups - 1)
    dma = pltpu.SemaphoreType.DMA
    scratch = [
        pltpu.VMEM((parts, local, pix), BF16),
        pltpu.VMEM((parts, local, pix), BF16),
        pltpu.VMEM((parts, local, STEP), BF16),
        pltpu.VMEM((pix, LANES), F32),
        pltpu.VMEM((tiles, pix, LANES), F32),
        pltpu.VMEM((CROP, CROP, 8, LANES), F32),
        pltpu.VMEM((CROP, CROP, 8, LANES), F32),
        pltpu.VMEM((4, 2 * CROP, 8, LANES), F32),
        pltpu.VMEM((40, LANES), F32),
        pltpu.VMEM((parts, 40, LANES), F32),
        pltpu.VMEM((tiles, 32, LANES), F32),
        pltpu.VMEM((tiles, 32, LANES), F32),
        pltpu.VMEM((ff, LANES), F32),
        pltpu.VMEM((width, LANES), F32),
        pltpu.VMEM((LANES, width), F32),
        pltpu.VMEM((LANES, LANES), F32),
        pltpu.VMEM((width, ff), BF16),
        pltpu.VMEM((ff, width), BF16),
        pltpu.VMEM((parts, shard, width), BF16),
        pltpu.VMEM((width, ff), BF16),
        pltpu.VMEM((ff, STEP), BF16),
        pltpu.VMEM((ff, STEP), BF16),
        pltpu.VMEM((ff, STEP), BF16),
        pltpu.VMEM((parts, local, STEP), BF16),
        pltpu.VMEM((2, parts, shard, width), F32),
        pltpu.VMEM((2, parts, slab, width), F32),
        pltpu.VMEM((2, parts, slab, width), BF16),
        pltpu.VMEM((parts, 2, slab, width), BF16),
        pltpu.VMEM((2, slab, width), F32),
        pltpu.VMEM((ff, LANES), F32),
        pltpu.VMEM((4, width, LANES), F32),
        pltpu.VMEM((parts, 40, LANES), F32),
        pltpu.VMEM((groups, parts, 40, LANES), F32),
        pltpu.VMEM((parts, 40, LANES), F32),
        pltpu.VMEM((parts, 40, LANES), F32),
        dma((remotes,)),
        dma((remotes,)),
        dma((10,)),
        dma((4, 3)),
        dma((3, 3)),
        dma((parts,)),
        dma((parts,)),
        dma((parts,)),
        dma((parts,)),
        dma((tiles, parts - 1)),
        dma((tiles, parts - 1)),
        dma((tiles,)),
    ]
    return pl.pallas_call(
        functools.partial(block_kernel, parts, groups),
        out_shape=[o[0] for o in outs],
        in_specs=in_specs,
        out_specs=[o[1] for o in outs],
        scratch_shapes=scratch,
        compiler_params=pltpu.CompilerParams(
            collective_id=0, has_side_effects=True, vmem_limit_bytes=VMEM
        ),
        name="block",
    )(*args)


def finish_kernel(parts, n_sums, *refs):
    sums, refs = refs[:n_sums], refs[n_sums:]
    res_ref, g_ref, result_ref, grad_ref = refs[:4]
    n_small = (len(refs) - 11 - n_sums) // 2
    smalls, refs = refs[4 : 4 + n_small], refs[4 + n_small :]
    res_near, g_near, grad_near = refs[:3]
    sums_near = refs[3 : 3 + n_sums]
    near = refs[3 + n_sums : 3 + n_sums + n_small]
    came, left, sums_came, smalls_left = refs[3 + n_sums + n_small :]
    pix = g_near.shape[2]
    in_copies, out_copies = [], []
    for i, (a, b) in enumerate(((g_ref, g_near), (res_ref, res_near))):
        for s in range(parts):
            in_copies.append(pltpu.make_async_copy(a.at[s], b.at[s], came.at[i, s]))
            in_copies[-1].start()
        if i == 0:
            small_in = [
                pltpu.make_async_copy(sums[k], sums_near[k], sums_came.at[k]) for k in range(n_sums)
            ]
            for copy in small_in:
                copy.start()

    def put(src, dst, sem):
        out_copies.append(pltpu.make_async_copy(src, dst, sem))
        out_copies[-1].start()

    for s in range(parts):
        in_copies[s].wait()
        grad_near[s] = g_near[s].astype(F32)
        put(grad_near.at[s], grad_ref.at[:, pl.ds(s * pix, pix)], left.at[0, s])
        if s == 0:
            for copy in small_in:
                copy.wait()
            dw, g_alog, g_aimag, g_height, g_width, rows = sums_near
            alog, aimag, height, width, dt, skip, gain, bias, win, bin_, wout, bout, scale = near
            for out, ref in ((alog, g_alog), (aimag, g_aimag), (height, g_height), (width, g_width)):
                out[...] = ref[...]
            local = skip.shape[0]
            dt[...] = rows[29:31, 0:local]
            for out, k in ((skip, 28), (gain, 33), (bias, 34), (bout, 32), (scale, 35)):
                out[...] = rows[k : k + 1, 0:local].reshape(local)
            bin_[...] = jnp.concatenate(
                [rows[36 + k : 37 + k, 0:local] for k in range(bin_.shape[0] // local)], axis=1
            ).reshape(bin_.shape)
            win[...] = jnp.transpose(dw[1])
            wout[...] = dw[0]
            for k in range(n_small):
                put(near[k], smalls[k], smalls_left.at[k])
    for s in range(parts):
        in_copies[parts + s].wait()
        put(res_near.at[s], result_ref.at[:, pl.ds(s * pix, pix)], left.at[1, s])
    for copy in out_copies:
        copy.wait()


def finish(res_own, g_own, sums):
    parts, local, pix = g_own.shape
    dw, g_alog, _, g_height, _, _ = sums
    hbm = pl.BlockSpec(memory_space=pl.ANY)
    dma = pltpu.SemaphoreType.DMA
    shape = jax.ShapeDtypeStruct
    line = (local,)
    small = (
        g_alog.shape,
        g_alog.shape,
        g_height.shape,
        g_height.shape,
        (2, local),
        line,
        line,
        line,
        (dw.shape[2], dw.shape[1]),
        (dw.shape[1],),
        dw.shape[1:],
        line,
        line,
    )
    return pl.pallas_call(
        functools.partial(finish_kernel, parts, len(sums)),
        out_shape=(shape((local, parts * pix), BF16), shape((local, parts * pix), F32))
        + tuple(shape(a, F32) for a in small),
        in_specs=[hbm] * (2 + len(sums)),
        out_specs=(hbm,) * (2 + len(small)),
        scratch_shapes=[
            pltpu.VMEM(g_own.shape, BF16),
            pltpu.VMEM(g_own.shape, BF16),
            pltpu.VMEM(g_own.shape, F32),
        ]
        + [pltpu.VMEM(a.shape, F32) for a in sums]
        + [pltpu.VMEM(a, F32) for a in small]
        + [dma((2, parts)), dma((2, parts)), dma((len(sums),)), dma((len(small),))],
        compiler_params=pltpu.CompilerParams(vmem_limit_bytes=VMEM),
        name="finish",
    )(*sums, res_own, g_own)


def per_device(
    parts,
    dp_size,
    inputs,
    crop_size,
    crop_offset,
    a_log,
    a_imag,
    c_height,
    c_width,
    log_dt,
    skip_gain,
    ln_gain,
    ln_bias,
    w_in,
    b_in,
    w_out,
    b_out,
    layer_scale,
    grad_out,
):
    canvases = crop_size.shape[0]
    groups = min(dp_size, 8)
    args = (
        inputs,
        grad_out,
        jnp.transpose(crop_size.reshape(canvases, 8)),
        jnp.transpose(crop_offset.reshape(canvases, 8)),
        jnp.transpose(a_log),
        jnp.transpose(a_imag),
        jnp.transpose(c_height, (0, 2, 1)),
        jnp.transpose(c_width, (0, 2, 1)),
        log_dt,
        skip_gain,
        ln_gain,
        ln_bias,
        w_in,
        b_in,
        w_out,
        b_out,
        layer_scale,
    )
    out = block(parts, groups, args)
    sums = tuple(out[2:8])
    if dp_size > groups:
        teams = [[r + groups * g for g in range(dp_size // groups)] for r in range(groups)]
        sums = lax.psum(sums, "dp", axis_index_groups=teams)
    done = finish(out[0], out[1], sums)
    return (
        done[0],
        done[1],
        jnp.transpose(done[2]),
        jnp.transpose(done[3]),
        jnp.transpose(done[4], (0, 2, 1)),
        jnp.transpose(done[5], (0, 2, 1)),
        *done[6:],
    )


def solution(mesh):
    in_specs = (
        P("tensor", "dp"),
        P("dp", None, None),
        P("dp", None, None),
        P("tensor", None),
        P("tensor", None),
        P(None, "tensor", None),
        P(None, "tensor", None),
        P(None, "tensor"),
        P("tensor"),
        P(),
        P(),
        P(None, "tensor"),
        P("tensor"),
        P("tensor", None),
        P(),
        P(),
        P("tensor", "dp"),
    )
    out_specs = (
        P("tensor", "dp"),
        P("tensor", "dp"),
        P("tensor", None),
        P("tensor", None),
        P(None, "tensor", None),
        P(None, "tensor", None),
        P(None, "tensor"),
        P("tensor"),
        P("tensor"),
        P("tensor"),
        P(None, "tensor"),
        P("tensor"),
        P("tensor", None),
        P("tensor"),
        P("tensor"),
    )
    return jax.shard_map(
        functools.partial(per_device, mesh.shape["tensor"], mesh.shape["dp"]),
        mesh=mesh,
        in_specs=in_specs,
        out_specs=out_specs,
        check_vma=False,
    )
```

```python
import functools

import jax
import jax.numpy as jnp
from jax import lax
from jax.experimental import pallas as pl
from jax.experimental.pallas import tpu as pltpu
from jax.sharding import PartitionSpec as P

F32, BF16 = jnp.float32, jnp.bfloat16
CROP = 14
SIDE = 2 * CROP
NPIX = SIDE * SIDE
LANES = 128
GROUP = 32
STEP = 896
EPS = 1e-06
GELU_C = 0.7978845608028654
GELU_A = 0.044715
VMEM = 63 << 20
MESH = pl.DeviceIdType.MESH


def nn(a, b):
    return lax.dot_general(a, b, (((1,), (0,)), ((), ())), preferred_element_type=F32)


def nt(a, b):
    return lax.dot_general(a, b, (((1,), (1,)), ((), ())), preferred_element_type=F32)


def conv(y, taps):
    return [sum((taps[l] * y[i - l] for l in range(1, i + 1)), taps[0] * y[i]) for i in range(CROP)]


def conv_back(y, taps):
    return [
        sum((taps[l] * y[i + l] for l in range(1, CROP - i)), taps[0] * y[i]) for i in range(CROP)
    ]


def spot(slot, h, w):
    first = (slot // 2) * (CROP * SIDE) + (slot % 2) * CROP
    return pl.ds(first + h * SIDE + w, 8, stride=NPIX)


def lanes_to_rows(load, rows):
    @pl.loop(0, rows.shape[0] // STEP)
    def _(j):
        off = pl.multiple_of(j * STEP, LANES)
        rows[pl.ds(off, STEP), :] = jnp.transpose(load(off).astype(F32))


def rows_to_lanes(rows, store):
    @pl.loop(0, rows.shape[0] // STEP)
    def _(j):
        off = pl.multiple_of(j * STEP, LANES)
        store(off, jnp.transpose(rows[pl.ds(off, STEP), :]).astype(BF16))


def tap_rows(kern, q, base):
    return [jnp.broadcast_to(kern[q, pl.ds(base + l, 1), :], (8, LANES)) for l in range(CROP)]


def tile_of(ref, q, off):
    return ref[:, pl.ds(pl.multiple_of(q * GROUP, GROUP), GROUP), pl.ds(off, STEP)].reshape(
        LANES, STEP
    )


def put_tile(ref, q, off, v):
    ref[:, pl.ds(pl.multiple_of(q * GROUP, GROUP), GROUP), pl.ds(off, STEP)] = v.reshape(
        ref.shape[0], GROUP, STEP
    )


def along_width(q, slot, rows, kern, mask, inner):
    @pl.loop(0, CROP)
    def _(h):
        taps = tap_rows(kern, q, CROP)
        row_in = mask[slot, h]
        y = [rows[spot(slot, h, w), :] * mask[slot, CROP + w] for w in range(CROP)]
        for w, v in enumerate(conv(y, taps)):
            inner[h, w] = v * row_in


def mix_fwd(q, x_all, rows, kern, mask, inner, mixed):
    lanes_to_rows(lambda off: tile_of(x_all, q, off), rows)
    skip = jnp.broadcast_to(kern[q, pl.ds(2 * CROP, 1), :], (8, LANES))

    @pl.loop(0, 4)
    def _(slot):
        along_width(q, slot, rows, kern, mask, inner)

        @pl.loop(0, CROP)
        def _(w):
            taps = tap_rows(kern, q, 0)
            col_in = mask[slot, CROP + w]
            y = [inner[h, w] for h in range(CROP)]
            for h, v in enumerate(conv(y, taps)):
                at = spot(slot, h, w)
                rows[at, :] = v * (mask[slot, h] * col_in) + skip * rows[at, :]

    rows_to_lanes(rows, lambda off, v: put_tile(mixed, q, off, v))


def mix_bwd(q, x_all, rows, grow, kern, mask, inner, mid, out, gkern):
    lanes_to_rows(lambda off: tile_of(x_all, q, off), rows)
    skip = jnp.broadcast_to(kern[q, pl.ds(2 * CROP, 1), :], (8, LANES))
    zero = jnp.zeros((8, LANES), F32)

    def per_slot(slot, sums):
        gk_height, gk_width, gskip = sums
        along_width(q, slot, rows, kern, mask, inner)

        def down(w, acc):
            taps = tap_rows(kern, q, 0)
            col_in = mask[slot, CROP + w]
            u = [grow[q, spot(slot, h, w), :] * (mask[slot, h] * col_in) for h in range(CROP)]
            for h, v in enumerate(conv_back(u, taps)):
                mid[h, w] = v * mask[slot, h]
            a = [inner[h, w] for h in range(CROP)]
            return tuple(
                sum((u[h] * a[h - l] for h in range(l, CROP)), acc[l]) for l in range(CROP)
            )

        gk_height = lax.fori_loop(0, CROP, down, gk_height)

        def across(h, acc):
            gk_width, gskip = acc
            taps = tap_rows(kern, q, CROP)
            u = [mid[h, w] for w in range(CROP)]
            x = [rows[spot(slot, h, w), :] for w in range(CROP)]
            y = [x[w] * mask[slot, CROP + w] for w in range(CROP)]
            gk_width = tuple(
                sum((u[w] * y[w - l] for w in range(l, CROP)), gk_width[l]) for l in range(CROP)
            )
            for w, v in enumerate(conv_back(u, taps)):
                at = spot(slot, h, w)
                g = grow[q, at, :]
                gskip = gskip + g * x[w]
                grow[q, at, :] = v * mask[slot, CROP + w] + skip * g
            return gk_width, gskip

        gk_width, gskip = lax.fori_loop(0, CROP, across, (gk_width, gskip))
        return gk_height, gk_width, gskip

    gk_height, gk_width, gskip = lax.fori_loop(
        0, 4, per_slot, ((zero,) * CROP, (zero,) * CROP, zero)
    )
    gkern[q] = jnp.zeros((32, LANES), F32)
    for row, v in enumerate((*gk_height, *gk_width, gskip)):
        gkern[q, pl.ds(row, 1), :] = jnp.sum(v, axis=0, keepdims=True)

    @pl.loop(0, rows.shape[0] // STEP)
    def _(j):
        off = pl.multiple_of(j * STEP, LANES)
        turned = jnp.transpose(grow[q, pl.ds(off, STEP), :])
        put_tile(out, q, off, (tile_of(out, q, off).astype(F32) + turned).astype(BF16))


def lag_waves(step, a_log, a_imag):
    rate = -step * jnp.exp(a_log)
    phase = step * a_imag
    size = jnp.exp(rate)
    re1, im1 = size * jnp.cos(phase), size * jnp.sin(phase)
    re, im = jnp.ones_like(re1), jnp.zeros_like(im1)
    out = []
    for _ in range(CROP):
        out.append((re, im))
        re, im = re * re1 - im * im1, re * im1 + im * re1
    return rate, phase, out


def column_set(acc, k, col):
    lane = lax.broadcasted_iota(jnp.int32, acc.shape, 1)
    return jnp.where(lane == k, col, acc)


def lag_kernels(steps, a_log, a_imag, coefs, out):
    local = a_log.shape[1]
    for j in range(2):
        _, _, waves = lag_waves(steps[j], a_log[...], a_imag[...])
        for l, (re, im) in enumerate(waves):
            row = jnp.sum(coefs[j][0] * re - coefs[j][1] * im, axis=0, keepdims=True)
            out[CROP * j + l : CROP * j + l + 1, 0:local] = row


def lag_grads(rows, steps, a_log, a_imag, coefs, g_alog, g_aimag, g_coefs):
    ga, gi, gdt = 0.0, 0.0, []
    for j in range(2):
        rate, phase, waves = lag_waves(steps[j], a_log[...], a_imag[...])
        cre, cim = coefs[j][0], coefs[j][1]
        g_re = g_im = p = r = 0.0
        for l, (re, im) in enumerate(waves):
            g = rows[CROP * j + l : CROP * j + l + 1, 0 : a_log.shape[1]]
            g_re = g_re + g * re
            g_im = g_im - g * im
            if l:
                p = p + (l * g) * (cre * re - cim * im)
                r = r - (l * g) * (cre * im + cim * re)
        g_coefs[j][0] = g_re
        g_coefs[j][1] = g_im
        ga = ga + p * rate
        gi = gi + r * steps[j]
        gdt.append(jnp.sum(p * rate + r * phase, axis=0, keepdims=True))
    g_alog[...] = ga
    g_aimag[...] = gi
    return gdt


def norm(m):
    centered = m - jnp.mean(m, axis=0, keepdims=True)
    scale = lax.rsqrt(jnp.mean(centered * centered, axis=0, keepdims=True) + EPS)
    return centered * scale, scale


def fold(v):
    return sum(
        (v[:, i * LANES : (i + 1) * LANES] for i in range(1, v.shape[1] // LANES)), v[:, :LANES]
    )


def block_kernel(
    parts,
    groups,
    x,
    go,
    size_ref,
    offset_ref,
    a_log,
    a_imag,
    c_height,
    c_width,
    log_dt,
    skip_gain,
    ln_gain,
    ln_bias,
    w_in,
    b_in,
    w_out,
    b_out,
    layer_scale,
    res_own,
    g_own,
    dw_own,
    g_alog,
    g_aimag,
    g_height,
    g_width,
    row_own,
    go_all,
    hid_far,
    slope_far,
    res,
    dw_peer,
    x_all,
    mixed,
    res_near,
    rows,
    grow,
    inner,
    mid,
    mask,
    small_mine,
    small_all,
    kern,
    gkern,
    bin_col,
    chan,
    square,
    turned,
    win,
    win_t,
    wout,
    wout_t,
    hid,
    slope,
    gp,
    go_near,
    dw,
    dw_sum,
    dw_low,
    dw_tensor,
    dw_pass,
    dw_done,
    bin_acc,
    vec,
    pack_mine,
    pack_peer,
    pack_sum,
    pack_tensor,
    pack_pass,
    send,
    recv,
    own,
    hop_send,
    hop_recv,
    leg_send,
    leg_recv,
    hid_sem,
    slope_sem,
    go_sem,
    res_sem,
    gx_send,
    gx_recv,
    gx_own,
):
    local, pix = x_all.shape[1], x_all.shape[2]
    width = local * parts
    ff = win_t.shape[0]
    shard = ff // parts
    slab = shard // groups
    chunks = pix // STEP
    me = lax.axis_index("tensor")
    dp = lax.axis_index("dp")
    mine = lax.rem(dp, groups)
    first = dp - mine
    across = [{"tensor": lax.rem(me + s, parts)} for s in range(1, parts)]
    beside = [{"dp": first + lax.rem(mine + s, groups)} for s in range(1, groups)]

    barrier = pltpu.get_barrier_semaphore()
    for peer in across + beside:
        pl.semaphore_signal(barrier, inc=1, device_id=peer, device_id_type=MESH)
    pl.semaphore_wait(barrier, len(across) + len(beside))

    count = [0, 0]

    def remote(src, dst, peer, sems=None):
        if sems is None:
            sems = (send.at[count[0]], recv.at[count[0]])
            count[0] += 1
        copy = pltpu.make_async_remote_copy(
            src_ref=src,
            dst_ref=dst,
            send_sem=sems[0],
            recv_sem=sems[1],
            device_id=peer,
            device_id_type=MESH,
        )
        copy.start()
        return copy

    def near(src, dst, sem=None):
        if sem is None:
            sem = own.at[count[1]]
            count[1] += 1
        copy = pltpu.make_async_copy(src, dst, sem)
        copy.start()
        return copy

    sent = []

    def arrived(copies):
        for copy in copies:
            copy.wait_recv()
        sent.extend(copies)

    def pixels(ref, peer):
        return ref.at[:, pl.ds(pl.multiple_of(peer * pix, LANES), pix)]

    def to_owner(ref, out):
        return [remote(pixels(ref, p["tensor"]), out.at[me], p) for p in across]

    my_slab = pl.ds(pl.multiple_of(mine * slab, slab), slab)
    steps = [jnp.exp(log_dt[j : j + 1, :]) for j in range(2)]
    coefs = [c_height, c_width]

    partner = {"tensor": me + 1 - 2 * lax.rem(me, 2)}
    inner_device = {"tensor": jnp.where(me < 2, 2, 1)}
    is_inner = (me == 1) | (me == 2)
    other_half = 2 - 2 * (me // 2)

    def cols_of(t):
        return pl.ds(pl.multiple_of(t * shard, LANES), shard)

    def pieces(t):
        return [
            (win.at[my_slab, cols_of(t)], win.at[my_slab, cols_of(t)]),
            (wout.at[t, my_slab, :], wout.at[t, my_slab, :]),
            (small_all.at[t], small_all.at[t]),
        ]

    def hop(i, k, pair, peer, way):
        return pltpu.make_async_remote_copy(
            src_ref=pair[0],
            dst_ref=pair[1],
            send_sem=hop_send.at[way, i],
            recv_sem=hop_recv.at[k, i],
            device_id=peer,
            device_id_type=MESH,
        )

    first_hops = []
    slabs = [w_in.at[my_slab, :], w_out.at[my_slab, :], small_mine]
    for i in range(3):
        if i == 2:
            small_mine[...] = jnp.zeros_like(small_mine)
            lag_kernels(steps, a_log, a_imag, coefs, small_mine)
            small_mine[2 * CROP : 2 * CROP + 1, 0:local] = skip_gain[...].reshape(1, local)
            biases = b_in[...].reshape(1, shard)
            for j in range(shard // LANES):
                small_mine[32 + j : 33 + j, :] = biases[:, j * LANES : (j + 1) * LANES]
        pair = (slabs[i], pieces(me)[i][1])
        first_hops.append(hop(i, 0, pair, partner, 0))
        first_hops.append(hop(i, 1 + lax.rem(me, 2), pair, inner_device, 1))
        for copy in first_hops[-2:]:
            copy.start()
    w_near = [near(slabs[i], pieces(me)[i][1]) for i in range(2)]
    small_all[me] = small_mine[...]

    def handed_on(k):
        found = pieces(other_half + k)
        return [hop(i, 1 + k, found[i], partner, 2 + k) for i in range(3)]

    @pl.when(is_inner)
    def _():
        for k in range(2):
            for copy in handed_on(k):
                copy.wait_recv()
            for copy in handed_on(k):
                copy.start()

    x_copies = to_owner(x, x_all)
    x_near = near(pixels(x, me), x_all.at[me])

    @pl.when(jnp.logical_not(is_inner))
    def _():
        for k in range(2):
            for copy in handed_on(k):
                copy.wait_recv()

    for copy in w_near:
        copy.wait()
    for copy in first_hops[::2]:
        copy.wait_recv()
    w_copies = [remote(win.at[my_slab, :], win.at[my_slab, :], p) for p in beside]
    w_copies += [remote(wout.at[:, my_slab, :], wout.at[:, my_slab, :], p) for p in beside]

    square[...] = jnp.zeros_like(square)
    for row, ref in enumerate((ln_gain, ln_bias, b_out, layer_scale)):
        square[row : row + 1, :] = ref[...].reshape(1, width)
    for i in range(width // LANES):
        chan[i * LANES : (i + 1) * LANES, :] = jnp.transpose(square[:, i * LANES : (i + 1) * LANES])
    canvases = size_ref.shape[1]
    square[0:8, 0:canvases] = offset_ref[...].astype(F32)
    square[8:16, 0:canvases] = size_ref[...].astype(F32)
    turned[...] = jnp.transpose(square[:, 0:LANES])
    at = pl.ds(pl.multiple_of(me * 8, 8), 8)
    for slot in range(4):
        for j in range(2):
            k = 2 * slot + j
            low = jnp.broadcast_to(turned[at, k : k + 1], (8, LANES))
            high = low + jnp.broadcast_to(turned[at, 8 + k : 9 + k], (8, LANES))
            for s in range(CROP):
                mask[slot, CROP * j + s] = jnp.where((low <= s) & (s < high), 1.0, 0.0)
    for q in range(local // GROUP):
        kern[q] = jnp.concatenate(
            [small_all[t, 0:32, q * GROUP : (q + 1) * GROUP] for t in range(parts)], axis=1
        )
    for t in range(parts):
        for i in range(shard // LANES):
            block = jnp.broadcast_to(small_all[t, 32 + i : 33 + i, :], (LANES, LANES))
            bin_col[t * shard + i * LANES : t * shard + (i + 1) * LANES, :] = jnp.transpose(block)
    arrived(w_copies)
    for t in range(parts):
        cols = slice(t * shard, (t + 1) * shard)
        win_t[cols, :] = jnp.transpose(win[:, cols].astype(F32)).astype(BF16)
        wout_t[:, cols] = jnp.transpose(wout[t].astype(F32)).astype(BF16)

    arrived(x_copies)
    x_near.wait()
    go_copies = to_owner(go, go_all)

    @pl.loop(0, local // GROUP)
    def _(q):
        mix_fwd(q, x_all, rows, kern, mask, inner, mixed)

    def hid_copy(t, j, back):
        sl = pl.ds(t * shard, shard)
        lanes = pl.ds(pl.multiple_of(j * STEP, LANES), STEP)
        pair = [(hid.at[sl, :], hid_far.at[sl, lanes]), (slope.at[sl, :], slope_far.at[sl, lanes])]
        pair = [p[::-1] if back else p for p in pair]
        return [
            pltpu.make_async_copy(*p, sem.at[t]) for p, sem in zip(pair, (hid_sem, slope_sem))
        ]

    others = [p["tensor"] for p in across]

    def res_chunk(j):
        lanes = pl.ds(pl.multiple_of(j * STEP, LANES), STEP)
        pairs = [(t, res) for t in others] + [(me, res_own)]
        return [
            pltpu.make_async_copy(res_near.at[t], ref.at[t, :, lanes], res_sem.at[i])
            for i, (t, ref) in enumerate(pairs)
        ]

    def low_of(off):
        normed, scale = norm(mixed[:, :, pl.ds(off, STEP)].reshape(width, STEP).astype(F32))
        return normed, scale, (normed * chan[:, 0:1] + chan[:, 1:2]).astype(BF16)

    @pl.loop(0, chunks)
    def _(j):
        off = pl.multiple_of(j * STEP, LANES)
        _, _, low = low_of(off)
        for t in range(parts):
            sl = pl.ds(t * shard, shard)
            pre = nn(win_t[sl, :], low) + bin_col[sl, 0:1]
            square_pre = pre * pre
            th = jnp.tanh(pre * (GELU_C + (GELU_C * GELU_A) * square_pre))
            half = 0.5 * th + 0.5
            inner_slope = GELU_C + (3 * GELU_C * GELU_A) * square_pre

            @pl.when(j > 0)
            def _():
                for copy in hid_copy(t, j, False):
                    copy.wait()

            hid[sl, :] = (pre * half).astype(BF16)
            slope[sl, :] = (half + pre * (0.5 - 0.5 * th * th) * inner_slope).astype(BF16)
            for copy in hid_copy(t, j, False):
                copy.start()
        branch = nn(wout_t[...], hid[...]) + chan[:, 2:3]
        source = x_all[:, :, pl.ds(off, STEP)].reshape(width, STEP).astype(F32)
        out = (source + chan[:, 3:4] * branch).astype(BF16)

        @pl.when(j > 0)
        def _():
            for copy in res_chunk(j):
                copy.wait()

        res_near[...] = out.reshape(parts, local, STEP)
        for copy in res_chunk(j):
            copy.start()

    for t in range(parts):
        for copy in hid_copy(t, 0, False):
            copy.wait()
        for copy in hid_copy(t, 0, True):
            copy.start()

    for copy in res_chunk(0):
        copy.wait()

    arrived(go_copies)
    res_copies = [remote(res.at[p["tensor"]], res_own.at[me], p) for p in across]

    for ref in (dw, bin_acc, vec):
        ref[...] = jnp.zeros_like(ref)

    def go_chunk(j):
        off = pl.multiple_of(j * STEP, LANES)
        mine_at = pl.ds(pl.multiple_of(me * pix + off, LANES), STEP)
        sources = [(t, go_all.at[t, :, pl.ds(off, STEP)]) for t in others] + [(me, go.at[:, mine_at])]
        return [
            pltpu.make_async_copy(src, go_near.at[t], go_sem.at[i])
            for i, (t, src) in enumerate(sources)
        ]

    for copy in go_chunk(0):
        copy.start()

    @pl.loop(0, chunks)
    def _(j):
        off = pl.multiple_of(j * STEP, LANES)
        for copy in go_chunk(j):
            copy.wait()
        grad = go_near[...].reshape(width, STEP).astype(F32)
        gb = (grad * chan[:, 3:4]).astype(BF16)
        vec[0] += fold(gb.astype(F32))
        vec[3] += fold(grad)

        @pl.when(j + 1 < chunks)
        def _():
            for copy in go_chunk(j + 1):
                copy.start()

        normed, scale, low = low_of(off)
        for t in range(parts):
            sl = pl.ds(t * shard, shard)
            for copy in hid_copy(t, j, True):
                copy.wait()
            tile = (nn(wout[t], gb) * slope[sl, :].astype(F32)).astype(BF16)
            gp[sl, :] = tile
            bin_acc[sl, :] += fold(tile.astype(F32))
            dw[0, t] += nt(hid[sl, :], gb)
            dw[1, t] += nt(tile, low)

            @pl.when(j + 1 < chunks)
            def _():
                for copy in hid_copy(t, j + 1, True):
                    copy.start()

        gn = nn(win[...], gp[...])
        vec[1] += fold(gn * normed)
        vec[2] += fold(gn)
        g1 = gn * chan[:, 0:1]
        m1 = jnp.mean(g1, axis=0, keepdims=True)
        m2 = jnp.mean(g1 * normed, axis=0, keepdims=True)
        gm = (scale * (g1 - m1 - normed * m2)).reshape(parts, local, STEP)
        for q in range(local // GROUP):
            block = gm[:, q * GROUP : (q + 1) * GROUP, :].reshape(LANES, STEP)
            grow[q, pl.ds(off, STEP), :] = jnp.transpose(block)

    def slab_of(peer):
        return pl.ds(pl.multiple_of((peer["dp"] - first) * slab, slab), slab)

    dw_near = near(dw.at[:, :, my_slab, :], dw_peer.at[:, :, my_slab, :])
    dw_copies = [
        remote(dw.at[:, :, slab_of(p), :], dw_peer.at[:, :, my_slab, :], p) for p in beside
    ]

    back = [near(go_all.at[t], mixed.at[t]) for t in others]
    back.append(near(pixels(go, me), mixed.at[me]))
    for copy in back:
        copy.wait()

    def gx_tile(q):
        return pl.ds(pl.multiple_of(q * GROUP, GROUP), GROUP)

    def gx_copies(q):
        at = gx_tile(q)
        return [
            pltpu.make_async_remote_copy(
                src_ref=mixed.at[p["tensor"], at, :],
                dst_ref=g_own.at[me, at, :],
                send_sem=gx_send.at[q, s],
                recv_sem=gx_recv.at[q, s],
                device_id=p,
                device_id_type=MESH,
            )
            for s, p in enumerate(across)
        ] + [pltpu.make_async_copy(mixed.at[me, at, :], g_own.at[me, at, :], gx_own.at[q])]

    @pl.loop(0, local // GROUP)
    def _(q):
        mix_bwd(q, x_all, rows, grow, kern, mask, inner, mid, mixed, gkern)

        @pl.when(q == 0)
        def _():
            for copy in gx_copies(q):
                copy.start()

    for t in range(parts):
        lanes = slice(t * GROUP, (t + 1) * GROUP)
        pack_mine[t] = jnp.zeros(pack_mine.shape[1:], F32)
        pack_mine[t, 0:32, 0:local] = jnp.concatenate(
            [gkern[q, 0:32, lanes] for q in range(local // GROUP)], axis=1
        )
    acc = jnp.zeros((width, LANES), F32)
    sums = [jnp.sum(vec[k], axis=1, keepdims=True) for k in range(4)]
    for k in range(3):
        acc = column_set(acc, k, sums[k])
    square[0:1, :] = sum(
        jnp.sum(wout[t].astype(F32) * dw[0, t], axis=0, keepdims=True) for t in range(parts)
    )
    products = jnp.concatenate(
        [
            jnp.transpose(square[:, i * LANES : (i + 1) * LANES])[:, 0:1]
            for i in range(width // LANES)
        ]
    )
    acc = column_set(acc, 3, products / chan[:, 3:4] + chan[:, 2:3] * sums[3])
    hidden_sums = jnp.sum(bin_acc[...], axis=1, keepdims=True)
    for k in range(shard // local):
        starts = [t * shard + k * local for t in range(parts)]
        acc = column_set(acc, 4 + k, jnp.concatenate([hidden_sums[i : i + local] for i in starts]))
    for t in range(parts):
        square[0:local, 0:LANES] = acc[t * local : (t + 1) * local]
        pack_mine[t, 32:40, :] = jnp.transpose(square[:, 0:LANES])[0:8]
    pack_peer[mine] = pack_mine[...]
    pack_copies = [remote(pack_mine, pack_peer.at[mine], p) for p in beside]

    dw_near.wait()
    for copy in dw_copies:
        copy.wait()
    near(dw_peer, dw).wait()
    terms = [dw[:, :, i * slab : (i + 1) * slab, :] for i in range(groups)]
    dw_sum[...] = sum(terms[1:], terms[0])
    dw_low[...] = dw_sum[...].astype(BF16)

    def leg(kind, way, src, slot, peer):
        return pltpu.make_async_remote_copy(
            src_ref=src,
            dst_ref=(dw_tensor, pack_tensor)[kind].at[slot],
            send_sem=leg_send.at[kind, way],
            recv_sem=leg_recv.at[kind, slot],
            device_id=peer,
            device_id_type=MESH,
        )

    def term(kind, t):
        return pack_sum.at[t] if kind else dw_low.at[:, t]

    def to_partner(kind):
        return leg(kind, 0, term(kind, partner["tensor"]), 0, partner)

    def to_inner(kind, k):
        return leg(kind, 1 + k, term(kind, other_half + k), 2 + k, partner)

    def crossing(kind, k):
        src = (dw_pass, pack_pass)[kind].at[k]
        return leg(kind, 3 + k, src, 1, {"tensor": other_half + k})

    def start_leg(kind):
        to_partner(kind).start()

        @pl.when(jnp.logical_not(is_inner))
        def _():
            for k in range(2):
                to_inner(kind, k).start()

    start_leg(0)
    arrived(pack_copies)
    pack_sum[...] = sum((pack_peer[i] for i in range(1, groups)), pack_peer[0])
    start_leg(1)
    for copy in gx_copies(1):
        copy.start()

    @pl.when(is_inner)
    def _():
        for kind in range(2):
            for k in range(2):
                to_inner(kind, k).wait_recv()
        for k in range(2):
            dw_pass[k] = (dw_sum[:, other_half + k] + dw_tensor[2 + k].astype(F32)).astype(BF16)
            pack_pass[k] = pack_sum[other_half + k] + pack_tensor[2 + k]
        for kind in range(2):
            for k in range(2):
                crossing(kind, k).start()

    for q in range(2, local // GROUP):
        for copy in gx_copies(q):
            copy.start()

    def received(kind):
        to_partner(kind).wait_recv()
        crossing(kind, 0).wait_recv()

    received(0)
    dw_done[...] = dw_sum[:, me] + dw_tensor[0].astype(F32) + dw_tensor[1].astype(F32)
    dw_near = near(dw_done, dw_own.at[:, my_slab, :])
    dw_copies = [remote(dw_done, dw_own.at[:, my_slab, :], p) for p in beside]
    received(1)
    total = pack_sum[me] + pack_tensor[0] + pack_tensor[1]
    gdt = lag_grads(total, steps, a_log, a_imag, coefs, g_alog, g_aimag, [g_height, g_width])
    row_own[...] = total
    for j in range(2):
        row_own[29 + j : 30 + j, 0:local] = gdt[j]

    arrived(dw_copies)
    dw_near.wait()
    arrived(res_copies)

    @pl.loop(0, local // GROUP)
    def _(q):
        for copy in gx_copies(q):
            copy.wait()

    for copy in sent + first_hops:
        copy.wait_send()

    for kind in range(2):
        to_partner(kind).wait_send()

    @pl.when(is_inner)
    def _():
        for k in range(2):
            for copy in handed_on(k):
                copy.wait_send()
            for kind in range(2):
                crossing(kind, k).wait_send()

    @pl.when(jnp.logical_not(is_inner))
    def _():
        for k in range(2):
            for kind in range(2):
                to_inner(kind, k).wait_send()


def block(parts, groups, args):
    x, size = args[0], args[2]
    local, pixels = x.shape
    pix = pixels // parts
    width = local * parts
    w_in = args[12]
    shard = w_in.shape[1]
    ff = shard * parts
    slab = shard // groups
    tiles = local // GROUP
    states = args[4].shape[0]
    shape = jax.ShapeDtypeStruct
    vmem = pl.BlockSpec(memory_space=pltpu.VMEM)
    hbm = pl.BlockSpec(memory_space=pl.ANY)
    in_specs = [hbm, hbm] + [vmem] * 10 + [hbm, vmem, hbm, vmem, vmem]
    outs = [
        (shape((parts, local, pix), BF16), hbm),
        (shape((parts, local, pix), BF16), hbm),
        (shape((2, shard, width), F32), hbm),
        (shape((states, local), F32), vmem),
        (shape((states, local), F32), vmem),
        (shape((2, states, local), F32), vmem),
        (shape((2, states, local), F32), vmem),
        (shape((40, LANES), F32), vmem),
        (shape((parts, local, pix), BF16), hbm),
        (shape((ff, pix), BF16), hbm),
        (shape((ff, pix), BF16), hbm),
        (shape((parts, local, pix), BF16), hbm),
        (shape((2, parts, shard, width), F32), hbm),
    ]
    remotes = 4 * (parts - 1) + 5 * (groups - 1)
    dma = pltpu.SemaphoreType.DMA
    scratch = [
        pltpu.VMEM((parts, local, pix), BF16),
        pltpu.VMEM((parts, local, pix), BF16),
        pltpu.VMEM((parts, local, STEP), BF16),
        pltpu.VMEM((pix, LANES), F32),
        pltpu.VMEM((tiles, pix, LANES), F32),
        pltpu.VMEM((CROP, CROP, 8, LANES), F32),
        pltpu.VMEM((CROP, CROP, 8, LANES), F32),
        pltpu.VMEM((4, 2 * CROP, 8, LANES), F32),
        pltpu.VMEM((40, LANES), F32),
        pltpu.VMEM((parts, 40, LANES), F32),
        pltpu.VMEM((tiles, 32, LANES), F32),
        pltpu.VMEM((tiles, 32, LANES), F32),
        pltpu.VMEM((ff, LANES), F32),
        pltpu.VMEM((width, LANES), F32),
        pltpu.VMEM((LANES, width), F32),
        pltpu.VMEM((LANES, LANES), F32),
        pltpu.VMEM((width, ff), BF16),
        pltpu.VMEM((ff, width), BF16),
        pltpu.VMEM((parts, shard, width), BF16),
        pltpu.VMEM((width, ff), BF16),
        pltpu.VMEM((ff, STEP), BF16),
        pltpu.VMEM((ff, STEP), BF16),
        pltpu.VMEM((ff, STEP), BF16),
        pltpu.VMEM((parts, local, STEP), BF16),
        pltpu.VMEM((2, parts, shard, width), F32),
        pltpu.VMEM((2, parts, slab, width), F32),
        pltpu.VMEM((2, parts, slab, width), BF16),
        pltpu.VMEM((4, 2, slab, width), BF16),
        pltpu.VMEM((2, 2, slab, width), BF16),
        pltpu.VMEM((2, slab, width), F32),
        pltpu.VMEM((ff, LANES), F32),
        pltpu.VMEM((4, width, LANES), F32),
        pltpu.VMEM((parts, 40, LANES), F32),
        pltpu.VMEM((groups, parts, 40, LANES), F32),
        pltpu.VMEM((parts, 40, LANES), F32),
        pltpu.VMEM((4, 40, LANES), F32),
        pltpu.VMEM((2, 40, LANES), F32),
        dma((remotes,)),
        dma((remotes,)),
        dma((10,)),
        dma((4, 3)),
        dma((3, 3)),
        dma((2, 5)),
        dma((2, 4)),
        dma((parts,)),
        dma((parts,)),
        dma((parts,)),
        dma((parts,)),
        dma((tiles, parts - 1)),
        dma((tiles, parts - 1)),
        dma((tiles,)),
    ]
    return pl.pallas_call(
        functools.partial(block_kernel, parts, groups),
        out_shape=[o[0] for o in outs],
        in_specs=in_specs,
        out_specs=[o[1] for o in outs],
        scratch_shapes=scratch,
        compiler_params=pltpu.CompilerParams(
            collective_id=0, has_side_effects=True, vmem_limit_bytes=VMEM
        ),
        name="block",
    )(*args)


def finish_kernel(parts, n_sums, *refs):
    sums, refs = refs[:n_sums], refs[n_sums:]
    res_ref, g_ref, result_ref, grad_ref = refs[:4]
    n_small = (len(refs) - 11 - n_sums) // 2
    smalls, refs = refs[4 : 4 + n_small], refs[4 + n_small :]
    res_near, g_near, grad_near = refs[:3]
    sums_near = refs[3 : 3 + n_sums]
    near = refs[3 + n_sums : 3 + n_sums + n_small]
    came, left, sums_came, smalls_left = refs[3 + n_sums + n_small :]
    pix = g_near.shape[2]
    in_copies, out_copies = [], []
    for i, (a, b) in enumerate(((g_ref, g_near), (res_ref, res_near))):
        for s in range(parts):
            in_copies.append(pltpu.make_async_copy(a.at[s], b.at[s], came.at[i, s]))
            in_copies[-1].start()
        if i == 0:
            small_in = [
                pltpu.make_async_copy(sums[k], sums_near[k], sums_came.at[k]) for k in range(n_sums)
            ]
            for copy in small_in:
                copy.start()

    def put(src, dst, sem):
        out_copies.append(pltpu.make_async_copy(src, dst, sem))
        out_copies[-1].start()

    for s in range(parts):
        in_copies[s].wait()
        grad_near[s] = g_near[s].astype(F32)
        put(grad_near.at[s], grad_ref.at[:, pl.ds(s * pix, pix)], left.at[0, s])
        if s == 0:
            for copy in small_in:
                copy.wait()
            dw, g_alog, g_aimag, g_height, g_width, rows = sums_near
            alog, aimag, height, width, dt, skip, gain, bias, win, bin_, wout, bout, scale = near
            for out, ref in ((alog, g_alog), (aimag, g_aimag), (height, g_height), (width, g_width)):
                out[...] = ref[...]
            local = skip.shape[0]
            dt[...] = rows[29:31, 0:local]
            for out, k in ((skip, 28), (gain, 33), (bias, 34), (bout, 32), (scale, 35)):
                out[...] = rows[k : k + 1, 0:local].reshape(local)
            bin_[...] = jnp.concatenate(
                [rows[36 + k : 37 + k, 0:local] for k in range(bin_.shape[0] // local)], axis=1
            ).reshape(bin_.shape)
            win[...] = jnp.transpose(dw[1])
            wout[...] = dw[0]
            for k in range(n_small):
                put(near[k], smalls[k], smalls_left.at[k])
    for s in range(parts):
        in_copies[parts + s].wait()
        put(res_near.at[s], result_ref.at[:, pl.ds(s * pix, pix)], left.at[1, s])
    for copy in out_copies:
        copy.wait()


def finish(res_own, g_own, sums):
    parts, local, pix = g_own.shape
    dw, g_alog, _, g_height, _, _ = sums
    hbm = pl.BlockSpec(memory_space=pl.ANY)
    dma = pltpu.SemaphoreType.DMA
    shape = jax.ShapeDtypeStruct
    line = (local,)
    small = (
        g_alog.shape,
        g_alog.shape,
        g_height.shape,
        g_height.shape,
        (2, local),
        line,
        line,
        line,
        (dw.shape[2], dw.shape[1]),
        (dw.shape[1],),
        dw.shape[1:],
        line,
        line,
    )
    return pl.pallas_call(
        functools.partial(finish_kernel, parts, len(sums)),
        out_shape=(shape((local, parts * pix), BF16), shape((local, parts * pix), F32))
        + tuple(shape(a, F32) for a in small),
        in_specs=[hbm] * (2 + len(sums)),
        out_specs=(hbm,) * (2 + len(small)),
        scratch_shapes=[
            pltpu.VMEM(g_own.shape, BF16),
            pltpu.VMEM(g_own.shape, BF16),
            pltpu.VMEM(g_own.shape, F32),
        ]
        + [pltpu.VMEM(a.shape, F32) for a in sums]
        + [pltpu.VMEM(a, F32) for a in small]
        + [dma((2, parts)), dma((2, parts)), dma((len(sums),)), dma((len(small),))],
        compiler_params=pltpu.CompilerParams(vmem_limit_bytes=VMEM),
        name="finish",
    )(*sums, res_own, g_own)


def per_device(
    parts,
    dp_size,
    inputs,
    crop_size,
    crop_offset,
    a_log,
    a_imag,
    c_height,
    c_width,
    log_dt,
    skip_gain,
    ln_gain,
    ln_bias,
    w_in,
    b_in,
    w_out,
    b_out,
    layer_scale,
    grad_out,
):
    canvases = crop_size.shape[0]
    groups = min(dp_size, 8)
    args = (
        inputs,
        grad_out,
        jnp.transpose(crop_size.reshape(canvases, 8)),
        jnp.transpose(crop_offset.reshape(canvases, 8)),
        jnp.transpose(a_log),
        jnp.transpose(a_imag),
        jnp.transpose(c_height, (0, 2, 1)),
        jnp.transpose(c_width, (0, 2, 1)),
        log_dt,
        skip_gain,
        ln_gain,
        ln_bias,
        w_in,
        b_in,
        w_out,
        b_out,
        layer_scale,
    )
    out = block(parts, groups, args)
    sums = tuple(out[2:8])
    if dp_size > groups:
        teams = [[r + groups * g for g in range(dp_size // groups)] for r in range(groups)]
        sums = lax.psum(sums, "dp", axis_index_groups=teams)
    done = finish(out[0], out[1], sums)
    return (
        done[0],
        done[1],
        jnp.transpose(done[2]),
        jnp.transpose(done[3]),
        jnp.transpose(done[4], (0, 2, 1)),
        jnp.transpose(done[5], (0, 2, 1)),
        *done[6:],
    )


def solution(mesh):
    in_specs = (
        P("tensor", "dp"),
        P("dp", None, None),
        P("dp", None, None),
        P("tensor", None),
        P("tensor", None),
        P(None, "tensor", None),
        P(None, "tensor", None),
        P(None, "tensor"),
        P("tensor"),
        P(),
        P(),
        P(None, "tensor"),
        P("tensor"),
        P("tensor", None),
        P(),
        P(),
        P("tensor", "dp"),
    )
    out_specs = (
        P("tensor", "dp"),
        P("tensor", "dp"),
        P("tensor", None),
        P("tensor", None),
        P(None, "tensor", None),
        P(None, "tensor", None),
        P(None, "tensor"),
        P("tensor"),
        P("tensor"),
        P("tensor"),
        P(None, "tensor"),
        P("tensor"),
        P("tensor", None),
        P("tensor"),
        P("tensor"),
    )
    return jax.shard_map(
        functools.partial(per_device, mesh.shape["tensor"], mesh.shape["dp"]),
        mesh=mesh,
        in_specs=in_specs,
        out_specs=out_specs,
        check_vma=False,
    )
```

```python
import functools

import jax
import jax.numpy as jnp
from jax import lax
from jax.experimental import pallas as pl
from jax.experimental.pallas import tpu as pltpu
from jax.sharding import PartitionSpec as P

F32, BF16 = jnp.float32, jnp.bfloat16
CROP = 14
SIDE = 2 * CROP
NPIX = SIDE * SIDE
LANES = 128
GROUP = 32
STEP = 896
EPS = 1e-06
GELU_C = 0.7978845608028654
GELU_A = 0.044715
VMEM = 53 << 20
MESH = pl.DeviceIdType.MESH


def nn(a, b):
    return lax.dot_general(a, b, (((1,), (0,)), ((), ())), preferred_element_type=F32)


def nt(a, b):
    return lax.dot_general(a, b, (((1,), (1,)), ((), ())), preferred_element_type=F32)


def conv(y, taps):
    return [sum((taps[l] * y[i - l] for l in range(1, i + 1)), taps[0] * y[i]) for i in range(CROP)]


def conv_back(y, taps):
    return [
        sum((taps[l] * y[i + l] for l in range(1, CROP - i)), taps[0] * y[i]) for i in range(CROP)
    ]


def spot(slot, h, w):
    first = (slot // 2) * (CROP * SIDE) + (slot % 2) * CROP
    return pl.ds(first + h * SIDE + w, 8, stride=NPIX)


def lanes_to_rows(load, rows):
    @pl.loop(0, rows.shape[0] // STEP)
    def _(j):
        off = pl.multiple_of(j * STEP, LANES)
        rows[pl.ds(off, STEP), :] = jnp.transpose(load(off).astype(F32))


def rows_to_lanes(rows, store):
    @pl.loop(0, rows.shape[0] // STEP)
    def _(j):
        off = pl.multiple_of(j * STEP, LANES)
        store(off, jnp.transpose(rows[pl.ds(off, STEP), :]).astype(BF16))


def tap_rows(kern, q, base):
    return [jnp.broadcast_to(kern[q, pl.ds(base + l, 1), :], (8, LANES)) for l in range(CROP)]


def tile_of(ref, q, off):
    return ref[:, pl.ds(pl.multiple_of(q * GROUP, GROUP), GROUP), pl.ds(off, STEP)].reshape(
        LANES, STEP
    )


def put_tile(ref, q, off, v):
    ref[:, pl.ds(pl.multiple_of(q * GROUP, GROUP), GROUP), pl.ds(off, STEP)] = v.reshape(
        ref.shape[0], GROUP, STEP
    )


def along_width(q, slot, rows, kern, mask, inner):
    @pl.loop(0, CROP)
    def _(h):
        taps = tap_rows(kern, q, CROP)
        row_in = mask[slot, h]
        y = [rows[spot(slot, h, w), :] * mask[slot, CROP + w] for w in range(CROP)]
        for w, v in enumerate(conv(y, taps)):
            inner[h, w] = v * row_in


def mix_fwd(q, x_all, rows, kern, mask, inner, mixed):
    lanes_to_rows(lambda off: tile_of(x_all, q, off), rows)
    skip = jnp.broadcast_to(kern[q, pl.ds(2 * CROP, 1), :], (8, LANES))

    @pl.loop(0, 4)
    def _(slot):
        along_width(q, slot, rows, kern, mask, inner)

        @pl.loop(0, CROP)
        def _(w):
            taps = tap_rows(kern, q, 0)
            col_in = mask[slot, CROP + w]
            y = [inner[h, w] for h in range(CROP)]
            for h, v in enumerate(conv(y, taps)):
                at = spot(slot, h, w)
                rows[at, :] = v * (mask[slot, h] * col_in) + skip * rows[at, :]

    rows_to_lanes(rows, lambda off, v: put_tile(mixed, q, off, v))


def mix_bwd(q, x_all, rows, grow, kern, mask, inner, mid, out, gkern):
    lanes_to_rows(lambda off: tile_of(x_all, q, off), rows)
    skip = jnp.broadcast_to(kern[q, pl.ds(2 * CROP, 1), :], (8, LANES))
    zero = jnp.zeros((8, LANES), F32)

    def per_slot(slot, sums):
        gk_height, gk_width, gskip = sums
        along_width(q, slot, rows, kern, mask, inner)

        def down(w, acc):
            taps = tap_rows(kern, q, 0)
            col_in = mask[slot, CROP + w]
            u = [grow[q, spot(slot, h, w), :] * (mask[slot, h] * col_in) for h in range(CROP)]
            for h, v in enumerate(conv_back(u, taps)):
                mid[h, w] = v * mask[slot, h]
            a = [inner[h, w] for h in range(CROP)]
            return tuple(
                sum((u[h] * a[h - l] for h in range(l, CROP)), acc[l]) for l in range(CROP)
            )

        gk_height = lax.fori_loop(0, CROP, down, gk_height)

        def across(h, acc):
            gk_width, gskip = acc
            taps = tap_rows(kern, q, CROP)
            u = [mid[h, w] for w in range(CROP)]
            x = [rows[spot(slot, h, w), :] for w in range(CROP)]
            y = [x[w] * mask[slot, CROP + w] for w in range(CROP)]
            gk_width = tuple(
                sum((u[w] * y[w - l] for w in range(l, CROP)), gk_width[l]) for l in range(CROP)
            )
            for w, v in enumerate(conv_back(u, taps)):
                at = spot(slot, h, w)
                g = grow[q, at, :]
                gskip = gskip + g * x[w]
                grow[q, at, :] = v * mask[slot, CROP + w] + skip * g
            return gk_width, gskip

        gk_width, gskip = lax.fori_loop(0, CROP, across, (gk_width, gskip))
        return gk_height, gk_width, gskip

    gk_height, gk_width, gskip = lax.fori_loop(
        0, 4, per_slot, ((zero,) * CROP, (zero,) * CROP, zero)
    )
    gkern[q] = jnp.zeros((32, LANES), F32)
    for row, v in enumerate((*gk_height, *gk_width, gskip)):
        gkern[q, pl.ds(row, 1), :] = jnp.sum(v, axis=0, keepdims=True)

    @pl.loop(0, rows.shape[0] // STEP)
    def _(j):
        off = pl.multiple_of(j * STEP, LANES)
        turned = jnp.transpose(grow[q, pl.ds(off, STEP), :])
        put_tile(out, q, off, (tile_of(out, q, off).astype(F32) + turned).astype(BF16))


def lag_waves(step, a_log, a_imag):
    rate = -step * jnp.exp(a_log)
    phase = step * a_imag
    size = jnp.exp(rate)
    re1, im1 = size * jnp.cos(phase), size * jnp.sin(phase)
    re, im = jnp.ones_like(re1), jnp.zeros_like(im1)
    out = []
    for _ in range(CROP):
        out.append((re, im))
        re, im = re * re1 - im * im1, re * im1 + im * re1
    return rate, phase, out


def column_set(acc, k, col):
    lane = lax.broadcasted_iota(jnp.int32, acc.shape, 1)
    return jnp.where(lane == k, col, acc)


def lag_kernels(steps, a_log, a_imag, coefs, out):
    local = a_log.shape[1]
    for j in range(2):
        _, _, waves = lag_waves(steps[j], a_log[...], a_imag[...])
        for l, (re, im) in enumerate(waves):
            row = jnp.sum(coefs[j][0] * re - coefs[j][1] * im, axis=0, keepdims=True)
            out[CROP * j + l : CROP * j + l + 1, 0:local] = row


def lag_grads(rows, steps, a_log, a_imag, coefs, g_alog, g_aimag, g_coefs):
    ga, gi, gdt = 0.0, 0.0, []
    for j in range(2):
        rate, phase, waves = lag_waves(steps[j], a_log[...], a_imag[...])
        cre, cim = coefs[j][0], coefs[j][1]
        g_re = g_im = p = r = 0.0
        for l, (re, im) in enumerate(waves):
            g = rows[CROP * j + l : CROP * j + l + 1, 0 : a_log.shape[1]]
            g_re = g_re + g * re
            g_im = g_im - g * im
            if l:
                p = p + (l * g) * (cre * re - cim * im)
                r = r - (l * g) * (cre * im + cim * re)
        g_coefs[j][0] = g_re
        g_coefs[j][1] = g_im
        ga = ga + p * rate
        gi = gi + r * steps[j]
        gdt.append(jnp.sum(p * rate + r * phase, axis=0, keepdims=True))
    g_alog[...] = ga
    g_aimag[...] = gi
    return gdt


def norm(m):
    centered = m - jnp.mean(m, axis=0, keepdims=True)
    scale = lax.rsqrt(jnp.mean(centered * centered, axis=0, keepdims=True) + EPS)
    return centered * scale, scale


def fold(v):
    return sum(
        (v[:, i * LANES : (i + 1) * LANES] for i in range(1, v.shape[1] // LANES)), v[:, :LANES]
    )


def block_kernel(
    parts,
    groups,
    x,
    go,
    size_ref,
    offset_ref,
    a_log,
    a_imag,
    c_height,
    c_width,
    log_dt,
    skip_gain,
    ln_gain,
    ln_bias,
    w_in,
    b_in,
    w_out,
    b_out,
    layer_scale,
    res_own,
    g_own,
    dw_own,
    g_alog,
    g_aimag,
    g_height,
    g_width,
    row_own,
    go_all,
    hid_far,
    slope_far,
    res,
    dw_peer,
    x_all,
    mixed,
    rows,
    grow,
    inner,
    mid,
    mask,
    small_mine,
    small_all,
    kern,
    gkern,
    bin_col,
    chan,
    square,
    turned,
    win,
    wout,
    wout_t,
    hid,
    slope,
    gp,
    chunk_near,
    dw,
    dw_sum,
    dw_low,
    dw_tensor,
    dw_pass,
    dw_done,
    bin_acc,
    vec,
    pack_mine,
    pack_peer,
    pack_sum,
    pack_tensor,
    pack_pass,
    send,
    recv,
    own,
    hop_send,
    hop_recv,
    leg_send,
    leg_recv,
    hid_sem,
    slope_sem,
    go_sem,
    res_sem,
    gx_send,
    gx_recv,
    gx_own,
):
    local, pix = x_all.shape[1], x_all.shape[2]
    width = local * parts
    ff = gp.shape[0]
    win_t = gp.at[:, 0:width]
    shard = ff // parts
    slab = shard // groups
    chunks = pix // STEP
    me = lax.axis_index("tensor")
    dp = lax.axis_index("dp")
    mine = lax.rem(dp, groups)
    first = dp - mine
    across = [{"tensor": lax.rem(me + s, parts)} for s in range(1, parts)]
    beside = [{"dp": first + lax.rem(mine + s, groups)} for s in range(1, groups)]

    barrier = pltpu.get_barrier_semaphore()
    for peer in across + beside:
        pl.semaphore_signal(barrier, inc=1, device_id=peer, device_id_type=MESH)
    pl.semaphore_wait(barrier, len(across) + len(beside))

    count = [0, 0]

    def remote(src, dst, peer, sems=None):
        if sems is None:
            sems = (send.at[count[0]], recv.at[count[0]])
            count[0] += 1
        copy = pltpu.make_async_remote_copy(
            src_ref=src,
            dst_ref=dst,
            send_sem=sems[0],
            recv_sem=sems[1],
            device_id=peer,
            device_id_type=MESH,
        )
        copy.start()
        return copy

    def near(src, dst, sem=None):
        if sem is None:
            sem = own.at[count[1]]
            count[1] += 1
        copy = pltpu.make_async_copy(src, dst, sem)
        copy.start()
        return copy

    sent = []

    def arrived(copies):
        for copy in copies:
            copy.wait_recv()
        sent.extend(copies)

    def pixels(ref, peer):
        return ref.at[:, pl.ds(pl.multiple_of(peer * pix, LANES), pix)]

    def to_owner(ref, out):
        return [remote(pixels(ref, p["tensor"]), out.at[me], p) for p in across]

    my_slab = pl.ds(pl.multiple_of(mine * slab, slab), slab)
    steps = [jnp.exp(log_dt[j : j + 1, :]) for j in range(2)]
    coefs = [c_height, c_width]

    partner = {"tensor": me + 1 - 2 * lax.rem(me, 2)}
    inner_device = {"tensor": jnp.where(me < 2, 2, 1)}
    is_inner = (me == 1) | (me == 2)
    other_half = 2 - 2 * (me // 2)

    def cols_of(t):
        return pl.ds(pl.multiple_of(t * shard, LANES), shard)

    def pieces(t):
        return [
            (win.at[my_slab, cols_of(t)], win.at[my_slab, cols_of(t)]),
            (wout.at[t, my_slab, :], wout.at[t, my_slab, :]),
            (small_all.at[t], small_all.at[t]),
        ]

    def hop(i, k, pair, peer, way):
        return pltpu.make_async_remote_copy(
            src_ref=pair[0],
            dst_ref=pair[1],
            send_sem=hop_send.at[way, i],
            recv_sem=hop_recv.at[k, i],
            device_id=peer,
            device_id_type=MESH,
        )

    first_hops = []
    slabs = [w_in.at[my_slab, :], w_out.at[my_slab, :], small_mine]
    for i in range(3):
        if i == 2:
            small_mine[...] = jnp.zeros_like(small_mine)
            lag_kernels(steps, a_log, a_imag, coefs, small_mine)
            small_mine[2 * CROP : 2 * CROP + 1, 0:local] = skip_gain[...].reshape(1, local)
            biases = b_in[...].reshape(1, shard)
            for j in range(shard // LANES):
                small_mine[32 + j : 33 + j, :] = biases[:, j * LANES : (j + 1) * LANES]
        pair = (slabs[i], pieces(me)[i][1])
        first_hops.append(hop(i, 0, pair, partner, 0))
        first_hops.append(hop(i, 1 + lax.rem(me, 2), pair, inner_device, 1))
        for copy in first_hops[-2:]:
            copy.start()
    w_near = [near(slabs[i], pieces(me)[i][1]) for i in range(2)]
    small_all[me] = small_mine[...]

    def handed_on(k):
        found = pieces(other_half + k)
        return [hop(i, 1 + k, found[i], partner, 2 + k) for i in range(3)]

    @pl.when(is_inner)
    def _():
        for k in range(2):
            for copy in handed_on(k):
                copy.wait_recv()
            for copy in handed_on(k):
                copy.start()

    x_copies = to_owner(x, x_all)
    x_near = near(pixels(x, me), x_all.at[me])

    @pl.when(jnp.logical_not(is_inner))
    def _():
        for k in range(2):
            for copy in handed_on(k):
                copy.wait_recv()

    for copy in w_near:
        copy.wait()
    for copy in first_hops[::2]:
        copy.wait_recv()
    w_copies = [remote(win.at[my_slab, :], win.at[my_slab, :], p) for p in beside]
    w_copies += [remote(wout.at[:, my_slab, :], wout.at[:, my_slab, :], p) for p in beside]

    square[...] = jnp.zeros_like(square)
    for row, ref in enumerate((ln_gain, ln_bias, b_out, layer_scale)):
        square[row : row + 1, :] = ref[...].reshape(1, width)
    for i in range(width // LANES):
        chan[i * LANES : (i + 1) * LANES, :] = jnp.transpose(square[:, i * LANES : (i + 1) * LANES])
    canvases = size_ref.shape[1]
    square[0:8, 0:canvases] = offset_ref[...].astype(F32)
    square[8:16, 0:canvases] = size_ref[...].astype(F32)
    turned[...] = jnp.transpose(square[:, 0:LANES])
    at = pl.ds(pl.multiple_of(me * 8, 8), 8)
    for slot in range(4):
        for j in range(2):
            k = 2 * slot + j
            low = jnp.broadcast_to(turned[at, k : k + 1], (8, LANES))
            high = low + jnp.broadcast_to(turned[at, 8 + k : 9 + k], (8, LANES))
            for s in range(CROP):
                mask[slot, CROP * j + s] = jnp.where((low <= s) & (s < high), 1.0, 0.0)
    for q in range(local // GROUP):
        kern[q] = jnp.concatenate(
            [small_all[t, 0:32, q * GROUP : (q + 1) * GROUP] for t in range(parts)], axis=1
        )
    for t in range(parts):
        for i in range(shard // LANES):
            block = jnp.broadcast_to(small_all[t, 32 + i : 33 + i, :], (LANES, LANES))
            bin_col[t * shard + i * LANES : t * shard + (i + 1) * LANES, :] = jnp.transpose(block)
    arrived(w_copies)
    for t in range(parts):
        cols = slice(t * shard, (t + 1) * shard)
        win_t[cols, :] = jnp.transpose(win[:, cols].astype(F32)).astype(BF16)
        wout_t[:, cols] = jnp.transpose(wout[t].astype(F32)).astype(BF16)

    arrived(x_copies)
    x_near.wait()
    go_copies = to_owner(go, go_all)

    @pl.loop(0, local // GROUP)
    def _(q):
        mix_fwd(q, x_all, rows, kern, mask, inner, mixed)

    def hid_copy(t, j, back):
        sl = pl.ds(t * shard, shard)
        lanes = pl.ds(pl.multiple_of(j * STEP, LANES), STEP)
        pair = [(hid.at[sl, :], hid_far.at[sl, lanes]), (slope.at[sl, :], slope_far.at[sl, lanes])]
        pair = [p[::-1] if back else p for p in pair]
        return [
            pltpu.make_async_copy(*p, sem.at[t]) for p, sem in zip(pair, (hid_sem, slope_sem))
        ]

    others = [p["tensor"] for p in across]

    def res_chunk(j):
        lanes = pl.ds(pl.multiple_of(j * STEP, LANES), STEP)
        pairs = [(t, res) for t in others] + [(me, res_own)]
        return [
            pltpu.make_async_copy(chunk_near.at[t], ref.at[t, :, lanes], res_sem.at[i])
            for i, (t, ref) in enumerate(pairs)
        ]

    def low_of(off):
        normed, scale = norm(mixed[:, :, pl.ds(off, STEP)].reshape(width, STEP).astype(F32))
        return normed, scale, (normed * chan[:, 0:1] + chan[:, 1:2]).astype(BF16)

    @pl.loop(0, chunks)
    def _(j):
        off = pl.multiple_of(j * STEP, LANES)
        _, _, low = low_of(off)
        for t in range(parts):
            @pl.when(j > 0)
            def _():
                for copy in hid_copy(t, j, False):
                    copy.wait()

            for part in range(2):
                sl = pl.ds(t * shard + part * (shard // 2), shard // 2)
                pre = nn(win_t[sl, :], low) + bin_col[sl, 0:1]
                square_pre = pre * pre
                th = jnp.tanh(pre * (GELU_C + (GELU_C * GELU_A) * square_pre))
                half = 0.5 * th + 0.5
                inner_slope = GELU_C + (3 * GELU_C * GELU_A) * square_pre
                hid[sl, :] = (pre * half).astype(BF16)
                slope[sl, :] = (half + pre * (0.5 - 0.5 * th * th) * inner_slope).astype(BF16)
            for copy in hid_copy(t, j, False):
                copy.start()
        branch = nn(wout_t[...], hid[...]) + chan[:, 2:3]
        source = x_all[:, :, pl.ds(off, STEP)].reshape(width, STEP).astype(F32)
        out = (source + chan[:, 3:4] * branch).astype(BF16)

        @pl.when(j > 0)
        def _():
            for copy in res_chunk(j):
                copy.wait()

        chunk_near[...] = out.reshape(parts, local, STEP)
        for copy in res_chunk(j):
            copy.start()

    for t in range(parts):
        for copy in hid_copy(t, 0, False):
            copy.wait()
        for copy in hid_copy(t, 0, True):
            copy.start()

    for copy in res_chunk(0):
        copy.wait()

    arrived(go_copies)
    res_copies = [remote(res.at[p["tensor"]], res_own.at[me], p) for p in across]

    for ref in (dw, bin_acc, vec):
        ref[...] = jnp.zeros_like(ref)

    def go_chunk(j):
        off = pl.multiple_of(j * STEP, LANES)
        mine_at = pl.ds(pl.multiple_of(me * pix + off, LANES), STEP)
        sources = [(t, go_all.at[t, :, pl.ds(off, STEP)]) for t in others] + [(me, go.at[:, mine_at])]
        return [
            pltpu.make_async_copy(src, chunk_near.at[t], go_sem.at[i])
            for i, (t, src) in enumerate(sources)
        ]

    for copy in go_chunk(0):
        copy.start()

    @pl.loop(0, chunks)
    def _(j):
        off = pl.multiple_of(j * STEP, LANES)
        for copy in go_chunk(j):
            copy.wait()
        grad = chunk_near[...].reshape(width, STEP).astype(F32)
        gb = (grad * chan[:, 3:4]).astype(BF16)
        vec[0] += fold(gb.astype(F32))
        vec[3] += fold(grad)

        @pl.when(j + 1 < chunks)
        def _():
            for copy in go_chunk(j + 1):
                copy.start()

        normed, scale, low = low_of(off)
        for t in range(parts):
            sl = pl.ds(t * shard, shard)
            for copy in hid_copy(t, j, True):
                copy.wait()
            tile = (nn(wout[t], gb) * slope[sl, :].astype(F32)).astype(BF16)
            gp[sl, :] = tile
            bin_acc[sl, :] += fold(tile.astype(F32))
            dw[0, t] += nt(hid[sl, :], gb)
            dw[1, t] += nt(tile, low)

            @pl.when(j + 1 < chunks)
            def _():
                for copy in hid_copy(t, j + 1, True):
                    copy.start()

        gn = nn(win[...], gp[...])
        vec[1] += fold(gn * normed)
        vec[2] += fold(gn)
        g1 = gn * chan[:, 0:1]
        m1 = jnp.mean(g1, axis=0, keepdims=True)
        m2 = jnp.mean(g1 * normed, axis=0, keepdims=True)
        gm = (scale * (g1 - m1 - normed * m2)).reshape(parts, local, STEP)
        for q in range(local // GROUP):
            block = gm[:, q * GROUP : (q + 1) * GROUP, :].reshape(LANES, STEP)
            grow[q, pl.ds(off, STEP), :] = jnp.transpose(block)

    def slab_of(peer):
        return pl.ds(pl.multiple_of((peer["dp"] - first) * slab, slab), slab)

    dw_near = near(dw.at[:, :, my_slab, :], dw_peer.at[:, :, my_slab, :])
    dw_copies = [
        remote(dw.at[:, :, slab_of(p), :], dw_peer.at[:, :, my_slab, :], p) for p in beside
    ]

    back = [near(go_all.at[t], mixed.at[t]) for t in others]
    back.append(near(pixels(go, me), mixed.at[me]))
    for copy in back:
        copy.wait()

    def gx_tile(q):
        return pl.ds(pl.multiple_of(q * GROUP, GROUP), GROUP)

    def gx_copies(q):
        at = gx_tile(q)
        return [
            pltpu.make_async_remote_copy(
                src_ref=mixed.at[p["tensor"], at, :],
                dst_ref=g_own.at[me, at, :],
                send_sem=gx_send.at[q, s],
                recv_sem=gx_recv.at[q, s],
                device_id=p,
                device_id_type=MESH,
            )
            for s, p in enumerate(across)
        ] + [pltpu.make_async_copy(mixed.at[me, at, :], g_own.at[me, at, :], gx_own.at[q])]

    @pl.loop(0, local // GROUP)
    def _(q):
        mix_bwd(q, x_all, rows, grow, kern, mask, inner, mid, mixed, gkern)

        @pl.when(q == 0)
        def _():
            for copy in gx_copies(q):
                copy.start()

    for t in range(parts):
        lanes = slice(t * GROUP, (t + 1) * GROUP)
        pack_mine[t] = jnp.zeros(pack_mine.shape[1:], F32)
        pack_mine[t, 0:32, 0:local] = jnp.concatenate(
            [gkern[q, 0:32, lanes] for q in range(local // GROUP)], axis=1
        )
    acc = jnp.zeros((width, LANES), F32)
    sums = [jnp.sum(vec[k], axis=1, keepdims=True) for k in range(4)]
    for k in range(3):
        acc = column_set(acc, k, sums[k])
    square[0:1, :] = sum(
        jnp.sum(wout[t].astype(F32) * dw[0, t], axis=0, keepdims=True) for t in range(parts)
    )
    products = jnp.concatenate(
        [
            jnp.transpose(square[:, i * LANES : (i + 1) * LANES])[:, 0:1]
            for i in range(width // LANES)
        ]
    )
    acc = column_set(acc, 3, products / chan[:, 3:4] + chan[:, 2:3] * sums[3])
    hidden_sums = jnp.sum(bin_acc[...], axis=1, keepdims=True)
    for k in range(shard // local):
        starts = [t * shard + k * local for t in range(parts)]
        acc = column_set(acc, 4 + k, jnp.concatenate([hidden_sums[i : i + local] for i in starts]))
    for t in range(parts):
        square[0:local, 0:LANES] = acc[t * local : (t + 1) * local]
        pack_mine[t, 32:40, :] = jnp.transpose(square[:, 0:LANES])[0:8]
    pack_peer[mine] = pack_mine[...]
    pack_copies = [remote(pack_mine, pack_peer.at[mine], p) for p in beside]

    dw_near.wait()
    for copy in dw_copies:
        copy.wait()
    near(dw_peer, dw).wait()
    terms = [dw[:, :, i * slab : (i + 1) * slab, :] for i in range(groups)]
    dw_sum[...] = sum(terms[1:], terms[0])
    dw_low[...] = dw_sum[...].astype(BF16)

    def leg(kind, way, src, slot, peer):
        return pltpu.make_async_remote_copy(
            src_ref=src,
            dst_ref=(dw_tensor, pack_tensor)[kind].at[slot],
            send_sem=leg_send.at[kind, way],
            recv_sem=leg_recv.at[kind, slot],
            device_id=peer,
            device_id_type=MESH,
        )

    def term(kind, t):
        return pack_sum.at[t] if kind else dw_low.at[:, t]

    def to_partner(kind):
        return leg(kind, 0, term(kind, partner["tensor"]), 0, partner)

    def to_inner(kind, k):
        return leg(kind, 1 + k, term(kind, other_half + k), 2 + k, partner)

    def crossing(kind, k):
        src = (dw_pass, pack_pass)[kind].at[k]
        return leg(kind, 3 + k, src, 1, {"tensor": other_half + k})

    def start_leg(kind):
        to_partner(kind).start()

        @pl.when(jnp.logical_not(is_inner))
        def _():
            for k in range(2):
                to_inner(kind, k).start()

    start_leg(0)
    arrived(pack_copies)
    pack_sum[...] = sum((pack_peer[i] for i in range(1, groups)), pack_peer[0])
    start_leg(1)
    for copy in gx_copies(1):
        copy.start()

    @pl.when(is_inner)
    def _():
        for kind in range(2):
            for k in range(2):
                to_inner(kind, k).wait_recv()
        for k in range(2):
            dw_pass[k] = (dw_sum[:, other_half + k] + dw_tensor[2 + k].astype(F32)).astype(BF16)
            pack_pass[k] = pack_sum[other_half + k] + pack_tensor[2 + k]
        for kind in range(2):
            for k in range(2):
                crossing(kind, k).start()

    for q in range(2, local // GROUP):
        for copy in gx_copies(q):
            copy.start()

    def received(kind):
        to_partner(kind).wait_recv()
        crossing(kind, 0).wait_recv()

    received(0)
    dw_done[...] = dw_sum[:, me] + dw_tensor[0].astype(F32) + dw_tensor[1].astype(F32)
    dw_near = near(dw_done, dw_own.at[:, my_slab, :])
    dw_copies = [remote(dw_done, dw_own.at[:, my_slab, :], p) for p in beside]
    received(1)
    total = pack_sum[me] + pack_tensor[0] + pack_tensor[1]
    gdt = lag_grads(total, steps, a_log, a_imag, coefs, g_alog, g_aimag, [g_height, g_width])
    row_own[...] = total
    for j in range(2):
        row_own[29 + j : 30 + j, 0:local] = gdt[j]

    arrived(dw_copies)
    dw_near.wait()
    arrived(res_copies)

    @pl.loop(0, local // GROUP)
    def _(q):
        for copy in gx_copies(q):
            copy.wait()

    for copy in sent + first_hops:
        copy.wait_send()

    for kind in range(2):
        to_partner(kind).wait_send()

    @pl.when(is_inner)
    def _():
        for k in range(2):
            for copy in handed_on(k):
                copy.wait_send()
            for kind in range(2):
                crossing(kind, k).wait_send()

    @pl.when(jnp.logical_not(is_inner))
    def _():
        for k in range(2):
            for kind in range(2):
                to_inner(kind, k).wait_send()


def block(parts, groups, args):
    x, size = args[0], args[2]
    local, pixels = x.shape
    pix = pixels // parts
    width = local * parts
    w_in = args[12]
    shard = w_in.shape[1]
    ff = shard * parts
    slab = shard // groups
    tiles = local // GROUP
    states = args[4].shape[0]
    shape = jax.ShapeDtypeStruct
    vmem = pl.BlockSpec(memory_space=pltpu.VMEM)
    hbm = pl.BlockSpec(memory_space=pl.ANY)
    in_specs = [hbm, hbm] + [vmem] * 10 + [hbm, vmem, hbm, vmem, vmem]
    outs = [
        (pltpu.VMEM((parts, local, pix), BF16), vmem),
        (pltpu.VMEM((parts, local, pix), BF16), vmem),
        (pltpu.VMEM((2, shard, width), F32), vmem),
        (pltpu.VMEM((states, local), F32), vmem),
        (pltpu.VMEM((states, local), F32), vmem),
        (pltpu.VMEM((2, states, local), F32), vmem),
        (pltpu.VMEM((2, states, local), F32), vmem),
        (pltpu.VMEM((40, LANES), F32), vmem),
        (shape((parts, local, pix), BF16), hbm),
        (shape((ff, pix), BF16), hbm),
        (shape((ff, pix), BF16), hbm),
        (shape((parts, local, pix), BF16), hbm),
        (shape((2, parts, shard, width), F32), hbm),
    ]
    remotes = 4 * (parts - 1) + 5 * (groups - 1)
    dma = pltpu.SemaphoreType.DMA
    scratch = [
        pltpu.VMEM((parts, local, pix), BF16),
        pltpu.VMEM((parts, local, pix), BF16),
        pltpu.VMEM((pix, LANES), F32),
        pltpu.VMEM((tiles, pix, LANES), F32),
        pltpu.VMEM((CROP, CROP, 8, LANES), F32),
        pltpu.VMEM((CROP, CROP, 8, LANES), F32),
        pltpu.VMEM((4, 2 * CROP, 8, LANES), F32),
        pltpu.VMEM((40, LANES), F32),
        pltpu.VMEM((parts, 40, LANES), F32),
        pltpu.VMEM((tiles, 32, LANES), F32),
        pltpu.VMEM((tiles, 32, LANES), F32),
        pltpu.VMEM((ff, LANES), F32),
        pltpu.VMEM((width, LANES), F32),
        pltpu.VMEM((LANES, width), F32),
        pltpu.VMEM((LANES, LANES), F32),
        pltpu.VMEM((width, ff), BF16),
        pltpu.VMEM((parts, shard, width), BF16),
        pltpu.VMEM((width, ff), BF16),
        pltpu.VMEM((ff, STEP), BF16),
        pltpu.VMEM((ff, STEP), BF16),
        pltpu.VMEM((ff, STEP), BF16),
        pltpu.VMEM((parts, local, STEP), BF16),
        pltpu.VMEM((2, parts, shard, width), F32),
        pltpu.VMEM((2, parts, slab, width), F32),
        pltpu.VMEM((2, parts, slab, width), BF16),
        pltpu.VMEM((4, 2, slab, width), BF16),
        pltpu.VMEM((2, 2, slab, width), BF16),
        pltpu.VMEM((2, slab, width), F32),
        pltpu.VMEM((ff, LANES), F32),
        pltpu.VMEM((4, width, LANES), F32),
        pltpu.VMEM((parts, 40, LANES), F32),
        pltpu.VMEM((groups, parts, 40, LANES), F32),
        pltpu.VMEM((parts, 40, LANES), F32),
        pltpu.VMEM((4, 40, LANES), F32),
        pltpu.VMEM((2, 40, LANES), F32),
        dma((remotes,)),
        dma((remotes,)),
        dma((10,)),
        dma((4, 3)),
        dma((3, 3)),
        dma((2, 5)),
        dma((2, 4)),
        dma((parts,)),
        dma((parts,)),
        dma((parts,)),
        dma((parts,)),
        dma((tiles, parts - 1)),
        dma((tiles, parts - 1)),
        dma((tiles,)),
    ]
    return pl.pallas_call(
        functools.partial(block_kernel, parts, groups),
        out_shape=[o[0] for o in outs],
        in_specs=in_specs,
        out_specs=[o[1] for o in outs],
        scratch_shapes=scratch,
        compiler_params=pltpu.CompilerParams(
            collective_id=0, has_side_effects=True, vmem_limit_bytes=VMEM
        ),
        name="block",
    )(*args)


def finish_kernel(parts, n_sums, *refs):
    sums, refs = refs[:n_sums], refs[n_sums:]
    res_ref, g_ref, result_ref, grad_ref = refs[:4]
    n_small = (len(refs) - 7) // 2
    smalls, refs = refs[4 : 4 + n_small], refs[4 + n_small :]
    grad_near = refs[0]
    near = refs[1 : 1 + n_small]
    left, smalls_left = refs[1 + n_small :]
    pix = g_ref.shape[2]
    out_copies = []

    def put(src, dst, sem):
        out_copies.append(pltpu.make_async_copy(src, dst, sem))
        out_copies[-1].start()

    for s in range(parts):
        put(res_ref.at[s], result_ref.at[:, pl.ds(s * pix, pix)], left.at[1, s])
    for s in range(parts):
        grad_near[s] = g_ref[s].astype(F32)
        put(grad_near.at[s], grad_ref.at[:, pl.ds(s * pix, pix)], left.at[0, s])
        if s == 0:
            dw, g_alog, g_aimag, g_height, g_width, rows = sums
            alog, aimag, height, width, dt, skip, gain, bias, win, bin_, wout, bout, scale = near
            for out, ref in ((alog, g_alog), (aimag, g_aimag), (height, g_height), (width, g_width)):
                out[...] = ref[...]
            local = skip.shape[0]
            dt[...] = rows[29:31, 0:local]
            for out, k in ((skip, 28), (gain, 33), (bias, 34), (bout, 32), (scale, 35)):
                out[...] = rows[k : k + 1, 0:local].reshape(local)
            bin_[...] = jnp.concatenate(
                [rows[36 + k : 37 + k, 0:local] for k in range(bin_.shape[0] // local)], axis=1
            ).reshape(bin_.shape)
            win[...] = jnp.transpose(dw[1])
            wout[...] = dw[0]
            for k in range(n_small):
                put(near[k], smalls[k], smalls_left.at[k])
    for copy in out_copies:
        copy.wait()


def finish(res_own, g_own, sums):
    parts, local, pix = g_own.shape
    dw, g_alog, _, g_height, _, _ = sums
    hbm = pl.BlockSpec(memory_space=pl.ANY)
    vmem = pl.BlockSpec(memory_space=pltpu.VMEM)
    dma = pltpu.SemaphoreType.DMA
    shape = jax.ShapeDtypeStruct
    line = (local,)
    small = (
        g_alog.shape,
        g_alog.shape,
        g_height.shape,
        g_height.shape,
        (2, local),
        line,
        line,
        line,
        (dw.shape[2], dw.shape[1]),
        (dw.shape[1],),
        dw.shape[1:],
        line,
        line,
    )
    return pl.pallas_call(
        functools.partial(finish_kernel, parts, len(sums)),
        out_shape=(shape((local, parts * pix), BF16), shape((local, parts * pix), F32))
        + tuple(shape(a, F32) for a in small),
        in_specs=[vmem] * (len(sums) + 2),
        out_specs=(hbm,) * (2 + len(small)),
        scratch_shapes=[
            pltpu.VMEM(g_own.shape, F32),
        ]
        + [pltpu.VMEM(a, F32) for a in small]
        + [dma((2, parts)), dma((len(small),))],
        compiler_params=pltpu.CompilerParams(vmem_limit_bytes=24 << 20),
        name="finish",
    )(*sums, res_own, g_own)


def per_device(
    parts,
    dp_size,
    inputs,
    crop_size,
    crop_offset,
    a_log,
    a_imag,
    c_height,
    c_width,
    log_dt,
    skip_gain,
    ln_gain,
    ln_bias,
    w_in,
    b_in,
    w_out,
    b_out,
    layer_scale,
    grad_out,
):
    canvases = crop_size.shape[0]
    groups = min(dp_size, 8)
    args = (
        inputs,
        grad_out,
        jnp.transpose(crop_size.reshape(canvases, 8)),
        jnp.transpose(crop_offset.reshape(canvases, 8)),
        jnp.transpose(a_log),
        jnp.transpose(a_imag),
        jnp.transpose(c_height, (0, 2, 1)),
        jnp.transpose(c_width, (0, 2, 1)),
        log_dt,
        skip_gain,
        ln_gain,
        ln_bias,
        w_in,
        b_in,
        w_out,
        b_out,
        layer_scale,
    )
    out = block(parts, groups, args)
    sums = tuple(out[2:8])
    if dp_size > groups:
        teams = [[r + groups * g for g in range(dp_size // groups)] for r in range(groups)]
        sums = lax.psum(sums, "dp", axis_index_groups=teams)
    done = finish(out[0], out[1], sums)
    return (
        done[0],
        done[1],
        jnp.transpose(done[2]),
        jnp.transpose(done[3]),
        jnp.transpose(done[4], (0, 2, 1)),
        jnp.transpose(done[5], (0, 2, 1)),
        *done[6:],
    )


def solution(mesh):
    in_specs = (
        P("tensor", "dp"),
        P("dp", None, None),
        P("dp", None, None),
        P("tensor", None),
        P("tensor", None),
        P(None, "tensor", None),
        P(None, "tensor", None),
        P(None, "tensor"),
        P("tensor"),
        P(),
        P(),
        P(None, "tensor"),
        P("tensor"),
        P("tensor", None),
        P(),
        P(),
        P("tensor", "dp"),
    )
    out_specs = (
        P("tensor", "dp"),
        P("tensor", "dp"),
        P("tensor", None),
        P("tensor", None),
        P(None, "tensor", None),
        P(None, "tensor", None),
        P(None, "tensor"),
        P("tensor"),
        P("tensor"),
        P("tensor"),
        P(None, "tensor"),
        P("tensor"),
        P("tensor", None),
        P("tensor"),
        P("tensor"),
    )
    return jax.shard_map(
        functools.partial(per_device, mesh.shape["tensor"], mesh.shape["dp"]),
        mesh=mesh,
        in_specs=in_specs,
        out_specs=out_specs,
        check_vma=False,
    )
```

```python
import functools

import jax
import jax.numpy as jnp
from jax import lax
from jax.experimental import pallas as pl
from jax.experimental.pallas import tpu as pltpu
from jax.sharding import PartitionSpec as P

F32, BF16 = jnp.float32, jnp.bfloat16
CROP = 14
SIDE = 2 * CROP
NPIX = SIDE * SIDE
LANES = 128
GROUP = 32
STEP = 896
EPS = 1e-06
GELU_C = 0.7978845608028654
GELU_A = 0.044715
VMEM = 53 << 20
MESH = pl.DeviceIdType.MESH


def nn(a, b):
    return lax.dot_general(a, b, (((1,), (0,)), ((), ())), preferred_element_type=F32)


def nt(a, b):
    return lax.dot_general(a, b, (((1,), (1,)), ((), ())), preferred_element_type=F32)


def conv(y, taps):
    return [sum((taps[l] * y[i - l] for l in range(1, i + 1)), taps[0] * y[i]) for i in range(CROP)]


def conv_back(y, taps):
    return [
        sum((taps[l] * y[i + l] for l in range(1, CROP - i)), taps[0] * y[i]) for i in range(CROP)
    ]


def spot(slot, h, w):
    first = (slot // 2) * (CROP * SIDE) + (slot % 2) * CROP
    return pl.ds(first + h * SIDE + w, 8, stride=NPIX)


def lanes_to_rows(load, rows):
    @pl.loop(0, rows.shape[0] // STEP)
    def _(j):
        off = pl.multiple_of(j * STEP, LANES)
        rows[pl.ds(off, STEP), :] = jnp.transpose(load(off).astype(F32))


def rows_to_lanes(rows, store):
    @pl.loop(0, rows.shape[0] // STEP)
    def _(j):
        off = pl.multiple_of(j * STEP, LANES)
        store(off, jnp.transpose(rows[pl.ds(off, STEP), :]).astype(BF16))


def tap_rows(kern, q, base):
    return [jnp.broadcast_to(kern[q, pl.ds(base + l, 1), :], (8, LANES)) for l in range(CROP)]


def tile_of(ref, q, off):
    return ref[:, pl.ds(pl.multiple_of(q * GROUP, GROUP), GROUP), pl.ds(off, STEP)].reshape(
        LANES, STEP
    )


def put_tile(ref, q, off, v):
    ref[:, pl.ds(pl.multiple_of(q * GROUP, GROUP), GROUP), pl.ds(off, STEP)] = v.reshape(
        ref.shape[0], GROUP, STEP
    )


def along_width(q, slot, rows, kern, mask, inner):
    @pl.loop(0, CROP)
    def _(h):
        taps = tap_rows(kern, q, CROP)
        row_in = mask[slot, h]
        y = [rows[spot(slot, h, w), :] * mask[slot, CROP + w] for w in range(CROP)]
        for w, v in enumerate(conv(y, taps)):
            inner[h, w] = v * row_in


def mix_fwd(q, x_all, rows, kern, mask, inner, mixed):
    lanes_to_rows(lambda off: tile_of(x_all, q, off), rows)
    skip = jnp.broadcast_to(kern[q, pl.ds(2 * CROP, 1), :], (8, LANES))

    @pl.loop(0, 4)
    def _(slot):
        along_width(q, slot, rows, kern, mask, inner)

        @pl.loop(0, CROP)
        def _(w):
            taps = tap_rows(kern, q, 0)
            col_in = mask[slot, CROP + w]
            y = [inner[h, w] for h in range(CROP)]
            for h, v in enumerate(conv(y, taps)):
                at = spot(slot, h, w)
                rows[at, :] = v * (mask[slot, h] * col_in) + skip * rows[at, :]

    rows_to_lanes(rows, lambda off, v: put_tile(mixed, q, off, v))


def mix_bwd(q, x_all, rows, grow, kern, mask, inner, mid, out, gkern):
    lanes_to_rows(lambda off: tile_of(x_all, q, off), rows)
    skip = jnp.broadcast_to(kern[q, pl.ds(2 * CROP, 1), :], (8, LANES))
    zero = jnp.zeros((8, LANES), F32)

    def per_slot(slot, sums):
        gk_height, gk_width, gskip = sums
        along_width(q, slot, rows, kern, mask, inner)

        def down(w, acc):
            taps = tap_rows(kern, q, 0)
            col_in = mask[slot, CROP + w]
            u = [grow[q, spot(slot, h, w), :] * (mask[slot, h] * col_in) for h in range(CROP)]
            for h, v in enumerate(conv_back(u, taps)):
                mid[h, w] = v * mask[slot, h]
            a = [inner[h, w] for h in range(CROP)]
            return tuple(
                sum((u[h] * a[h - l] for h in range(l, CROP)), acc[l]) for l in range(CROP)
            )

        gk_height = lax.fori_loop(0, CROP, down, gk_height)

        def across(h, acc):
            gk_width, gskip = acc
            taps = tap_rows(kern, q, CROP)
            u = [mid[h, w] for w in range(CROP)]
            x = [rows[spot(slot, h, w), :] for w in range(CROP)]
            y = [x[w] * mask[slot, CROP + w] for w in range(CROP)]
            gk_width = tuple(
                sum((u[w] * y[w - l] for w in range(l, CROP)), gk_width[l]) for l in range(CROP)
            )
            for w, v in enumerate(conv_back(u, taps)):
                at = spot(slot, h, w)
                g = grow[q, at, :]
                gskip = gskip + g * x[w]
                grow[q, at, :] = v * mask[slot, CROP + w] + skip * g
            return gk_width, gskip

        gk_width, gskip = lax.fori_loop(0, CROP, across, (gk_width, gskip))
        return gk_height, gk_width, gskip

    gk_height, gk_width, gskip = lax.fori_loop(
        0, 4, per_slot, ((zero,) * CROP, (zero,) * CROP, zero)
    )
    gkern[q] = jnp.zeros((32, LANES), F32)
    for row, v in enumerate((*gk_height, *gk_width, gskip)):
        gkern[q, pl.ds(row, 1), :] = jnp.sum(v, axis=0, keepdims=True)

    @pl.loop(0, rows.shape[0] // STEP)
    def _(j):
        off = pl.multiple_of(j * STEP, LANES)
        turned = jnp.transpose(grow[q, pl.ds(off, STEP), :])
        put_tile(out, q, off, (tile_of(out, q, off).astype(F32) + turned).astype(BF16))


def lag_waves(step, a_log, a_imag):
    rate = -step * jnp.exp(a_log)
    phase = step * a_imag
    size = jnp.exp(rate)
    re1, im1 = size * jnp.cos(phase), size * jnp.sin(phase)
    re, im = jnp.ones_like(re1), jnp.zeros_like(im1)
    out = []
    for _ in range(CROP):
        out.append((re, im))
        re, im = re * re1 - im * im1, re * im1 + im * re1
    return rate, phase, out


def column_set(acc, k, col):
    lane = lax.broadcasted_iota(jnp.int32, acc.shape, 1)
    return jnp.where(lane == k, col, acc)


def lag_kernels(steps, a_log, a_imag, coefs, out):
    local = a_log.shape[1]
    for j in range(2):
        _, _, waves = lag_waves(steps[j], a_log[...], a_imag[...])
        for l, (re, im) in enumerate(waves):
            row = jnp.sum(coefs[j][0] * re - coefs[j][1] * im, axis=0, keepdims=True)
            out[CROP * j + l : CROP * j + l + 1, 0:local] = row


def lag_grads(rows, steps, a_log, a_imag, coefs, g_alog, g_aimag, g_coefs):
    ga, gi, gdt = 0.0, 0.0, []
    for j in range(2):
        rate, phase, waves = lag_waves(steps[j], a_log[...], a_imag[...])
        cre, cim = coefs[j][0], coefs[j][1]
        g_re = g_im = p = r = 0.0
        for l, (re, im) in enumerate(waves):
            g = rows[CROP * j + l : CROP * j + l + 1, 0 : a_log.shape[1]]
            g_re = g_re + g * re
            g_im = g_im - g * im
            if l:
                p = p + (l * g) * (cre * re - cim * im)
                r = r - (l * g) * (cre * im + cim * re)
        g_coefs[j][0] = g_re
        g_coefs[j][1] = g_im
        ga = ga + p * rate
        gi = gi + r * steps[j]
        gdt.append(jnp.sum(p * rate + r * phase, axis=0, keepdims=True))
    g_alog[...] = ga
    g_aimag[...] = gi
    return gdt


def norm(m):
    centered = m - jnp.mean(m, axis=0, keepdims=True)
    scale = lax.rsqrt(jnp.mean(centered * centered, axis=0, keepdims=True) + EPS)
    return centered * scale, scale


def fold(v):
    return sum(
        (v[:, i * LANES : (i + 1) * LANES] for i in range(1, v.shape[1] // LANES)), v[:, :LANES]
    )


def block_kernel(
    parts,
    groups,
    x,
    go,
    size_ref,
    offset_ref,
    a_log,
    a_imag,
    c_height,
    c_width,
    log_dt,
    skip_gain,
    ln_gain,
    ln_bias,
    w_in,
    b_in,
    w_out,
    b_out,
    layer_scale,
    res_own,
    g_own,
    dw_own,
    g_alog,
    g_aimag,
    g_height,
    g_width,
    row_own,
    go_all,
    hid_far,
    slope_far,
    res,
    dw_peer,
    x_all,
    mixed,
    rows,
    grow,
    inner,
    mid,
    mask,
    small_mine,
    small_all,
    kern,
    gkern,
    bin_col,
    chan,
    square,
    turned,
    win,
    wout,
    wout_t,
    hid,
    slope,
    gp,
    chunk_near,
    dw,
    dw_sum,
    dw_low,
    dw_tensor,
    dw_pass,
    dw_done,
    bin_acc,
    vec,
    pack_mine,
    pack_peer,
    pack_sum,
    pack_tensor,
    pack_pass,
    send,
    recv,
    own,
    x_send,
    x_recv,
    hop_send,
    hop_recv,
    leg_send,
    leg_recv,
    hid_sem,
    slope_sem,
    go_sem,
    res_sem,
    gx_send,
    gx_recv,
    gx_own,
):
    local, pix = x_all.shape[1], x_all.shape[2]
    width = local * parts
    ff = gp.shape[0]
    win_t = gp.at[:, 0:width]
    shard = ff // parts
    slab = shard // groups
    chunks = pix // STEP
    me = lax.axis_index("tensor")
    dp = lax.axis_index("dp")
    mine = lax.rem(dp, groups)
    first = dp - mine
    across = [{"tensor": lax.rem(me + s, parts)} for s in range(1, parts)]
    beside = [{"dp": first + lax.rem(mine + s, groups)} for s in range(1, groups)]

    barrier = pltpu.get_barrier_semaphore()
    for peer in across + beside:
        pl.semaphore_signal(barrier, inc=1, device_id=peer, device_id_type=MESH)
    pl.semaphore_wait(barrier, len(across) + len(beside))

    count = [0, 0]

    def remote(src, dst, peer, sems=None):
        if sems is None:
            sems = (send.at[count[0]], recv.at[count[0]])
            count[0] += 1
        copy = pltpu.make_async_remote_copy(
            src_ref=src,
            dst_ref=dst,
            send_sem=sems[0],
            recv_sem=sems[1],
            device_id=peer,
            device_id_type=MESH,
        )
        copy.start()
        return copy

    def near(src, dst, sem=None):
        if sem is None:
            sem = own.at[count[1]]
            count[1] += 1
        copy = pltpu.make_async_copy(src, dst, sem)
        copy.start()
        return copy

    sent = []

    def arrived(copies):
        for copy in copies:
            copy.wait_recv()
        sent.extend(copies)

    def pixels(ref, peer):
        return ref.at[:, pl.ds(pl.multiple_of(peer * pix, LANES), pix)]

    def to_owner(ref, out):
        return [remote(pixels(ref, p["tensor"]), out.at[me], p) for p in across]

    my_slab = pl.ds(pl.multiple_of(mine * slab, slab), slab)
    steps = [jnp.exp(log_dt[j : j + 1, :]) for j in range(2)]
    coefs = [c_height, c_width]

    partner = {"tensor": me + 1 - 2 * lax.rem(me, 2)}
    inner_device = {"tensor": jnp.where(me < 2, 2, 1)}
    is_inner = (me == 1) | (me == 2)
    other_half = 2 - 2 * (me // 2)

    def cols_of(t):
        return pl.ds(pl.multiple_of(t * shard, LANES), shard)

    def pieces(t):
        return [
            (win.at[my_slab, cols_of(t)], win.at[my_slab, cols_of(t)]),
            (wout.at[t, my_slab, :], wout.at[t, my_slab, :]),
            (small_all.at[t], small_all.at[t]),
        ]

    def hop(i, k, pair, peer, way):
        return pltpu.make_async_remote_copy(
            src_ref=pair[0],
            dst_ref=pair[1],
            send_sem=hop_send.at[way, i],
            recv_sem=hop_recv.at[k, i],
            device_id=peer,
            device_id_type=MESH,
        )

    first_hops = []
    slabs = [w_in.at[my_slab, :], w_out.at[my_slab, :], small_mine]
    for i in range(3):
        if i == 2:
            small_mine[...] = jnp.zeros_like(small_mine)
            lag_kernels(steps, a_log, a_imag, coefs, small_mine)
            small_mine[2 * CROP : 2 * CROP + 1, 0:local] = skip_gain[...].reshape(1, local)
            biases = b_in[...].reshape(1, shard)
            for j in range(shard // LANES):
                small_mine[32 + j : 33 + j, :] = biases[:, j * LANES : (j + 1) * LANES]
        pair = (slabs[i], pieces(me)[i][1])
        first_hops.append(hop(i, 0, pair, partner, 0))
        first_hops.append(hop(i, 1 + lax.rem(me, 2), pair, inner_device, 1))
        for copy in first_hops[-2:]:
            copy.start()
    w_near = [near(slabs[i], pieces(me)[i][1]) for i in range(2)]
    small_all[me] = small_mine[...]

    def handed_on(k):
        found = pieces(other_half + k)
        return [hop(i, 1 + k, found[i], partner, 2 + k) for i in range(3)]

    def x_copy(k, came=False):
        peer = partner["tensor"] if k == 2 else other_half + k
        slot = k if k == 2 or came else lax.rem(me, 2)
        return pltpu.make_async_remote_copy(
            src_ref=pixels(x, peer),
            dst_ref=x_all.at[peer if came else me],
            send_sem=x_send.at[k],
            recv_sem=x_recv.at[slot],
            device_id={"tensor": peer},
            device_id_type=MESH,
        )

    for k in range(2):
        x_copy(k).start()

    @pl.when(is_inner)
    def _():
        for k in range(2):
            for copy in handed_on(k):
                copy.wait_recv()
            for copy in handed_on(k):
                copy.start()

    x_copy(2).start()
    x_near = near(pixels(x, me), x_all.at[me])

    @pl.when(jnp.logical_not(is_inner))
    def _():
        for k in range(2):
            for copy in handed_on(k):
                copy.wait_recv()

    for copy in w_near:
        copy.wait()
    for copy in first_hops[::2]:
        copy.wait_recv()
    w_copies = [remote(win.at[my_slab, :], win.at[my_slab, :], p) for p in beside]
    w_copies += [remote(wout.at[:, my_slab, :], wout.at[:, my_slab, :], p) for p in beside]

    square[...] = jnp.zeros_like(square)
    for row, ref in enumerate((ln_gain, ln_bias, b_out, layer_scale)):
        square[row : row + 1, :] = ref[...].reshape(1, width)
    for i in range(width // LANES):
        chan[i * LANES : (i + 1) * LANES, :] = jnp.transpose(square[:, i * LANES : (i + 1) * LANES])
    canvases = size_ref.shape[1]
    square[0:8, 0:canvases] = offset_ref[...].astype(F32)
    square[8:16, 0:canvases] = size_ref[...].astype(F32)
    turned[...] = jnp.transpose(square[:, 0:LANES])
    at = pl.ds(pl.multiple_of(me * 8, 8), 8)
    for slot in range(4):
        for j in range(2):
            k = 2 * slot + j
            low = jnp.broadcast_to(turned[at, k : k + 1], (8, LANES))
            high = low + jnp.broadcast_to(turned[at, 8 + k : 9 + k], (8, LANES))
            for s in range(CROP):
                mask[slot, CROP * j + s] = jnp.where((low <= s) & (s < high), 1.0, 0.0)
    for q in range(local // GROUP):
        kern[q] = jnp.concatenate(
            [small_all[t, 0:32, q * GROUP : (q + 1) * GROUP] for t in range(parts)], axis=1
        )
    for t in range(parts):
        for i in range(shard // LANES):
            block = jnp.broadcast_to(small_all[t, 32 + i : 33 + i, :], (LANES, LANES))
            bin_col[t * shard + i * LANES : t * shard + (i + 1) * LANES, :] = jnp.transpose(block)
    arrived(w_copies)
    for t in range(parts):
        cols = slice(t * shard, (t + 1) * shard)
        win_t[cols, :] = jnp.transpose(win[:, cols].astype(F32)).astype(BF16)
        wout_t[:, cols] = jnp.transpose(wout[t].astype(F32)).astype(BF16)

    for k in range(3):
        x_copy(k, came=True).wait_recv()
    x_near.wait()
    go_copies = to_owner(go, go_all)

    @pl.loop(0, local // GROUP)
    def _(q):
        mix_fwd(q, x_all, rows, kern, mask, inner, mixed)

    def hid_copy(t, j, back):
        sl = pl.ds(t * shard, shard)
        lanes = pl.ds(pl.multiple_of(j * STEP, LANES), STEP)
        pair = [(hid.at[sl, :], hid_far.at[sl, lanes]), (slope.at[sl, :], slope_far.at[sl, lanes])]
        pair = [p[::-1] if back else p for p in pair]
        return [
            pltpu.make_async_copy(*p, sem.at[t]) for p, sem in zip(pair, (hid_sem, slope_sem))
        ]

    others = [p["tensor"] for p in across]

    def res_chunk(j):
        lanes = pl.ds(pl.multiple_of(j * STEP, LANES), STEP)
        pairs = [(t, res) for t in others] + [(me, res_own)]
        return [
            pltpu.make_async_copy(chunk_near.at[t], ref.at[t, :, lanes], res_sem.at[i])
            for i, (t, ref) in enumerate(pairs)
        ]

    def low_of(off):
        normed, scale = norm(mixed[:, :, pl.ds(off, STEP)].reshape(width, STEP).astype(F32))
        return normed, scale, (normed * chan[:, 0:1] + chan[:, 1:2]).astype(BF16)

    @pl.loop(0, chunks)
    def _(j):
        off = pl.multiple_of(j * STEP, LANES)
        _, _, low = low_of(off)
        for t in range(parts):
            @pl.when(j > 0)
            def _():
                for copy in hid_copy(t, j, False):
                    copy.wait()

            for part in range(2):
                sl = pl.ds(t * shard + part * (shard // 2), shard // 2)
                pre = nn(win_t[sl, :], low) + bin_col[sl, 0:1]
                square_pre = pre * pre
                th = jnp.tanh(pre * (GELU_C + (GELU_C * GELU_A) * square_pre))
                half = 0.5 * th + 0.5
                inner_slope = GELU_C + (3 * GELU_C * GELU_A) * square_pre
                hid[sl, :] = (pre * half).astype(BF16)
                slope[sl, :] = (half + pre * (0.5 - 0.5 * th * th) * inner_slope).astype(BF16)
            for copy in hid_copy(t, j, False):
                copy.start()
        branch = nn(wout_t[...], hid[...]) + chan[:, 2:3]
        source = x_all[:, :, pl.ds(off, STEP)].reshape(width, STEP).astype(F32)
        out = (source + chan[:, 3:4] * branch).astype(BF16)

        @pl.when(j > 0)
        def _():
            for copy in res_chunk(j):
                copy.wait()

        chunk_near[...] = out.reshape(parts, local, STEP)
        for copy in res_chunk(j):
            copy.start()

    for t in range(parts):
        for copy in hid_copy(t, 0, False):
            copy.wait()
        for copy in hid_copy(t, 0, True):
            copy.start()

    for copy in res_chunk(0):
        copy.wait()

    arrived(go_copies)
    res_copies = [remote(res.at[p["tensor"]], res_own.at[me], p) for p in across]

    for ref in (dw, bin_acc, vec):
        ref[...] = jnp.zeros_like(ref)

    def go_chunk(j):
        off = pl.multiple_of(j * STEP, LANES)
        mine_at = pl.ds(pl.multiple_of(me * pix + off, LANES), STEP)
        sources = [(t, go_all.at[t, :, pl.ds(off, STEP)]) for t in others] + [(me, go.at[:, mine_at])]
        return [
            pltpu.make_async_copy(src, chunk_near.at[t], go_sem.at[i])
            for i, (t, src) in enumerate(sources)
        ]

    for copy in go_chunk(0):
        copy.start()

    @pl.loop(0, chunks)
    def _(j):
        off = pl.multiple_of(j * STEP, LANES)
        for copy in go_chunk(j):
            copy.wait()
        grad = chunk_near[...].reshape(width, STEP).astype(F32)
        gb = (grad * chan[:, 3:4]).astype(BF16)
        vec[0] += fold(gb.astype(F32))
        vec[3] += fold(grad)

        @pl.when(j + 1 < chunks)
        def _():
            for copy in go_chunk(j + 1):
                copy.start()

        normed, scale, low = low_of(off)
        for t in range(parts):
            sl = pl.ds(t * shard, shard)
            for copy in hid_copy(t, j, True):
                copy.wait()
            tile = (nn(wout[t], gb) * slope[sl, :].astype(F32)).astype(BF16)
            gp[sl, :] = tile
            bin_acc[sl, :] += fold(tile.astype(F32))
            dw[0, t] += nt(hid[sl, :], gb)
            dw[1, t] += nt(tile, low)

            @pl.when(j + 1 < chunks)
            def _():
                for copy in hid_copy(t, j + 1, True):
                    copy.start()

        gn = nn(win[...], gp[...])
        vec[1] += fold(gn * normed)
        vec[2] += fold(gn)
        g1 = gn * chan[:, 0:1]
        m1 = jnp.mean(g1, axis=0, keepdims=True)
        m2 = jnp.mean(g1 * normed, axis=0, keepdims=True)
        gm = (scale * (g1 - m1 - normed * m2)).reshape(parts, local, STEP)
        for q in range(local // GROUP):
            block = gm[:, q * GROUP : (q + 1) * GROUP, :].reshape(LANES, STEP)
            grow[q, pl.ds(off, STEP), :] = jnp.transpose(block)

    def slab_of(peer):
        return pl.ds(pl.multiple_of((peer["dp"] - first) * slab, slab), slab)

    dw_near = near(dw.at[:, :, my_slab, :], dw_peer.at[:, :, my_slab, :])
    dw_copies = [
        remote(dw.at[:, :, slab_of(p), :], dw_peer.at[:, :, my_slab, :], p) for p in beside
    ]

    back = [near(go_all.at[t], mixed.at[t]) for t in others]
    back.append(near(pixels(go, me), mixed.at[me]))
    for copy in back:
        copy.wait()

    def gx_tile(q):
        return pl.ds(pl.multiple_of(q * GROUP, GROUP), GROUP)

    def gx_copies(q):
        at = gx_tile(q)
        return [
            pltpu.make_async_remote_copy(
                src_ref=mixed.at[p["tensor"], at, :],
                dst_ref=g_own.at[me, at, :],
                send_sem=gx_send.at[q, s],
                recv_sem=gx_recv.at[q, s],
                device_id=p,
                device_id_type=MESH,
            )
            for s, p in enumerate(across)
        ] + [pltpu.make_async_copy(mixed.at[me, at, :], g_own.at[me, at, :], gx_own.at[q])]

    @pl.loop(0, local // GROUP)
    def _(q):
        mix_bwd(q, x_all, rows, grow, kern, mask, inner, mid, mixed, gkern)

        @pl.when(q == 0)
        def _():
            for copy in gx_copies(q):
                copy.start()

    for t in range(parts):
        lanes = slice(t * GROUP, (t + 1) * GROUP)
        pack_mine[t] = jnp.zeros(pack_mine.shape[1:], F32)
        pack_mine[t, 0:32, 0:local] = jnp.concatenate(
            [gkern[q, 0:32, lanes] for q in range(local // GROUP)], axis=1
        )
    acc = jnp.zeros((width, LANES), F32)
    sums = [jnp.sum(vec[k], axis=1, keepdims=True) for k in range(4)]
    for k in range(3):
        acc = column_set(acc, k, sums[k])
    square[0:1, :] = sum(
        jnp.sum(wout[t].astype(F32) * dw[0, t], axis=0, keepdims=True) for t in range(parts)
    )
    products = jnp.concatenate(
        [
            jnp.transpose(square[:, i * LANES : (i + 1) * LANES])[:, 0:1]
            for i in range(width // LANES)
        ]
    )
    acc = column_set(acc, 3, products / chan[:, 3:4] + chan[:, 2:3] * sums[3])
    hidden_sums = jnp.sum(bin_acc[...], axis=1, keepdims=True)
    for k in range(shard // local):
        starts = [t * shard + k * local for t in range(parts)]
        acc = column_set(acc, 4 + k, jnp.concatenate([hidden_sums[i : i + local] for i in starts]))
    for t in range(parts):
        square[0:local, 0:LANES] = acc[t * local : (t + 1) * local]
        pack_mine[t, 32:40, :] = jnp.transpose(square[:, 0:LANES])[0:8]
    pack_peer[mine] = pack_mine[...]
    pack_copies = [remote(pack_mine, pack_peer.at[mine], p) for p in beside]

    dw_near.wait()
    for copy in dw_copies:
        copy.wait()
    near(dw_peer, dw).wait()
    terms = [dw[:, :, i * slab : (i + 1) * slab, :] for i in range(groups)]
    dw_sum[...] = sum(terms[1:], terms[0])
    dw_low[...] = dw_sum[...].astype(BF16)

    def leg(kind, way, src, slot, peer):
        return pltpu.make_async_remote_copy(
            src_ref=src,
            dst_ref=(dw_tensor, pack_tensor)[kind].at[slot],
            send_sem=leg_send.at[kind, way],
            recv_sem=leg_recv.at[kind, slot],
            device_id=peer,
            device_id_type=MESH,
        )

    def term(kind, t):
        return pack_sum.at[t] if kind else dw_low.at[:, t]

    def to_partner(kind):
        return leg(kind, 0, term(kind, partner["tensor"]), 0, partner)

    def to_inner(kind, k):
        return leg(kind, 1 + k, term(kind, other_half + k), 2 + k, partner)

    def crossing(kind, k):
        src = (dw_pass, pack_pass)[kind].at[k]
        return leg(kind, 3 + k, src, 1, {"tensor": other_half + k})

    def start_leg(kind):
        to_partner(kind).start()

        @pl.when(jnp.logical_not(is_inner))
        def _():
            for k in range(2):
                to_inner(kind, k).start()

    start_leg(0)
    arrived(pack_copies)
    pack_sum[...] = sum((pack_peer[i] for i in range(1, groups)), pack_peer[0])
    start_leg(1)
    for copy in gx_copies(1):
        copy.start()

    @pl.when(is_inner)
    def _():
        for kind in range(2):
            for k in range(2):
                to_inner(kind, k).wait_recv()
        for k in range(2):
            dw_pass[k] = (dw_sum[:, other_half + k] + dw_tensor[2 + k].astype(F32)).astype(BF16)
            pack_pass[k] = pack_sum[other_half + k] + pack_tensor[2 + k]
        for kind in range(2):
            for k in range(2):
                crossing(kind, k).start()

    for q in range(2, local // GROUP):
        for copy in gx_copies(q):
            copy.start()

    def received(kind):
        to_partner(kind).wait_recv()
        crossing(kind, 0).wait_recv()

    received(0)
    dw_done[...] = dw_sum[:, me] + dw_tensor[0].astype(F32) + dw_tensor[1].astype(F32)
    dw_near = near(dw_done, dw_own.at[:, my_slab, :])
    dw_copies = [remote(dw_done, dw_own.at[:, my_slab, :], p) for p in beside]
    received(1)
    total = pack_sum[me] + pack_tensor[0] + pack_tensor[1]
    gdt = lag_grads(total, steps, a_log, a_imag, coefs, g_alog, g_aimag, [g_height, g_width])
    row_own[...] = total
    for j in range(2):
        row_own[29 + j : 30 + j, 0:local] = gdt[j]

    arrived(dw_copies)
    dw_near.wait()
    arrived(res_copies)

    @pl.loop(0, local // GROUP)
    def _(q):
        for copy in gx_copies(q):
            copy.wait()

    for copy in sent + first_hops + [x_copy(k) for k in range(3)]:
        copy.wait_send()

    for kind in range(2):
        to_partner(kind).wait_send()

    @pl.when(is_inner)
    def _():
        for k in range(2):
            for copy in handed_on(k):
                copy.wait_send()
            for kind in range(2):
                crossing(kind, k).wait_send()

    @pl.when(jnp.logical_not(is_inner))
    def _():
        for k in range(2):
            for kind in range(2):
                to_inner(kind, k).wait_send()


def block(parts, groups, args):
    x, size = args[0], args[2]
    local, pixels = x.shape
    pix = pixels // parts
    width = local * parts
    w_in = args[12]
    shard = w_in.shape[1]
    ff = shard * parts
    slab = shard // groups
    tiles = local // GROUP
    states = args[4].shape[0]
    shape = jax.ShapeDtypeStruct
    vmem = pl.BlockSpec(memory_space=pltpu.VMEM)
    hbm = pl.BlockSpec(memory_space=pl.ANY)
    in_specs = [hbm, hbm] + [vmem] * 10 + [hbm, vmem, hbm, vmem, vmem]
    outs = [
        (pltpu.VMEM((parts, local, pix), BF16), vmem),
        (pltpu.VMEM((parts, local, pix), BF16), vmem),
        (pltpu.VMEM((2, shard, width), F32), vmem),
        (pltpu.VMEM((states, local), F32), vmem),
        (pltpu.VMEM((states, local), F32), vmem),
        (pltpu.VMEM((2, states, local), F32), vmem),
        (pltpu.VMEM((2, states, local), F32), vmem),
        (pltpu.VMEM((40, LANES), F32), vmem),
        (shape((parts, local, pix), BF16), hbm),
        (shape((ff, pix), BF16), hbm),
        (shape((ff, pix), BF16), hbm),
        (shape((parts, local, pix), BF16), hbm),
        (shape((2, parts, shard, width), F32), hbm),
    ]
    remotes = 4 * (parts - 1) + 5 * (groups - 1)
    dma = pltpu.SemaphoreType.DMA
    scratch = [
        pltpu.VMEM((parts, local, pix), BF16),
        pltpu.VMEM((parts, local, pix), BF16),
        pltpu.VMEM((pix, LANES), F32),
        pltpu.VMEM((tiles, pix, LANES), F32),
        pltpu.VMEM((CROP, CROP, 8, LANES), F32),
        pltpu.VMEM((CROP, CROP, 8, LANES), F32),
        pltpu.VMEM((4, 2 * CROP, 8, LANES), F32),
        pltpu.VMEM((40, LANES), F32),
        pltpu.VMEM((parts, 40, LANES), F32),
        pltpu.VMEM((tiles, 32, LANES), F32),
        pltpu.VMEM((tiles, 32, LANES), F32),
        pltpu.VMEM((ff, LANES), F32),
        pltpu.VMEM((width, LANES), F32),
        pltpu.VMEM((LANES, width), F32),
        pltpu.VMEM((LANES, LANES), F32),
        pltpu.VMEM((width, ff), BF16),
        pltpu.VMEM((parts, shard, width), BF16),
        pltpu.VMEM((width, ff), BF16),
        pltpu.VMEM((ff, STEP), BF16),
        pltpu.VMEM((ff, STEP), BF16),
        pltpu.VMEM((ff, STEP), BF16),
        pltpu.VMEM((parts, local, STEP), BF16),
        pltpu.VMEM((2, parts, shard, width), F32),
        pltpu.VMEM((2, parts, slab, width), F32),
        pltpu.VMEM((2, parts, slab, width), BF16),
        pltpu.VMEM((4, 2, slab, width), BF16),
        pltpu.VMEM((2, 2, slab, width), BF16),
        pltpu.VMEM((2, slab, width), F32),
        pltpu.VMEM((ff, LANES), F32),
        pltpu.VMEM((4, width, LANES), F32),
        pltpu.VMEM((parts, 40, LANES), F32),
        pltpu.VMEM((groups, parts, 40, LANES), F32),
        pltpu.VMEM((parts, 40, LANES), F32),
        pltpu.VMEM((4, 40, LANES), F32),
        pltpu.VMEM((2, 40, LANES), F32),
        dma((remotes,)),
        dma((remotes,)),
        dma((10,)),
        dma((3,)),
        dma((3,)),
        dma((4, 3)),
        dma((3, 3)),
        dma((2, 5)),
        dma((2, 4)),
        dma((parts,)),
        dma((parts,)),
        dma((parts,)),
        dma((parts,)),
        dma((tiles, parts - 1)),
        dma((tiles, parts - 1)),
        dma((tiles,)),
    ]
    return pl.pallas_call(
        functools.partial(block_kernel, parts, groups),
        out_shape=[o[0] for o in outs],
        in_specs=in_specs,
        out_specs=[o[1] for o in outs],
        scratch_shapes=scratch,
        compiler_params=pltpu.CompilerParams(
            collective_id=0, has_side_effects=True, vmem_limit_bytes=VMEM
        ),
        name="block",
    )(*args)


def finish_kernel(parts, n_sums, *refs):
    sums, refs = refs[:n_sums], refs[n_sums:]
    res_ref, g_ref, result_ref, grad_ref = refs[:4]
    n_small = (len(refs) - 7) // 2
    smalls, refs = refs[4 : 4 + n_small], refs[4 + n_small :]
    grad_near = refs[0]
    near = refs[1 : 1 + n_small]
    left, smalls_left = refs[1 + n_small :]
    pix = g_ref.shape[2]
    out_copies = []

    def put(src, dst, sem):
        out_copies.append(pltpu.make_async_copy(src, dst, sem))
        out_copies[-1].start()

    for s in range(parts):
        put(res_ref.at[s], result_ref.at[:, pl.ds(s * pix, pix)], left.at[1, s])
    for s in range(parts):
        grad_near[s] = g_ref[s].astype(F32)
        put(grad_near.at[s], grad_ref.at[:, pl.ds(s * pix, pix)], left.at[0, s])
        if s == 0:
            dw, g_alog, g_aimag, g_height, g_width, rows = sums
            alog, aimag, height, width, dt, skip, gain, bias, win, bin_, wout, bout, scale = near
            for out, ref in ((alog, g_alog), (aimag, g_aimag), (height, g_height), (width, g_width)):
                out[...] = ref[...]
            local = skip.shape[0]
            dt[...] = rows[29:31, 0:local]
            for out, k in ((skip, 28), (gain, 33), (bias, 34), (bout, 32), (scale, 35)):
                out[...] = rows[k : k + 1, 0:local].reshape(local)
            bin_[...] = jnp.concatenate(
                [rows[36 + k : 37 + k, 0:local] for k in range(bin_.shape[0] // local)], axis=1
            ).reshape(bin_.shape)
            win[...] = jnp.transpose(dw[1])
            wout[...] = dw[0]
            for k in range(n_small):
                put(near[k], smalls[k], smalls_left.at[k])
    for copy in out_copies:
        copy.wait()


def finish(res_own, g_own, sums):
    parts, local, pix = g_own.shape
    dw, g_alog, _, g_height, _, _ = sums
    hbm = pl.BlockSpec(memory_space=pl.ANY)
    vmem = pl.BlockSpec(memory_space=pltpu.VMEM)
    dma = pltpu.SemaphoreType.DMA
    shape = jax.ShapeDtypeStruct
    line = (local,)
    small = (
        g_alog.shape,
        g_alog.shape,
        g_height.shape,
        g_height.shape,
        (2, local),
        line,
        line,
        line,
        (dw.shape[2], dw.shape[1]),
        (dw.shape[1],),
        dw.shape[1:],
        line,
        line,
    )
    return pl.pallas_call(
        functools.partial(finish_kernel, parts, len(sums)),
        out_shape=(shape((local, parts * pix), BF16), shape((local, parts * pix), F32))
        + tuple(shape(a, F32) for a in small),
        in_specs=[vmem] * (len(sums) + 2),
        out_specs=(hbm,) * (2 + len(small)),
        scratch_shapes=[
            pltpu.VMEM(g_own.shape, F32),
        ]
        + [pltpu.VMEM(a, F32) for a in small]
        + [dma((2, parts)), dma((len(small),))],
        compiler_params=pltpu.CompilerParams(vmem_limit_bytes=24 << 20),
        name="finish",
    )(*sums, res_own, g_own)


def per_device(
    parts,
    dp_size,
    inputs,
    crop_size,
    crop_offset,
    a_log,
    a_imag,
    c_height,
    c_width,
    log_dt,
    skip_gain,
    ln_gain,
    ln_bias,
    w_in,
    b_in,
    w_out,
    b_out,
    layer_scale,
    grad_out,
):
    canvases = crop_size.shape[0]
    groups = min(dp_size, 8)
    args = (
        inputs,
        grad_out,
        jnp.transpose(crop_size.reshape(canvases, 8)),
        jnp.transpose(crop_offset.reshape(canvases, 8)),
        jnp.transpose(a_log),
        jnp.transpose(a_imag),
        jnp.transpose(c_height, (0, 2, 1)),
        jnp.transpose(c_width, (0, 2, 1)),
        log_dt,
        skip_gain,
        ln_gain,
        ln_bias,
        w_in,
        b_in,
        w_out,
        b_out,
        layer_scale,
    )
    out = block(parts, groups, args)
    sums = tuple(out[2:8])
    if dp_size > groups:
        teams = [[r + groups * g for g in range(dp_size // groups)] for r in range(groups)]
        sums = lax.psum(sums, "dp", axis_index_groups=teams)
    done = finish(out[0], out[1], sums)
    return (
        done[0],
        done[1],
        jnp.transpose(done[2]),
        jnp.transpose(done[3]),
        jnp.transpose(done[4], (0, 2, 1)),
        jnp.transpose(done[5], (0, 2, 1)),
        *done[6:],
    )


def solution(mesh):
    in_specs = (
        P("tensor", "dp"),
        P("dp", None, None),
        P("dp", None, None),
        P("tensor", None),
        P("tensor", None),
        P(None, "tensor", None),
        P(None, "tensor", None),
        P(None, "tensor"),
        P("tensor"),
        P(),
        P(),
        P(None, "tensor"),
        P("tensor"),
        P("tensor", None),
        P(),
        P(),
        P("tensor", "dp"),
    )
    out_specs = (
        P("tensor", "dp"),
        P("tensor", "dp"),
        P("tensor", None),
        P("tensor", None),
        P(None, "tensor", None),
        P(None, "tensor", None),
        P(None, "tensor"),
        P("tensor"),
        P("tensor"),
        P("tensor"),
        P(None, "tensor"),
        P("tensor"),
        P("tensor", None),
        P("tensor"),
        P("tensor"),
    )
    return jax.shard_map(
        functools.partial(per_device, mesh.shape["tensor"], mesh.shape["dp"]),
        mesh=mesh,
        in_specs=in_specs,
        out_specs=out_specs,
        check_vma=False,
    )
```

```python
import functools

import jax
import jax.numpy as jnp
from jax import lax
from jax.experimental import pallas as pl
from jax.experimental.pallas import tpu as pltpu
from jax.sharding import PartitionSpec as P

F32, BF16 = jnp.float32, jnp.bfloat16
CROP = 14
SIDE = 2 * CROP
NPIX = SIDE * SIDE
LANES = 128
GROUP = 32
STEP = 896
EPS = 1e-06
GELU_C = 0.7978845608028654
GELU_A = 0.044715
VMEM = 53 << 20
MESH = pl.DeviceIdType.MESH


def nn(a, b):
    return lax.dot_general(a, b, (((1,), (0,)), ((), ())), preferred_element_type=F32)


def nt(a, b):
    return lax.dot_general(a, b, (((1,), (1,)), ((), ())), preferred_element_type=F32)


def conv(y, taps):
    return [sum((taps[l] * y[i - l] for l in range(1, i + 1)), taps[0] * y[i]) for i in range(CROP)]


def conv_back(y, taps):
    return [
        sum((taps[l] * y[i + l] for l in range(1, CROP - i)), taps[0] * y[i]) for i in range(CROP)
    ]


def spot(slot, h, w):
    first = (slot // 2) * (CROP * SIDE) + (slot % 2) * CROP
    return pl.ds(first + h * SIDE + w, 8, stride=NPIX)


def lanes_to_rows(load, rows):
    @pl.loop(0, rows.shape[0] // STEP)
    def _(j):
        off = pl.multiple_of(j * STEP, LANES)
        rows[pl.ds(off, STEP), :] = jnp.transpose(load(off).astype(F32))


def rows_to_lanes(rows, store):
    @pl.loop(0, rows.shape[0] // STEP)
    def _(j):
        off = pl.multiple_of(j * STEP, LANES)
        store(off, jnp.transpose(rows[pl.ds(off, STEP), :]).astype(BF16))


def tap_rows(kern, q, base):
    return [jnp.broadcast_to(kern[q, pl.ds(base + l, 1), :], (8, LANES)) for l in range(CROP)]


def tile_of(ref, q, off):
    return ref[:, pl.ds(pl.multiple_of(q * GROUP, GROUP), GROUP), pl.ds(off, STEP)].reshape(
        LANES, STEP
    )


def put_tile(ref, q, off, v):
    ref[:, pl.ds(pl.multiple_of(q * GROUP, GROUP), GROUP), pl.ds(off, STEP)] = v.reshape(
        ref.shape[0], GROUP, STEP
    )


def along_width(q, slot, rows, kern, mask, inner):
    @pl.loop(0, CROP)
    def _(h):
        taps = tap_rows(kern, q, CROP)
        row_in = mask[slot, h]
        y = [rows[spot(slot, h, w), :] * mask[slot, CROP + w] for w in range(CROP)]
        for w, v in enumerate(conv(y, taps)):
            inner[h, w] = v * row_in


def mix_fwd(q, x_all, rows, kern, mask, inner, mixed):
    lanes_to_rows(lambda off: tile_of(x_all, q, off), rows)
    skip = jnp.broadcast_to(kern[q, pl.ds(2 * CROP, 1), :], (8, LANES))

    @pl.loop(0, 4)
    def _(slot):
        along_width(q, slot, rows, kern, mask, inner)

        @pl.loop(0, CROP)
        def _(w):
            taps = tap_rows(kern, q, 0)
            col_in = mask[slot, CROP + w]
            y = [inner[h, w] for h in range(CROP)]
            for h, v in enumerate(conv(y, taps)):
                at = spot(slot, h, w)
                rows[at, :] = v * (mask[slot, h] * col_in) + skip * rows[at, :]

    rows_to_lanes(rows, lambda off, v: put_tile(mixed, q, off, v))


def mix_bwd(q, x_all, rows, grow, kern, mask, inner, mid, out, gkern):
    lanes_to_rows(lambda off: tile_of(x_all, q, off), rows)
    skip = jnp.broadcast_to(kern[q, pl.ds(2 * CROP, 1), :], (8, LANES))
    zero = jnp.zeros((8, LANES), F32)

    def per_slot(slot, sums):
        gk_height, gk_width, gskip = sums
        along_width(q, slot, rows, kern, mask, inner)

        def down(w, acc):
            taps = tap_rows(kern, q, 0)
            col_in = mask[slot, CROP + w]
            u = [grow[q, spot(slot, h, w), :] * (mask[slot, h] * col_in) for h in range(CROP)]
            for h, v in enumerate(conv_back(u, taps)):
                mid[h, w] = v * mask[slot, h]
            a = [inner[h, w] for h in range(CROP)]
            return tuple(
                sum((u[h] * a[h - l] for h in range(l, CROP)), acc[l]) for l in range(CROP)
            )

        gk_height = lax.fori_loop(0, CROP, down, gk_height)

        def across(h, acc):
            gk_width, gskip = acc
            taps = tap_rows(kern, q, CROP)
            u = [mid[h, w] for w in range(CROP)]
            x = [rows[spot(slot, h, w), :] for w in range(CROP)]
            y = [x[w] * mask[slot, CROP + w] for w in range(CROP)]
            gk_width = tuple(
                sum((u[w] * y[w - l] for w in range(l, CROP)), gk_width[l]) for l in range(CROP)
            )
            for w, v in enumerate(conv_back(u, taps)):
                at = spot(slot, h, w)
                g = grow[q, at, :]
                gskip = gskip + g * x[w]
                grow[q, at, :] = v * mask[slot, CROP + w] + skip * g
            return gk_width, gskip

        gk_width, gskip = lax.fori_loop(0, CROP, across, (gk_width, gskip))
        return gk_height, gk_width, gskip

    gk_height, gk_width, gskip = lax.fori_loop(
        0, 4, per_slot, ((zero,) * CROP, (zero,) * CROP, zero)
    )
    gkern[q] = jnp.zeros((32, LANES), F32)
    for row, v in enumerate((*gk_height, *gk_width, gskip)):
        gkern[q, pl.ds(row, 1), :] = jnp.sum(v, axis=0, keepdims=True)

    @pl.loop(0, rows.shape[0] // STEP)
    def _(j):
        off = pl.multiple_of(j * STEP, LANES)
        turned = jnp.transpose(grow[q, pl.ds(off, STEP), :])
        put_tile(out, q, off, (tile_of(out, q, off).astype(F32) + turned).astype(BF16))


def lag_waves(step, a_log, a_imag):
    rate = -step * jnp.exp(a_log)
    phase = step * a_imag
    size = jnp.exp(rate)
    re1, im1 = size * jnp.cos(phase), size * jnp.sin(phase)
    re, im = jnp.ones_like(re1), jnp.zeros_like(im1)
    out = []
    for _ in range(CROP):
        out.append((re, im))
        re, im = re * re1 - im * im1, re * im1 + im * re1
    return rate, phase, out


def column_set(acc, k, col):
    lane = lax.broadcasted_iota(jnp.int32, acc.shape, 1)
    return jnp.where(lane == k, col, acc)


def lag_kernels(steps, a_log, a_imag, coefs, out):
    local = a_log.shape[1]
    for j in range(2):
        _, _, waves = lag_waves(steps[j], a_log[...], a_imag[...])
        for l, (re, im) in enumerate(waves):
            row = jnp.sum(coefs[j][0] * re - coefs[j][1] * im, axis=0, keepdims=True)
            out[CROP * j + l : CROP * j + l + 1, 0:local] = row


def lag_grads(rows, steps, a_log, a_imag, coefs, g_alog, g_aimag, g_coefs):
    ga, gi, gdt = 0.0, 0.0, []
    for j in range(2):
        rate, phase, waves = lag_waves(steps[j], a_log[...], a_imag[...])
        cre, cim = coefs[j][0], coefs[j][1]
        g_re = g_im = p = r = 0.0
        for l, (re, im) in enumerate(waves):
            g = rows[CROP * j + l : CROP * j + l + 1, 0 : a_log.shape[1]]
            g_re = g_re + g * re
            g_im = g_im - g * im
            if l:
                p = p + (l * g) * (cre * re - cim * im)
                r = r - (l * g) * (cre * im + cim * re)
        g_coefs[j][0] = g_re
        g_coefs[j][1] = g_im
        ga = ga + p * rate
        gi = gi + r * steps[j]
        gdt.append(jnp.sum(p * rate + r * phase, axis=0, keepdims=True))
    g_alog[...] = ga
    g_aimag[...] = gi
    return gdt


def norm(m):
    centered = m - jnp.mean(m, axis=0, keepdims=True)
    scale = lax.rsqrt(jnp.mean(centered * centered, axis=0, keepdims=True) + EPS)
    return centered * scale, scale


def fold(v):
    return sum(
        (v[:, i * LANES : (i + 1) * LANES] for i in range(1, v.shape[1] // LANES)), v[:, :LANES]
    )


def block_kernel(
    parts,
    groups,
    x,
    go,
    size_ref,
    offset_ref,
    a_log,
    a_imag,
    c_height,
    c_width,
    log_dt,
    skip_gain,
    ln_gain,
    ln_bias,
    w_in,
    b_in,
    w_out,
    b_out,
    layer_scale,
    res_own,
    g_own,
    dw_own,
    g_alog,
    g_aimag,
    g_height,
    g_width,
    row_own,
    go_all,
    hid_far,
    slope_far,
    res,
    dw_peer,
    x_all,
    mixed,
    rows,
    grow,
    inner,
    mid,
    mask,
    small_mine,
    small_all,
    kern,
    gkern,
    bin_col,
    chan,
    square,
    turned,
    win,
    wout,
    wout_t,
    hid,
    slope,
    gp,
    chunk_near,
    dw,
    dw_sum,
    dw_low,
    dw_tensor,
    dw_pass,
    dw_done,
    bin_acc,
    vec,
    pack_mine,
    pack_peer,
    pack_sum,
    pack_tensor,
    pack_pass,
    send,
    recv,
    own,
    x_send,
    x_recv,
    hop_send,
    hop_recv,
    leg_send,
    leg_recv,
    hid_sem,
    slope_sem,
    go_sem,
    res_sem,
    gx_send,
    gx_recv,
    gx_own,
):
    local, pix = x_all.shape[1], x_all.shape[2]
    width = local * parts
    ff = gp.shape[0]
    win_t = gp.at[:, 0:width]
    shard = ff // parts
    slab = shard // groups
    chunks = pix // STEP
    me = lax.axis_index("tensor")
    dp = lax.axis_index("dp")
    mine = lax.rem(dp, groups)
    first = dp - mine
    across = [{"tensor": lax.rem(me + s, parts)} for s in range(1, parts)]
    beside = [{"dp": first + lax.rem(mine + s, groups)} for s in range(1, groups)]

    barrier = pltpu.get_barrier_semaphore()
    for peer in across + beside:
        pl.semaphore_signal(barrier, inc=1, device_id=peer, device_id_type=MESH)
    steps = [jnp.exp(log_dt[j : j + 1, :]) for j in range(2)]
    coefs = [c_height, c_width]
    small_mine[...] = jnp.zeros_like(small_mine)
    lag_kernels(steps, a_log, a_imag, coefs, small_mine)
    small_mine[2 * CROP : 2 * CROP + 1, 0:local] = skip_gain[...].reshape(1, local)
    biases = b_in[...].reshape(1, shard)
    for j in range(shard // LANES):
        small_mine[32 + j : 33 + j, :] = biases[:, j * LANES : (j + 1) * LANES]
    pl.semaphore_wait(barrier, len(across) + len(beside))

    count = [0, 0]

    def remote(src, dst, peer, sems=None):
        if sems is None:
            sems = (send.at[count[0]], recv.at[count[0]])
            count[0] += 1
        copy = pltpu.make_async_remote_copy(
            src_ref=src,
            dst_ref=dst,
            send_sem=sems[0],
            recv_sem=sems[1],
            device_id=peer,
            device_id_type=MESH,
        )
        copy.start()
        return copy

    def near(src, dst, sem=None):
        if sem is None:
            sem = own.at[count[1]]
            count[1] += 1
        copy = pltpu.make_async_copy(src, dst, sem)
        copy.start()
        return copy

    sent = []

    def arrived(copies):
        for copy in copies:
            copy.wait_recv()
        sent.extend(copies)

    def pixels(ref, peer):
        return ref.at[:, pl.ds(pl.multiple_of(peer * pix, LANES), pix)]

    def to_owner(ref, out):
        return [remote(pixels(ref, p["tensor"]), out.at[me], p) for p in across]

    my_slab = pl.ds(pl.multiple_of(mine * slab, slab), slab)

    partner = {"tensor": me + 1 - 2 * lax.rem(me, 2)}
    inner_device = {"tensor": jnp.where(me < 2, 2, 1)}
    is_inner = (me == 1) | (me == 2)
    other_half = 2 - 2 * (me // 2)

    def cols_of(t):
        return pl.ds(pl.multiple_of(t * shard, LANES), shard)

    def pieces(t):
        return [
            (win.at[my_slab, cols_of(t)], win.at[my_slab, cols_of(t)]),
            (wout.at[t, my_slab, :], wout.at[t, my_slab, :]),
            (small_all.at[t], small_all.at[t]),
        ]

    def hop(i, k, pair, peer, way):
        return pltpu.make_async_remote_copy(
            src_ref=pair[0],
            dst_ref=pair[1],
            send_sem=hop_send.at[way, i],
            recv_sem=hop_recv.at[k, i],
            device_id=peer,
            device_id_type=MESH,
        )

    first_hops = []
    slabs = [w_in.at[my_slab, :], w_out.at[my_slab, :], small_mine]
    for i in range(3):
        pair = (slabs[i], pieces(me)[i][1])
        first_hops.append(hop(i, 0, pair, partner, 0))
        first_hops.append(hop(i, 1 + lax.rem(me, 2), pair, inner_device, 1))
        for copy in first_hops[-2:]:
            copy.start()
    w_near = [near(slabs[i], pieces(me)[i][1]) for i in range(2)]
    small_all[me] = small_mine[...]

    def handed_on(k):
        found = pieces(other_half + k)
        return [hop(i, 1 + k, found[i], partner, 2 + k) for i in range(3)]

    def x_copy(k, came=False):
        peer = partner["tensor"] if k == 2 else other_half + k
        slot = k if k == 2 or came else lax.rem(me, 2)
        return pltpu.make_async_remote_copy(
            src_ref=pixels(x, peer),
            dst_ref=x_all.at[peer if came else me],
            send_sem=x_send.at[k],
            recv_sem=x_recv.at[slot],
            device_id={"tensor": peer},
            device_id_type=MESH,
        )

    for k in range(2):
        x_copy(k).start()

    @pl.when(is_inner)
    def _():
        for k in range(2):
            for copy in handed_on(k):
                copy.wait_recv()
            for copy in handed_on(k):
                copy.start()

    x_copy(2).start()
    x_near = near(pixels(x, me), x_all.at[me])

    @pl.when(jnp.logical_not(is_inner))
    def _():
        for k in range(2):
            for copy in handed_on(k):
                copy.wait_recv()

    for copy in w_near:
        copy.wait()
    for copy in first_hops[::2]:
        copy.wait_recv()
    w_copies = [remote(win.at[my_slab, :], win.at[my_slab, :], p) for p in beside]
    w_copies += [remote(wout.at[:, my_slab, :], wout.at[:, my_slab, :], p) for p in beside]

    square[...] = jnp.zeros_like(square)
    for row, ref in enumerate((ln_gain, ln_bias, b_out, layer_scale)):
        square[row : row + 1, :] = ref[...].reshape(1, width)
    for i in range(width // LANES):
        chan[i * LANES : (i + 1) * LANES, :] = jnp.transpose(square[:, i * LANES : (i + 1) * LANES])
    canvases = size_ref.shape[1]
    square[0:8, 0:canvases] = offset_ref[...].astype(F32)
    square[8:16, 0:canvases] = size_ref[...].astype(F32)
    turned[...] = jnp.transpose(square[:, 0:LANES])
    at = pl.ds(pl.multiple_of(me * 8, 8), 8)
    for slot in range(4):
        for j in range(2):
            k = 2 * slot + j
            low = jnp.broadcast_to(turned[at, k : k + 1], (8, LANES))
            high = low + jnp.broadcast_to(turned[at, 8 + k : 9 + k], (8, LANES))
            for s in range(CROP):
                mask[slot, CROP * j + s] = jnp.where((low <= s) & (s < high), 1.0, 0.0)
    for q in range(local // GROUP):
        kern[q] = jnp.concatenate(
            [small_all[t, 0:32, q * GROUP : (q + 1) * GROUP] for t in range(parts)], axis=1
        )
    for t in range(parts):
        for i in range(shard // LANES):
            block = jnp.broadcast_to(small_all[t, 32 + i : 33 + i, :], (LANES, LANES))
            bin_col[t * shard + i * LANES : t * shard + (i + 1) * LANES, :] = jnp.transpose(block)
    arrived(w_copies)
    for t in range(parts):
        cols = slice(t * shard, (t + 1) * shard)
        win_t[cols, :] = jnp.transpose(win[:, cols].astype(F32)).astype(BF16)
        wout_t[:, cols] = jnp.transpose(wout[t].astype(F32)).astype(BF16)

    for k in range(3):
        x_copy(k, came=True).wait_recv()
    x_near.wait()
    go_copies = to_owner(go, go_all)

    @pl.loop(0, local // GROUP)
    def _(q):
        mix_fwd(q, x_all, rows, kern, mask, inner, mixed)

    def hid_copy(t, j, back):
        sl = pl.ds(t * shard, shard)
        lanes = pl.ds(pl.multiple_of(j * STEP, LANES), STEP)
        pair = [(hid.at[sl, :], hid_far.at[sl, lanes]), (slope.at[sl, :], slope_far.at[sl, lanes])]
        pair = [p[::-1] if back else p for p in pair]
        return [
            pltpu.make_async_copy(*p, sem.at[t]) for p, sem in zip(pair, (hid_sem, slope_sem))
        ]

    others = [p["tensor"] for p in across]

    def res_chunk(j):
        lanes = pl.ds(pl.multiple_of(j * STEP, LANES), STEP)
        pairs = [(t, res) for t in others] + [(me, res_own)]
        return [
            pltpu.make_async_copy(chunk_near.at[t], ref.at[t, :, lanes], res_sem.at[i])
            for i, (t, ref) in enumerate(pairs)
        ]

    def low_of(off):
        normed, scale = norm(mixed[:, :, pl.ds(off, STEP)].reshape(width, STEP).astype(F32))
        return normed, scale, (normed * chan[:, 0:1] + chan[:, 1:2]).astype(BF16)

    @pl.loop(0, chunks)
    def _(j):
        off = pl.multiple_of(j * STEP, LANES)
        _, _, low = low_of(off)
        for t in range(parts):
            @pl.when(j > 0)
            def _():
                for copy in hid_copy(t, j, False):
                    copy.wait()

            for part in range(2):
                sl = pl.ds(t * shard + part * (shard // 2), shard // 2)
                pre = nn(win_t[sl, :], low) + bin_col[sl, 0:1]
                square_pre = pre * pre
                th = jnp.tanh(pre * (GELU_C + (GELU_C * GELU_A) * square_pre))
                half = 0.5 * th + 0.5
                inner_slope = GELU_C + (3 * GELU_C * GELU_A) * square_pre
                hid[sl, :] = (pre * half).astype(BF16)
                slope[sl, :] = (half + pre * (0.5 - 0.5 * th * th) * inner_slope).astype(BF16)
            for copy in hid_copy(t, j, False):
                copy.start()
        branch = nn(wout_t[...], hid[...]) + chan[:, 2:3]
        source = x_all[:, :, pl.ds(off, STEP)].reshape(width, STEP).astype(F32)
        out = (source + chan[:, 3:4] * branch).astype(BF16)

        @pl.when(j > 0)
        def _():
            for copy in res_chunk(j):
                copy.wait()

        chunk_near[...] = out.reshape(parts, local, STEP)
        for copy in res_chunk(j):
            copy.start()

    for t in range(parts):
        for copy in hid_copy(t, 0, False):
            copy.wait()
        for copy in hid_copy(t, 0, True):
            copy.start()

    for copy in res_chunk(0):
        copy.wait()

    arrived(go_copies)
    res_copies = [remote(res.at[p["tensor"]], res_own.at[me], p) for p in across]

    for ref in (dw, bin_acc, vec):
        ref[...] = jnp.zeros_like(ref)

    def go_chunk(j):
        off = pl.multiple_of(j * STEP, LANES)
        mine_at = pl.ds(pl.multiple_of(me * pix + off, LANES), STEP)
        sources = [(t, go_all.at[t, :, pl.ds(off, STEP)]) for t in others] + [(me, go.at[:, mine_at])]
        return [
            pltpu.make_async_copy(src, chunk_near.at[t], go_sem.at[i])
            for i, (t, src) in enumerate(sources)
        ]

    for copy in go_chunk(0):
        copy.start()

    @pl.loop(0, chunks)
    def _(j):
        off = pl.multiple_of(j * STEP, LANES)
        for copy in go_chunk(j):
            copy.wait()
        grad = chunk_near[...].reshape(width, STEP).astype(F32)
        gb = (grad * chan[:, 3:4]).astype(BF16)
        vec[0] += fold(gb.astype(F32))
        vec[3] += fold(grad)

        @pl.when(j + 1 < chunks)
        def _():
            for copy in go_chunk(j + 1):
                copy.start()

        normed, scale, low = low_of(off)
        for t in range(parts):
            sl = pl.ds(t * shard, shard)
            for copy in hid_copy(t, j, True):
                copy.wait()
            tile = (nn(wout[t], gb) * slope[sl, :].astype(F32)).astype(BF16)
            gp[sl, :] = tile
            bin_acc[sl, :] += fold(tile.astype(F32))
            dw[0, t] += nt(hid[sl, :], gb)
            dw[1, t] += nt(tile, low)

            @pl.when(j + 1 < chunks)
            def _():
                for copy in hid_copy(t, j + 1, True):
                    copy.start()

        gn = nn(win[...], gp[...])
        vec[1] += fold(gn * normed)
        vec[2] += fold(gn)
        g1 = gn * chan[:, 0:1]
        m1 = jnp.mean(g1, axis=0, keepdims=True)
        m2 = jnp.mean(g1 * normed, axis=0, keepdims=True)
        gm = (scale * (g1 - m1 - normed * m2)).reshape(parts, local, STEP)
        for q in range(local // GROUP):
            block = gm[:, q * GROUP : (q + 1) * GROUP, :].reshape(LANES, STEP)
            grow[q, pl.ds(off, STEP), :] = jnp.transpose(block)

    def slab_of(peer):
        return pl.ds(pl.multiple_of((peer["dp"] - first) * slab, slab), slab)

    dw_near = near(dw.at[:, :, my_slab, :], dw_peer.at[:, :, my_slab, :])
    dw_copies = [
        remote(dw.at[:, :, slab_of(p), :], dw_peer.at[:, :, my_slab, :], p) for p in beside
    ]

    back = [near(go_all.at[t], mixed.at[t]) for t in others]
    back.append(near(pixels(go, me), mixed.at[me]))
    for copy in back:
        copy.wait()

    def gx_tile(q):
        return pl.ds(pl.multiple_of(q * GROUP, GROUP), GROUP)

    def gx_copies(q):
        at = gx_tile(q)
        return [
            pltpu.make_async_remote_copy(
                src_ref=mixed.at[p["tensor"], at, :],
                dst_ref=g_own.at[me, at, :],
                send_sem=gx_send.at[q, s],
                recv_sem=gx_recv.at[q, s],
                device_id=p,
                device_id_type=MESH,
            )
            for s, p in enumerate(across)
        ] + [pltpu.make_async_copy(mixed.at[me, at, :], g_own.at[me, at, :], gx_own.at[q])]

    @pl.loop(0, local // GROUP)
    def _(q):
        mix_bwd(q, x_all, rows, grow, kern, mask, inner, mid, mixed, gkern)

        @pl.when(q == 0)
        def _():
            for copy in gx_copies(q):
                copy.start()

    for t in range(parts):
        lanes = slice(t * GROUP, (t + 1) * GROUP)
        pack_mine[t] = jnp.zeros(pack_mine.shape[1:], F32)
        pack_mine[t, 0:32, 0:local] = jnp.concatenate(
            [gkern[q, 0:32, lanes] for q in range(local // GROUP)], axis=1
        )
    acc = jnp.zeros((width, LANES), F32)
    sums = [jnp.sum(vec[k], axis=1, keepdims=True) for k in range(4)]
    for k in range(3):
        acc = column_set(acc, k, sums[k])
    square[0:1, :] = sum(
        jnp.sum(wout[t].astype(F32) * dw[0, t], axis=0, keepdims=True) for t in range(parts)
    )
    products = jnp.concatenate(
        [
            jnp.transpose(square[:, i * LANES : (i + 1) * LANES])[:, 0:1]
            for i in range(width // LANES)
        ]
    )
    acc = column_set(acc, 3, products / chan[:, 3:4] + chan[:, 2:3] * sums[3])
    hidden_sums = jnp.sum(bin_acc[...], axis=1, keepdims=True)
    for k in range(shard // local):
        starts = [t * shard + k * local for t in range(parts)]
        acc = column_set(acc, 4 + k, jnp.concatenate([hidden_sums[i : i + local] for i in starts]))
    for t in range(parts):
        square[0:local, 0:LANES] = acc[t * local : (t + 1) * local]
        pack_mine[t, 32:40, :] = jnp.transpose(square[:, 0:LANES])[0:8]
    pack_peer[mine] = pack_mine[...]
    pack_copies = [remote(pack_mine, pack_peer.at[mine], p) for p in beside]

    dw_near.wait()
    for copy in dw_copies:
        copy.wait()
    near(dw_peer, dw).wait()
    terms = [dw[:, :, i * slab : (i + 1) * slab, :] for i in range(groups)]
    dw_sum[...] = sum(terms[1:], terms[0])
    dw_low[...] = dw_sum[...].astype(BF16)

    def leg(kind, way, src, slot, peer):
        return pltpu.make_async_remote_copy(
            src_ref=src,
            dst_ref=(dw_tensor, pack_tensor)[kind].at[slot],
            send_sem=leg_send.at[kind, way],
            recv_sem=leg_recv.at[kind, slot],
            device_id=peer,
            device_id_type=MESH,
        )

    def term(kind, t):
        return pack_sum.at[t] if kind else dw_low.at[:, t]

    def to_partner(kind):
        return leg(kind, 0, term(kind, partner["tensor"]), 0, partner)

    def to_inner(kind, k):
        return leg(kind, 1 + k, term(kind, other_half + k), 2 + k, partner)

    def crossing(kind, k):
        src = (dw_pass, pack_pass)[kind].at[k]
        return leg(kind, 3 + k, src, 1, {"tensor": other_half + k})

    def start_leg(kind):
        to_partner(kind).start()

        @pl.when(jnp.logical_not(is_inner))
        def _():
            for k in range(2):
                to_inner(kind, k).start()

    start_leg(0)
    arrived(pack_copies)
    pack_sum[...] = sum((pack_peer[i] for i in range(1, groups)), pack_peer[0])
    start_leg(1)
    for copy in gx_copies(1):
        copy.start()

    @pl.when(is_inner)
    def _():
        for kind in range(2):
            for k in range(2):
                to_inner(kind, k).wait_recv()
        for k in range(2):
            dw_pass[k] = (dw_sum[:, other_half + k] + dw_tensor[2 + k].astype(F32)).astype(BF16)
            pack_pass[k] = pack_sum[other_half + k] + pack_tensor[2 + k]
        for kind in range(2):
            for k in range(2):
                crossing(kind, k).start()

    for q in range(2, local // GROUP):
        for copy in gx_copies(q):
            copy.start()

    def received(kind):
        to_partner(kind).wait_recv()
        crossing(kind, 0).wait_recv()

    received(0)
    dw_done[...] = dw_sum[:, me] + dw_tensor[0].astype(F32) + dw_tensor[1].astype(F32)
    dw_near = near(dw_done, dw_own.at[:, my_slab, :])
    dw_copies = [remote(dw_done, dw_own.at[:, my_slab, :], p) for p in beside]
    received(1)
    total = pack_sum[me] + pack_tensor[0] + pack_tensor[1]
    gdt = lag_grads(total, steps, a_log, a_imag, coefs, g_alog, g_aimag, [g_height, g_width])
    row_own[...] = total
    for j in range(2):
        row_own[29 + j : 30 + j, 0:local] = gdt[j]

    arrived(dw_copies)
    dw_near.wait()
    arrived(res_copies)

    @pl.loop(0, local // GROUP)
    def _(q):
        for copy in gx_copies(q):
            copy.wait()

    for copy in sent + first_hops + [x_copy(k) for k in range(3)]:
        copy.wait_send()

    for kind in range(2):
        to_partner(kind).wait_send()

    @pl.when(is_inner)
    def _():
        for k in range(2):
            for copy in handed_on(k):
                copy.wait_send()
            for kind in range(2):
                crossing(kind, k).wait_send()

    @pl.when(jnp.logical_not(is_inner))
    def _():
        for k in range(2):
            for kind in range(2):
                to_inner(kind, k).wait_send()


def block(parts, groups, args):
    x, size = args[0], args[2]
    local, pixels = x.shape
    pix = pixels // parts
    width = local * parts
    w_in = args[12]
    shard = w_in.shape[1]
    ff = shard * parts
    slab = shard // groups
    tiles = local // GROUP
    states = args[4].shape[0]
    shape = jax.ShapeDtypeStruct
    vmem = pl.BlockSpec(memory_space=pltpu.VMEM)
    hbm = pl.BlockSpec(memory_space=pl.ANY)
    in_specs = [hbm, hbm] + [vmem] * 10 + [hbm, vmem, hbm, vmem, vmem]
    outs = [
        (pltpu.VMEM((parts, local, pix), BF16), vmem),
        (pltpu.VMEM((parts, local, pix), BF16), vmem),
        (pltpu.VMEM((2, shard, width), F32), vmem),
        (pltpu.VMEM((states, local), F32), vmem),
        (pltpu.VMEM((states, local), F32), vmem),
        (pltpu.VMEM((2, states, local), F32), vmem),
        (pltpu.VMEM((2, states, local), F32), vmem),
        (pltpu.VMEM((40, LANES), F32), vmem),
        (shape((parts, local, pix), BF16), hbm),
        (shape((ff, pix), BF16), hbm),
        (shape((ff, pix), BF16), hbm),
        (shape((parts, local, pix), BF16), hbm),
        (shape((2, parts, shard, width), F32), hbm),
    ]
    remotes = 4 * (parts - 1) + 5 * (groups - 1)
    dma = pltpu.SemaphoreType.DMA
    scratch = [
        pltpu.VMEM((parts, local, pix), BF16),
        pltpu.VMEM((parts, local, pix), BF16),
        pltpu.VMEM((pix, LANES), F32),
        pltpu.VMEM((tiles, pix, LANES), F32),
        pltpu.VMEM((CROP, CROP, 8, LANES), F32),
        pltpu.VMEM((CROP, CROP, 8, LANES), F32),
        pltpu.VMEM((4, 2 * CROP, 8, LANES), F32),
        pltpu.VMEM((40, LANES), F32),
        pltpu.VMEM((parts, 40, LANES), F32),
        pltpu.VMEM((tiles, 32, LANES), F32),
        pltpu.VMEM((tiles, 32, LANES), F32),
        pltpu.VMEM((ff, LANES), F32),
        pltpu.VMEM((width, LANES), F32),
        pltpu.VMEM((LANES, width), F32),
        pltpu.VMEM((LANES, LANES), F32),
        pltpu.VMEM((width, ff), BF16),
        pltpu.VMEM((parts, shard, width), BF16),
        pltpu.VMEM((width, ff), BF16),
        pltpu.VMEM((ff, STEP), BF16),
        pltpu.VMEM((ff, STEP), BF16),
        pltpu.VMEM((ff, STEP), BF16),
        pltpu.VMEM((parts, local, STEP), BF16),
        pltpu.VMEM((2, parts, shard, width), F32),
        pltpu.VMEM((2, parts, slab, width), F32),
        pltpu.VMEM((2, parts, slab, width), BF16),
        pltpu.VMEM((4, 2, slab, width), BF16),
        pltpu.VMEM((2, 2, slab, width), BF16),
        pltpu.VMEM((2, slab, width), F32),
        pltpu.VMEM((ff, LANES), F32),
        pltpu.VMEM((4, width, LANES), F32),
        pltpu.VMEM((parts, 40, LANES), F32),
        pltpu.VMEM((groups, parts, 40, LANES), F32),
        pltpu.VMEM((parts, 40, LANES), F32),
        pltpu.VMEM((4, 40, LANES), F32),
        pltpu.VMEM((2, 40, LANES), F32),
        dma((remotes,)),
        dma((remotes,)),
        dma((10,)),
        dma((3,)),
        dma((3,)),
        dma((4, 3)),
        dma((3, 3)),
        dma((2, 5)),
        dma((2, 4)),
        dma((parts,)),
        dma((parts,)),
        dma((parts,)),
        dma((parts,)),
        dma((tiles, parts - 1)),
        dma((tiles, parts - 1)),
        dma((tiles,)),
    ]
    return pl.pallas_call(
        functools.partial(block_kernel, parts, groups),
        out_shape=[o[0] for o in outs],
        in_specs=in_specs,
        out_specs=[o[1] for o in outs],
        scratch_shapes=scratch,
        compiler_params=pltpu.CompilerParams(
            collective_id=0, has_side_effects=True, vmem_limit_bytes=VMEM
        ),
        name="block",
    )(*args)


def finish_kernel(parts, n_sums, *refs):
    sums, refs = refs[:n_sums], refs[n_sums:]
    res_ref, g_ref, result_ref, grad_ref = refs[:4]
    n_small = (len(refs) - 7) // 2
    smalls, refs = refs[4 : 4 + n_small], refs[4 + n_small :]
    grad_near = refs[0]
    near = refs[1 : 1 + n_small]
    left, smalls_left = refs[1 + n_small :]
    pix = g_ref.shape[2]
    out_copies = []

    def put(src, dst, sem):
        out_copies.append(pltpu.make_async_copy(src, dst, sem))
        out_copies[-1].start()

    for s in range(parts):
        put(res_ref.at[s], result_ref.at[:, pl.ds(s * pix, pix)], left.at[1, s])
    for s in range(parts):
        grad_near[s] = g_ref[s].astype(F32)
        put(grad_near.at[s], grad_ref.at[:, pl.ds(s * pix, pix)], left.at[0, s])
        if s == 0:
            dw, g_alog, g_aimag, g_height, g_width, rows = sums
            alog, aimag, height, width, dt, skip, gain, bias, win, bin_, wout, bout, scale = near
            for out, ref in ((alog, g_alog), (aimag, g_aimag), (height, g_height), (width, g_width)):
                out[...] = ref[...]
            local = skip.shape[0]
            dt[...] = rows[29:31, 0:local]
            for out, k in ((skip, 28), (gain, 33), (bias, 34), (bout, 32), (scale, 35)):
                out[...] = rows[k : k + 1, 0:local].reshape(local)
            bin_[...] = jnp.concatenate(
                [rows[36 + k : 37 + k, 0:local] for k in range(bin_.shape[0] // local)], axis=1
            ).reshape(bin_.shape)
            win[...] = jnp.transpose(dw[1])
            wout[...] = dw[0]
            for k in range(n_small):
                put(near[k], smalls[k], smalls_left.at[k])
    for copy in out_copies:
        copy.wait()


def finish(res_own, g_own, sums):
    parts, local, pix = g_own.shape
    dw, g_alog, _, g_height, _, _ = sums
    hbm = pl.BlockSpec(memory_space=pl.ANY)
    vmem = pl.BlockSpec(memory_space=pltpu.VMEM)
    dma = pltpu.SemaphoreType.DMA
    shape = jax.ShapeDtypeStruct
    line = (local,)
    small = (
        g_alog.shape,
        g_alog.shape,
        g_height.shape,
        g_height.shape,
        (2, local),
        line,
        line,
        line,
        (dw.shape[2], dw.shape[1]),
        (dw.shape[1],),
        dw.shape[1:],
        line,
        line,
    )
    return pl.pallas_call(
        functools.partial(finish_kernel, parts, len(sums)),
        out_shape=(shape((local, parts * pix), BF16), shape((local, parts * pix), F32))
        + tuple(shape(a, F32) for a in small),
        in_specs=[vmem] * (len(sums) + 2),
        out_specs=(hbm,) * (2 + len(small)),
        scratch_shapes=[
            pltpu.VMEM(g_own.shape, F32),
        ]
        + [pltpu.VMEM(a, F32) for a in small]
        + [dma((2, parts)), dma((len(small),))],
        compiler_params=pltpu.CompilerParams(vmem_limit_bytes=24 << 20),
        name="finish",
    )(*sums, res_own, g_own)


def per_device(
    parts,
    dp_size,
    inputs,
    crop_size,
    crop_offset,
    a_log,
    a_imag,
    c_height,
    c_width,
    log_dt,
    skip_gain,
    ln_gain,
    ln_bias,
    w_in,
    b_in,
    w_out,
    b_out,
    layer_scale,
    grad_out,
):
    canvases = crop_size.shape[0]
    groups = min(dp_size, 8)
    args = (
        inputs,
        grad_out,
        jnp.transpose(crop_size.reshape(canvases, 8)),
        jnp.transpose(crop_offset.reshape(canvases, 8)),
        jnp.transpose(a_log),
        jnp.transpose(a_imag),
        jnp.transpose(c_height, (0, 2, 1)),
        jnp.transpose(c_width, (0, 2, 1)),
        log_dt,
        skip_gain,
        ln_gain,
        ln_bias,
        w_in,
        b_in,
        w_out,
        b_out,
        layer_scale,
    )
    out = block(parts, groups, args)
    sums = tuple(out[2:8])
    if dp_size > groups:
        teams = [[r + groups * g for g in range(dp_size // groups)] for r in range(groups)]
        sums = lax.psum(sums, "dp", axis_index_groups=teams)
    done = finish(out[0], out[1], sums)
    return (
        done[0],
        done[1],
        jnp.transpose(done[2]),
        jnp.transpose(done[3]),
        jnp.transpose(done[4], (0, 2, 1)),
        jnp.transpose(done[5], (0, 2, 1)),
        *done[6:],
    )


def solution(mesh):
    in_specs = (
        P("tensor", "dp"),
        P("dp", None, None),
        P("dp", None, None),
        P("tensor", None),
        P("tensor", None),
        P(None, "tensor", None),
        P(None, "tensor", None),
        P(None, "tensor"),
        P("tensor"),
        P(),
        P(),
        P(None, "tensor"),
        P("tensor"),
        P("tensor", None),
        P(),
        P(),
        P("tensor", "dp"),
    )
    out_specs = (
        P("tensor", "dp"),
        P("tensor", "dp"),
        P("tensor", None),
        P("tensor", None),
        P(None, "tensor", None),
        P(None, "tensor", None),
        P(None, "tensor"),
        P("tensor"),
        P("tensor"),
        P("tensor"),
        P(None, "tensor"),
        P("tensor"),
        P("tensor", None),
        P("tensor"),
        P("tensor"),
    )
    return jax.shard_map(
        functools.partial(per_device, mesh.shape["tensor"], mesh.shape["dp"]),
        mesh=mesh,
        in_specs=in_specs,
        out_specs=out_specs,
        check_vma=False,
    )
```
